32 devices in a mesh: wide: 8 (over z, core), narrow: 4 (over y, x).
Axes of the slice: x: 2, y: 2, z: 4, core: 2. Of those that a mesh axis runs over, the one named last changes fastest.
Arguments:
- tokens: bfloat16 [4096, 2048], P('wide'), may hold values from -6 to 6
- attn_gain: bfloat16 [2048], replicated, may hold values from 0.099609375 to 1.8984375
- w_query: bfloat16 [2048, 2048], P(None, 'narrow'), may hold values from -0.125 to 0.125
- w_key: bfloat16 [2048, 512], P(None, 'narrow'), may hold values from -0.125 to 0.125
- w_value: bfloat16 [2048, 512], P(None, 'narrow'), may hold values from -0.125 to 0.125
- w_out: bfloat16 [2048, 2048], P('narrow'), may hold values from -2 to 2
- ffn_gain: bfloat16 [2048], replicated, may hold values from 0.099609375 to 1.8984375
- w_gate: bfloat16 [2048, 8192], P(None, 'narrow'), may hold values from -0.125 to 0.125
- w_up: bfloat16 [2048, 8192], P(None, 'narrow'), may hold values from -0.125 to 0.125
- w_down: bfloat16 [8192, 2048], P('narrow'), may hold values from -0.0625 to 0.0625
- doc_lengths: int32 [12], replicated, may hold values from 1 to 2048, 4096 in all
- cotangent: bfloat16 [4096, 2048], P('wide'), may hold values from -6 to 6
Outputs:
- output: bfloat16 [4096, 2048], P('wide')
- input_grad: bfloat16 [4096, 2048], P('wide')
- grad_attn_gain: float32 [2048], P('wide')
- grad_query: float32 [2048, 2048], P('wide', 'narrow')
- grad_key: float32 [2048, 512], P('wide', 'narrow')
- grad_value: float32 [2048, 512], P('wide', 'narrow')
- grad_out: float32 [2048, 2048], P('narrow', 'wide')
- grad_ffn_gain: float32 [2048], P('wide')
- grad_gate: float32 [2048, 8192], P('wide', 'narrow')
- grad_up: float32 [2048, 8192], P('wide', 'narrow')
- grad_down: float32 [8192, 2048], P('narrow', 'wide')
The draws below stay inside these ranges and needn't reach their ends.
Inputs may be any that keep to these rules, and one draw needn't show every extreme that they name: `doc_lengths`: the last entry is the padding at the row's end; the longest entry is exactly 2048.
All inputs are finite; a program needn't handle non-finite values.
Results may differ from the reference program's by a relative error of at most 0.02.
Values may be sent and summed in bfloat16 or wider, within the bound.
No kernel may reach another device: no remote copies, remote signals or barrier semaphores. Data moves between devices by JAX's collectives and lax.ppermute only.
A program may use at most 320 MiB of HBM per device.

```python
import math
import jax
import jax.numpy as jnp
import numpy as np
from jax import lax

D = 2048
H = 32
KV = 8
HD = 64
FF = 8192
QBLK = 512
DOCS = 12
TOKENS = 4096
MOST = 2048


def with_spikes(entries, rng, source, target, parts, factor):
    def block_of(axis_at):
        return (jnp.arange(entries.shape[axis_at]) // (entries.shape[axis_at] // parts)).reshape((-1,) + (1,) * (entries.ndim - 1 - axis_at))

    one_side = jax.random.permutation(rng, parts)[block_of(target)]
    other_side = (block_of(target) + parts // 2) % parts
    return jnp.where((block_of(source) == one_side) | (block_of(source) == other_side), factor * entries, entries)


def shard_levels(stream_key, shape, cuts, low, high):
    level = 1.0
    for dim, shards_of in cuts:
        heights = jax.random.uniform(jax.random.fold_in(jax.random.fold_in(stream_key, 6), dim), (shards_of,), jnp.float32, low / len(cuts), high / len(cuts))
        level = level * jnp.repeat(jnp.exp(heights), shape[dim] // shards_of).reshape((-1,) + (1,) * (len(shape) - 1 - dim))
    return level


def length_profile(count, total, limit, lean):
    weights = [(1 << 20) // math.isqrt(rank ** lean) + 1 for rank in range(2, count + 1)]
    spare, given = total - limit - (count - 1), [1] * (count - 1)
    while spare > 0:
        movable = [i for i in range(count - 1) if given[i] < limit]
        mass, budget = sum([weights[i] for i in movable]), spare
        for i in movable:
            more = min(limit - given[i], max(1, budget * weights[i] // mass), spare)
            given[i] = given[i] + more
            spare = spare - more
    return np.array([limit] + given)


def uneven_parts(stream_key, number_of, total, most, lean):
    if number_of == 2:
        one = jax.random.randint(stream_key, (), max(1, total - most), min(most, total - 1) + 1)
        return jnp.stack([one, total - one])
    lengths = jnp.asarray(length_profile(number_of, total, most, lean), jnp.int32)
    twos = (number_of - 1) // 2
    source_of, sink = lengths[1:1 + 2 * twos:2], lengths[2:2 + 2 * twos:2]
    room = jnp.minimum(source_of - 1, most - sink)
    moved = jax.random.randint(jax.random.fold_in(stream_key, 1), (twos,), 0, 1 << 20) % (room + 1)
    lengths = lengths.at[1:1 + 2 * twos:2].set(source_of - moved).at[2:2 + 2 * twos:2].set(sink + moved)
    return lengths[jax.random.permutation(jax.random.fold_in(stream_key, 2), number_of)]


def bell_draw(rng, extent, spread, reach, split=(), kind=jnp.bfloat16):
    drawn = jax.random.normal(rng, extent, jnp.float32) * spread
    if len(split) > 0:
        drawn = shard_levels(rng, extent, split, -0.22, 0.18) * drawn
    return jnp.clip(drawn, min=-reach, max=reach).astype(kind)


def noise_with(key, dims, width, most, pieces, heavy, kind=jnp.bfloat16):
    entries = width * jax.random.normal(key, dims, jnp.float32)
    if pieces:
        entries = entries * shard_levels(key, dims, pieces, -0.22, 0.18)
    return jnp.clip(with_spikes(entries, jax.random.fold_in(key, 3), *heavy), -most, most).astype(kind)


def setup_inputs(seed: int = 0) -> dict:
    seeds = jax.random.split(jax.random.key(seed), 13)
    return {
        "tokens": noise_with(seeds[0], (TOKENS, D), 1.0, 6.0, ((0, 8),), (0, 1, 8, 2.0)),
        "attn_gain": jnp.clip(1.0 + 0.18 * jax.random.normal(seeds[1], (D,), jnp.float32), 0.099609375, 1.8984375).astype(jnp.bfloat16),
        "w_query": bell_draw(seeds[2], (D, H * HD), D ** -0.5, 0.125, ((1, 4),)),
        "w_key": bell_draw(seeds[3], (D, KV * HD), D ** -0.5, 0.125, ((1, 4),)),
        "w_value": bell_draw(seeds[4], (D, KV * HD), D ** -0.5, 0.125, ((1, 4),)),
        "w_out": bell_draw(seeds[5], (H * HD, D), (max(1, H * HD * 16 // TOKENS)) ** -0.5, 2.0, ((0, 4),)),
        "ffn_gain": jnp.clip(1.0 + 0.18 * jax.random.normal(seeds[6], (D,), jnp.float32), 0.099609375, 1.8984375).astype(jnp.bfloat16),
        "w_gate": bell_draw(seeds[7], (D, FF), D ** -0.5, 0.125, ((1, 4),)),
        "w_up": bell_draw(seeds[8], (D, FF), D ** -0.5, 0.125, ((1, 4),)),
        "w_down": bell_draw(seeds[9], (FF, D), FF ** -0.5, 0.0625, ((0, 4),)),
        "doc_lengths": uneven_parts(seeds[10], DOCS, TOKENS, MOST, 2).astype(jnp.int32),
        "cotangent": noise_with(seeds[11], (TOKENS, D), 1.0, 6.0, ((0, 8),), (0, 1, 8, 2.0)),
    }


NORM_EPS = 1e-05
MASKED_SCORE = -1e+30
HIGHEST = lax.Precision.HIGHEST

@jax.custom_vjp
def low(v):
    return lax.optimization_barrier(v.astype(jnp.bfloat16)).astype(jnp.float32)

@jax.custom_vjp
def low_back(v):
    return v

def low_keep(v):
    return (low(v), None)

def low_pass(kept, grad):
    return (grad,)

def back_keep(v):
    return (v, None)

def back_low(kept, grad):
    return (low(grad),)
low.defvjp(low_keep, low_pass)
low_back.defvjp(back_keep, back_low)

def inverse_frequencies(head_size):
    frequency = 1.0 / 500000.0 ** (np.arange(0, head_size, 2) / head_size)
    wavelength = 2 * math.pi / frequency
    smoothing = (8192.0 / wavelength - 1.0) / 3.0
    scaled_freq = np.where(wavelength > 8192.0, frequency / 32.0, frequency)
    middle_band = (wavelength <= 8192.0) & (wavelength >= 2048.0)
    scaled_freq = np.where(middle_band, (1 - smoothing) * frequency / 32.0 + smoothing * frequency, scaled_freq)
    return scaled_freq.astype(np.float32)

def doc_layout(doc_lengths, index):
    ends = jnp.cumsum(doc_lengths).astype(jnp.int32)
    passed = (index[:, None] >= ends[None, :]).astype(jnp.int32)
    segment = lax.optimization_barrier(jnp.sum(passed, axis=1)).astype(jnp.int32)
    offset = lax.optimization_barrier(jnp.sum(passed * doc_lengths[None, :], axis=1)).astype(jnp.int32)
    position = (index - offset).astype(jnp.int32)
    valid = index < ends[DOCS - 2]
    return (segment, position, valid)

def rotate(values, position, heads):
    angle = position.astype(jnp.float32)[:, None] * jnp.asarray(inverse_frequencies(HD))[None, :]
    cosine = jnp.cos(angle)[:, None, :]
    sine = jnp.sin(angle)[:, None, :]
    shaped = values.reshape(values.shape[0], heads, 2, HD // 2)
    first = shaped[:, :, 0]
    second = shaped[:, :, 1]
    return jnp.stack([first * cosine - second * sine, second * cosine + first * sine], axis=2).reshape(values.shape)

def rms_norm(values, gain):
    scale = lax.rsqrt(lax.optimization_barrier(jnp.mean(values * values, axis=-1, keepdims=True)) + NORM_EPS)
    return values * scale * gain

def attention(query_r, keys_r, values_v, segment):
    blocks = TOKENS // QBLK
    group = H // KV
    index = jnp.arange(TOKENS, dtype=jnp.int32)
    query_blocks = query_r.reshape(blocks, QBLK, KV, group, HD).transpose(0, 2, 1, 3, 4)
    key_heads = keys_r.reshape(TOKENS, KV, HD).transpose(1, 0, 2)
    value_heads = values_v.reshape(TOKENS, KV, HD).transpose(1, 0, 2)

    def one_block(block_in):
        query_block, segment_block, index_block = block_in
        allowed = (segment_block[:, None] == segment[None, :]) & (index_block[:, None] >= index[None, :])

        def one_head(head_in):
            query_head, key_head, value_head = head_in
            raw_scores = jnp.einsum('qgd,kd->qgk', query_head, key_head, precision=HIGHEST)
            scores = low_back(raw_scores / math.sqrt(HD))
            scores = jnp.where(allowed[:, None, :], scores, MASKED_SCORE)
            weights = low(jax.nn.softmax(scores, axis=-1))
            return jnp.einsum('qgk,kd->qgd', weights, value_head, precision=HIGHEST)
        return lax.map(one_head, (query_block, key_heads, value_heads))
    result = lax.map(jax.checkpoint(one_block), (query_blocks, segment.reshape(blocks, QBLK), index.reshape(blocks, QBLK)))
    return result.transpose(0, 2, 1, 3, 4).reshape(TOKENS, H * HD)

def forward(inputs, attn_gain, w_query, w_key, w_value, w_out, ffn_gain, w_gate, w_up, w_down, segment, position, valid):
    normed = low(rms_norm(inputs, attn_gain))
    query = low_back(jnp.dot(normed, w_query, precision=HIGHEST))
    keys = low_back(jnp.dot(normed, w_key, precision=HIGHEST))
    values_v = low(low_back(jnp.dot(normed, w_value, precision=HIGHEST)))
    query_r = low(rotate(query, position, H))
    keys_r = low(rotate(keys, position, KV))
    mixed = attention(query_r, keys_r, values_v, segment)
    mixed = low(low_back(mixed * valid.astype(jnp.float32)[:, None]))
    attn_out = low_back(jnp.dot(mixed, w_out, precision=HIGHEST))
    hidden_one = inputs + attn_out
    normed_two = low(rms_norm(hidden_one, ffn_gain))
    gate = low_back(jnp.dot(normed_two, w_gate, precision=HIGHEST))
    up_proj = low_back(jnp.dot(normed_two, w_up, precision=HIGHEST))
    activ = low(jax.nn.silu(gate) * up_proj)
    ffn_out = low_back(jnp.dot(activ, w_down, precision=HIGHEST))
    return hidden_one + ffn_out

def reference(tokens, attn_gain, w_query, w_key, w_value, w_out, ffn_gain, w_gate, w_up, w_down, doc_lengths, cotangent):
    index = jnp.arange(TOKENS, dtype=jnp.int32)
    segment, position, valid = doc_layout(doc_lengths, index)
    params = [a.astype(jnp.float32) for a in (tokens, attn_gain, w_query, w_key, w_value, w_out, ffn_gain, w_gate, w_up, w_down)]

    def run(*weights):
        return forward(*weights, segment, position, valid)
    result, pullback = jax.vjp(run, *params)
    grads = pullback(cotangent.astype(jnp.float32))
    return (result.astype(jnp.bfloat16), grads[0].astype(jnp.bfloat16), grads[1], grads[2], grads[3], grads[4], grads[5], grads[6], grads[7], grads[8], grads[9])
```

```python
import functools
import math

import jax
import jax.numpy as jnp
import numpy as np
from jax import lax
from jax.experimental import pallas as pl
from jax.experimental.pallas import tpu as pltpu
from jax.sharding import PartitionSpec as P

HD = 64
DOCS = 12
NORM_EPS = 1e-05
MASKED_SCORE = -1e30
LOG2E = math.log2(math.e)
SCALE2 = LOG2E / math.sqrt(HD)
QT = 256
KT = 256
BF = jnp.bfloat16
F32 = jnp.float32


def inverse_frequencies(head_size):
    frequency = 1.0 / 500000.0 ** (np.arange(0, head_size, 2) / head_size)
    wavelength = 2 * math.pi / frequency
    smoothing = (8192.0 / wavelength - 1.0) / 3.0
    scaled_freq = np.where(wavelength > 8192.0, frequency / 32.0, frequency)
    middle_band = (wavelength <= 8192.0) & (wavelength >= 2048.0)
    scaled_freq = np.where(
        middle_band, (1 - smoothing) * frequency / 32.0 + smoothing * frequency, scaled_freq
    )
    return scaled_freq.astype(np.float32)


def doc_offsets(doc_lengths, index):
    ends = jnp.cumsum(doc_lengths)
    passed = (index[None, :] >= ends[:, None]).astype(jnp.int32)
    start = jnp.sum(passed * doc_lengths[:, None], axis=0)
    valid = index < ends[DOCS - 2]
    return start, valid


def rotate_t(values, cosine, sine):
    heads = values.shape[0] // HD
    shaped = values.reshape(heads, 2, HD // 2, values.shape[1])
    first = shaped[:, 0]
    second = shaped[:, 1]
    return jnp.stack(
        [first * cosine - second * sine, second * cosine + first * sine], axis=1
    ).reshape(values.shape)


def dims(left, right, a, b):
    return lax.dot_general(left, right, (((a,), (b,)), ((), ())), preferred_element_type=F32)


def tile_active(info_ref, tiles, tile, q_tile):
    key_base = info_ref[tile]
    q_base = info_ref[tiles] + q_tile * QT
    first_key = info_ref[tiles + 1 + q_tile]
    return (key_base <= q_base + QT - 1) & (key_base + KT > first_key), key_base, q_base


def tile_mask(key_base, q_base, start_row):
    keys = key_base + lax.broadcasted_iota(jnp.int32, (KT, QT), 0)
    queries = q_base + lax.broadcasted_iota(jnp.int32, (KT, QT), 1)
    return (keys <= queries) & (keys >= start_row)


def attend_kernel(slots, group, info_ref, start_ref, valid_ref, q_ref, *refs):
    k_refs = refs[:slots]
    v_refs = refs[slots : 2 * slots]
    o_ref, mixed_ref, lse_ref, keys_s, values_s, top_s, sum_s, acc_s = refs[2 * slots :]
    rows = q_ref.shape[1]
    per = rows // KT
    tiles = slots * per
    for slot in range(slots):
        for part in range(per):
            cut = slice(part * KT, (part + 1) * KT)
            keys_s[slot * per + part] = k_refs[slot][:, cut].T
            values_s[slot * per + part] = v_refs[slot][:, cut]
    for q_tile in range(rows // QT):
        q_cut = slice(q_tile * QT, (q_tile + 1) * QT)
        top_s[...] = jnp.full_like(top_s, MASKED_SCORE)
        sum_s[...] = jnp.zeros_like(sum_s)
        acc_s[...] = jnp.zeros_like(acc_s)
        start_row = start_ref[:, q_cut]

        def step(tile, carry, q_tile=q_tile, q_cut=q_cut, start_row=start_row):
            active, key_base, q_base = tile_active(info_ref, tiles, tile, q_tile)

            @pl.when(active)
            def _():
                allowed = tile_mask(key_base, q_base, start_row)
                keys = keys_s[tile]
                values = values_s[tile]
                for head in range(group):
                    scores = jnp.dot(
                        keys, q_ref[head * HD : (head + 1) * HD, q_cut], preferred_element_type=F32
                    )
                    scores = jnp.where(allowed, scores, MASKED_SCORE)
                    old = top_s[head : head + 1, :]
                    new = jnp.maximum(old, jnp.max(scores, axis=0, keepdims=True))
                    weight = jnp.exp2((scores - new) * SCALE2)
                    decay = jnp.exp2((old - new) * SCALE2)
                    top_s[head : head + 1, :] = new
                    sum_s[head : head + 1, :] = sum_s[head : head + 1, :] * decay + jnp.sum(
                        weight, axis=0, keepdims=True
                    )
                    acc_s[head] = acc_s[head] * decay + jnp.dot(
                        values, weight.astype(BF), preferred_element_type=F32
                    )

            return carry

        lax.fori_loop(0, tiles, step, 0)
        for head in range(group):
            h_cut = slice(head * HD, (head + 1) * HD)
            total = sum_s[head : head + 1, :]
            out = acc_s[head] / total
            o_ref[h_cut, q_cut] = out
            mixed_ref[h_cut, q_cut] = jnp.where(valid_ref[:, q_cut] != 0, out, 0.0).astype(BF)
            lse_ref[0, head : head + 1, q_cut] = (
                top_s[head : head + 1, :] * SCALE2 + jnp.log(total) * LOG2E
            )


def attend(info, start, valid, q_t, blocks, kv_heads):
    slots = len(blocks)
    heads = q_t.shape[0] // HD
    group = heads // kv_heads
    rows = q_t.shape[1]
    tiles = slots * (rows // KT)
    row_spec = pl.BlockSpec((1, rows), lambda g: (0, 0))
    q_spec = pl.BlockSpec((group * HD, rows), lambda g: (g, 0))
    return pl.pallas_call(
        functools.partial(attend_kernel, slots, group),
        grid=(kv_heads,),
        in_specs=[pl.BlockSpec(memory_space=pltpu.SMEM), row_spec, row_spec, q_spec]
        + [pl.BlockSpec((HD, rows), lambda g: (g, 0))] * slots
        + [pl.BlockSpec((HD, rows), lambda g: (kv_heads + g, 0))] * slots,
        out_specs=[q_spec, q_spec, pl.BlockSpec((1, group, rows), lambda g: (g, 0, 0))],
        out_shape=[
            jax.ShapeDtypeStruct(q_t.shape, F32),
            jax.ShapeDtypeStruct(q_t.shape, BF),
            jax.ShapeDtypeStruct((kv_heads, group, rows), F32),
        ],
        scratch_shapes=[
            pltpu.VMEM((tiles, KT, HD), BF),
            pltpu.VMEM((tiles, HD, KT), BF),
            pltpu.VMEM((group, QT), F32),
            pltpu.VMEM((group, QT), F32),
            pltpu.VMEM((group, HD, QT), F32),
        ],
        name="attend",
        cost_estimate=pl.CostEstimate(
            flops=4 * heads * rows * rows * 4 * HD,
            transcendentals=heads * rows * rows * 4,
            bytes_accessed=8 * rows * heads * HD,
        ),
    )(info, start, valid, q_t, *blocks, *blocks)


def attend_back_kernel(slots, group, info_ref, start_ref, q_ref, do_ref, o_ref, lse_ref, *refs):
    k_refs = refs[:slots]
    v_refs = refs[slots : 2 * slots]
    dq_ref, dkv_ref, keys_s, values_s, keys_t_s, dk_s, dv_s, q_s, do_s, dq_s, delta_s = refs[
        2 * slots :
    ]
    rows = q_ref.shape[1]
    per = rows // KT
    tiles = slots * per
    for slot in range(slots):
        for part in range(per):
            cut = slice(part * KT, (part + 1) * KT)
            tile = slot * per + part
            keys_s[tile] = k_refs[slot][:, cut].T
            keys_t_s[tile] = k_refs[slot][:, cut]
            values_s[tile] = v_refs[slot][:, cut].T
    dk_s[...] = jnp.zeros_like(dk_s)
    dv_s[...] = jnp.zeros_like(dv_s)
    for q_tile in range(rows // QT):
        q_cut = slice(q_tile * QT, (q_tile + 1) * QT)
        for head in range(group):
            h_cut = slice(head * HD, (head + 1) * HD)
            q_s[head] = q_ref[h_cut, q_cut].T
            do_s[head] = do_ref[h_cut, q_cut].T
            delta_s[head : head + 1, :] = jnp.sum(
                do_ref[h_cut, q_cut].astype(F32) * o_ref[h_cut, q_cut], axis=0, keepdims=True
            )
        dq_s[...] = jnp.zeros_like(dq_s)
        start_row = start_ref[:, q_cut]

        def step(tile, carry, q_tile=q_tile, q_cut=q_cut, start_row=start_row):
            active, key_base, q_base = tile_active(info_ref, tiles, tile, q_tile)

            @pl.when(active)
            def _():
                allowed = tile_mask(key_base, q_base, start_row)
                keys = keys_s[tile]
                values = values_s[tile]
                keys_t = keys_t_s[tile]
                dk = dk_s[tile]
                dv = dv_s[tile]
                for head in range(group):
                    h_cut = slice(head * HD, (head + 1) * HD)
                    scores = jnp.dot(keys, q_ref[h_cut, q_cut], preferred_element_type=F32)
                    scores = jnp.where(allowed, scores * SCALE2, MASKED_SCORE)
                    prob = jnp.exp2(scores - lse_ref[0, head : head + 1, q_cut])
                    prob_grad = jnp.dot(values, do_ref[h_cut, q_cut], preferred_element_type=F32)
                    d_scores = (prob * (prob_grad - delta_s[head : head + 1, :])).astype(BF)
                    dv = dv + jnp.dot(prob.astype(BF), do_s[head], preferred_element_type=F32)
                    dk = dk + jnp.dot(d_scores, q_s[head], preferred_element_type=F32)
                    dq_s[head] += jnp.dot(keys_t, d_scores, preferred_element_type=F32)
                dk_s[tile] = dk
                dv_s[tile] = dv

            return carry

        lax.fori_loop(0, tiles, step, 0)
        for head in range(group):
            dq_ref[head * HD : (head + 1) * HD, q_cut] = dq_s[head]
    for slot in range(slots):
        for part in range(per):
            cut = slice(part * KT, (part + 1) * KT)
            tile = slot * per + part
            dkv_ref[slot, 0, :, cut] = (dk_s[tile].T * (1.0 / math.sqrt(HD))).astype(BF)
            dkv_ref[slot, 1, :, cut] = dv_s[tile].T.astype(BF)


def attend_back(info, start, q_t, do_t, o_t, lse, blocks, kv_heads):
    slots = len(blocks)
    heads = q_t.shape[0] // HD
    group = heads // kv_heads
    rows = q_t.shape[1]
    tiles = slots * (rows // KT)
    row_spec = pl.BlockSpec((1, rows), lambda g: (0, 0))
    q_spec = pl.BlockSpec((group * HD, rows), lambda g: (g, 0))
    return pl.pallas_call(
        functools.partial(attend_back_kernel, slots, group),
        grid=(kv_heads,),
        in_specs=[pl.BlockSpec(memory_space=pltpu.SMEM), row_spec, q_spec, q_spec, q_spec]
        + [pl.BlockSpec((1, group, rows), lambda g: (g, 0, 0))]
        + [pl.BlockSpec((HD, rows), lambda g: (g, 0))] * slots
        + [pl.BlockSpec((HD, rows), lambda g: (kv_heads + g, 0))] * slots,
        out_specs=[q_spec, pl.BlockSpec((slots, 2, HD, rows), lambda g: (0, 0, g, 0))],
        out_shape=[
            jax.ShapeDtypeStruct(q_t.shape, F32),
            jax.ShapeDtypeStruct((slots, 2, kv_heads * HD, rows), BF),
        ],
        scratch_shapes=[
            pltpu.VMEM((tiles, KT, HD), BF),
            pltpu.VMEM((tiles, KT, HD), BF),
            pltpu.VMEM((tiles, HD, KT), BF),
            pltpu.VMEM((tiles, KT, HD), F32),
            pltpu.VMEM((tiles, KT, HD), F32),
            pltpu.VMEM((group, QT, HD), BF),
            pltpu.VMEM((group, QT, HD), BF),
            pltpu.VMEM((group, HD, QT), F32),
            pltpu.VMEM((group, QT), F32),
        ],
        name="attend_back",
        cost_estimate=pl.CostEstimate(
            flops=10 * heads * rows * rows * 4 * HD,
            transcendentals=heads * rows * rows * 4,
            bytes_accessed=16 * rows * heads * HD,
        ),
    )(info, start, q_t, do_t, o_t, lse, *blocks, *blocks)


def ffn_kernel(n_ref, da_ref, wg_ref, wu_ref, act_ref, dg_ref, du_ref):
    normed = n_ref[...]
    gate = jnp.dot(normed, wg_ref[...], preferred_element_type=F32)
    up = jnp.dot(normed, wu_ref[...], preferred_element_type=F32)
    sig = jax.nn.sigmoid(gate)
    silu = gate * sig
    act_ref[...] = (silu * up).astype(BF)
    d_act = da_ref[...]
    dg_ref[...] = (d_act * up * sig * (1.0 + gate * (1.0 - sig))).astype(BF)
    du_ref[...] = (d_act * silu).astype(BF)


def ffn_forward(normed, d_act, w_gate, w_up):
    rows, width = normed.shape
    units = w_gate.shape[1]
    step = min(512, units)
    tile = pl.BlockSpec((rows, step), lambda j: (0, j))
    weight = pl.BlockSpec((width, step), lambda j: (0, j))
    return pl.pallas_call(
        ffn_kernel,
        grid=(units // step,),
        in_specs=[pl.BlockSpec((rows, width), lambda j: (0, 0)), tile, weight, weight],
        out_specs=[tile, tile, tile],
        out_shape=[jax.ShapeDtypeStruct((rows, units), BF)] * 3,
        name="gate_up",
        cost_estimate=pl.CostEstimate(
            flops=4 * rows * width * units,
            transcendentals=rows * units,
            bytes_accessed=4 * width * units + 2 * rows * width + 10 * rows * units,
        ),
    )(normed, d_act, w_gate, w_up)


def pair_nt_kernel(a_ref, b_ref, wa_ref, wb_ref, o_ref):
    o_ref[...] = (
        dims(a_ref[...], wa_ref[...], 1, 1) + dims(b_ref[...], wb_ref[...], 1, 1)
    ).astype(BF)


def pair_nt(a, b, w_a, w_b):
    rows, units = a.shape
    width = w_a.shape[0]
    step = min(512, width)
    full = pl.BlockSpec((rows, units), lambda j: (0, 0))
    weight = pl.BlockSpec((step, units), lambda j: (j, 0))
    return pl.pallas_call(
        pair_nt_kernel,
        grid=(width // step,),
        in_specs=[full, full, weight, weight],
        out_specs=pl.BlockSpec((rows, step), lambda j: (0, j)),
        out_shape=jax.ShapeDtypeStruct((rows, width), BF),
        name="d_normed_two",
        cost_estimate=pl.CostEstimate(
            flops=4 * rows * width * units,
            transcendentals=0,
            bytes_accessed=4 * width * units + 4 * rows * units + 2 * rows * width,
        ),
    )(a, b, w_a, w_b)


def grad_down_kernel(a_ref, b_ref, ca_ref, cb_ref, o_ref):
    o_ref[...] = (
        dims(a_ref[...], ca_ref[...], 0, 0) + dims(b_ref[...], cb_ref[...], 0, 0)
    ).astype(BF)


def grad_down_of(act, act_other, cot, cot_other):
    rows, units = act.shape
    width = cot.shape[1]
    step = min(512, units)
    tile = pl.BlockSpec((rows, step), lambda j: (0, j))
    full = pl.BlockSpec((rows, width), lambda j: (0, 0))
    return pl.pallas_call(
        grad_down_kernel,
        grid=(units // step,),
        in_specs=[tile, tile, full, full],
        out_specs=pl.BlockSpec((step, width), lambda j: (j, 0)),
        out_shape=jax.ShapeDtypeStruct((units, width), BF),
        name="grad_down",
        cost_estimate=pl.CostEstimate(
            flops=4 * rows * width * units,
            transcendentals=0,
            bytes_accessed=4 * rows * units + 4 * rows * width + 2 * width * units,
        ),
    )(act, act_other, cot, cot_other)


def grad_in_kernel(half, n_ref, m_ref, ga_ref, gb_ref, ua_ref, ub_ref, o_ref):
    def of(a_ref, b_ref):
        o_ref[...] = (
            dims(n_ref[...], a_ref[...], 0, 0) + dims(m_ref[...], b_ref[...], 0, 0)
        ).astype(BF)

    pl.when(pl.program_id(0) < half)(lambda: of(ga_ref, gb_ref))
    pl.when(pl.program_id(0) >= half)(lambda: of(ua_ref, ub_ref))


def grad_in_of(normed, normed_other, dg, dg_other, du, du_other):
    rows, width = normed.shape
    units = dg.shape[1]
    step = min(512, units)
    half = units // step
    full = pl.BlockSpec((rows, width), lambda j: (0, 0))
    first = pl.BlockSpec((rows, step), lambda j: (0, jnp.minimum(j, half - 1)))
    second = pl.BlockSpec((rows, step), lambda j: (0, jnp.maximum(j - half, 0)))
    return pl.pallas_call(
        functools.partial(grad_in_kernel, half),
        grid=(2 * half,),
        in_specs=[full, full, first, first, second, second],
        out_specs=pl.BlockSpec((width, step), lambda j: (0, j)),
        out_shape=jax.ShapeDtypeStruct((width, 2 * units), BF),
        name="grad_gate_up",
        cost_estimate=pl.CostEstimate(
            flops=8 * rows * width * units,
            transcendentals=0,
            bytes_accessed=8 * rows * units + 4 * rows * width + 4 * width * units,
        ),
    )(normed, normed_other, dg, dg_other, du, du_other)


def norm_back(grad_normed, gain, values, inverse):
    scaled = grad_normed * gain
    return inverse * scaled - values * inverse**3 * jnp.mean(
        scaled * values, axis=-1, keepdims=True
    )


def body(
    tokens,
    attn_gain,
    w_query,
    w_key,
    w_value,
    w_out,
    ffn_gain,
    w_gate,
    w_up,
    w_down,
    doc_lengths,
    cotangent,
):
    rows, width = tokens.shape
    wide = lax.axis_size("wide")
    narrow = lax.axis_size("narrow")
    me_wide = lax.axis_index("wide")
    me = lax.axis_index("narrow")
    core = me_wide % 2
    kv_heads = w_key.shape[1] // HD
    shard = rows // narrow
    part = width // wide
    hops = wide // 4
    half_groups = [list(range(0, wide, 2)), list(range(1, wide, 2))]

    def other_core(value):
        return lax.ppermute(value, "wide", [(i, i ^ 1) for i in range(wide)])

    def chips_up(value, hop):
        return lax.ppermute(value, "wide", [(i, i + 2 * hop) for i in range(wide - 2 * hop)])

    def chips_down(value, hop):
        return lax.ppermute(value, "wide", [(i + 2 * hop, i) for i in range(wide - 2 * hop)])

    def swap(value, distance):
        return lax.ppermute(value, "narrow", [(i, i ^ distance) for i in range(narrow)])

    def rows_of(value, distance):
        return lax.dynamic_slice_in_dim(value, (me ^ distance) * shard, shard, 0)

    def sum_pieces(pieces):
        total = pieces[0].astype(F32)
        for distance in range(1, narrow):
            total = total + swap(pieces[distance], distance).astype(F32)
        return total

    def gather_near(piece):
        return [piece] + [swap(piece, distance) for distance in range(1, narrow)]

    def in_order(pieces):
        out = jnp.zeros((rows, width), pieces[0].dtype)
        for distance in range(narrow):
            out = lax.dynamic_update_slice_in_dim(
                out, pieces[distance], (me ^ distance) * shard, 0
            )
        return out

    def columns_of(value, which):
        return jnp.concatenate(
            [
                lax.dynamic_slice_in_dim(value, (2 * chip + which) * part, part, 1)
                for chip in range(wide // 2)
            ],
            axis=1,
        )

    def both_cores(value):
        return columns_of(value, core), other_core(columns_of(value, 1 - core))

    def scatter(value, dimension):
        return lax.psum_scatter(
            value,
            "wide",
            scatter_dimension=dimension,
            axis_index_groups=half_groups,
            tiled=True,
        )

    gain_one = attn_gain.astype(F32)
    gain_two = ffn_gain.astype(F32)

    base = me_wide * rows
    index = base + jnp.arange(rows, dtype=jnp.int32)
    start, valid = doc_offsets(doc_lengths, index)
    angle = jnp.asarray(inverse_frequencies(HD))[:, None] * (index - start).astype(F32)[None, :]
    cosine = jnp.cos(angle)
    sine = jnp.sin(angle)
    first_key = jnp.where(valid, start, index)
    key_tiles = []
    for hop in range(hops + 1):
        for side in range(2):
            block = ((me_wide // 2 - hop) * 2 + (core ^ side)) * rows
            key_tiles += [block + tile * KT for tile in range(rows // KT)]
    info = jnp.concatenate(
        [jnp.stack(key_tiles).astype(jnp.int32), base[None].astype(jnp.int32), first_key[::QT]]
    )
    start_row = first_key[None, :]
    valid_row = valid.astype(jnp.int32)[None, :]

    inputs = tokens.astype(F32)
    inv_one = lax.rsqrt(jnp.mean(inputs * inputs, axis=-1, keepdims=True) + NORM_EPS)
    normed = (inputs * inv_one * gain_one).astype(BF)
    keys_t = rotate_t(dims(w_key, normed, 0, 1), cosine, sine).astype(BF)
    values_t = dims(w_value, normed, 0, 1).astype(BF)
    packed = jnp.concatenate([keys_t, values_t], axis=0)
    blocks = [packed, other_core(packed)]
    for hop in range(1, hops + 1):
        near = chips_up(packed, hop)
        blocks += [near, other_core(near)]
    query_t = rotate_t(dims(w_query, normed, 0, 1), cosine, sine).astype(BF)
    o_t, mixed_t, lse = attend(info, start_row, valid_row, query_t, blocks, kv_heads)

    attn_part = dims(mixed_t, w_out, 0, 0).astype(BF)
    attn_sum = sum_pieces([rows_of(attn_part, d) for d in range(narrow)])
    inputs_mine = rows_of(tokens, 0).astype(F32)
    hidden_one = inputs_mine + attn_sum
    inv_two = lax.rsqrt(jnp.mean(hidden_one * hidden_one, axis=-1, keepdims=True) + NORM_EPS)
    normed_two_mine = (hidden_one * inv_two * gain_two).astype(BF)

    cot_near = jnp.concatenate([rows_of(cotangent, d) for d in range(narrow)], axis=0)
    cot_mine = cot_near[:shard].astype(F32)
    d_act = dims(cot_near, w_down, 1, 1)
    normed_two = jnp.concatenate(gather_near(normed_two_mine), axis=0)
    act, d_gate, d_up = ffn_forward(normed_two, d_act, w_gate, w_up)
    cot_cols, cot_cols_other = both_cores(cot_near)
    normed_two_cols, normed_two_cols_other = both_cores(normed_two)
    act_other = other_core(act)
    d_gate_other = other_core(d_gate)
    d_up_other = other_core(d_up)
    grad_down = scatter(grad_down_of(act, act_other, cot_cols, cot_cols_other), 1)

    d_norm_part = pair_nt(d_gate, d_up, w_gate, w_up)
    d_norm_two = sum_pieces([d_norm_part[d * shard : (d + 1) * shard] for d in range(narrow)])
    grad_gate_up = scatter(
        grad_in_of(
            normed_two_cols, normed_two_cols_other, d_gate, d_gate_other, d_up, d_up_other
        ),
        0,
    )
    units = w_gate.shape[1]
    grad_gate = grad_gate_up[:, :units].astype(F32)
    grad_up = grad_gate_up[:, units:].astype(F32)

    ffn_part = jnp.dot(act, w_down, preferred_element_type=F32).astype(BF)
    ffn_sum = sum_pieces([ffn_part[d * shard : (d + 1) * shard] for d in range(narrow)])
    output = in_order(gather_near((hidden_one + ffn_sum).astype(BF)))

    gain_two_part = jnp.sum(d_norm_two * hidden_one * inv_two, axis=0)
    d_hidden = cot_mine + norm_back(d_norm_two, gain_two, hidden_one, inv_two)
    d_hidden_b = in_order(gather_near(d_hidden.astype(BF)))

    d_mixed_t = jnp.where(valid[None, :], dims(w_out, d_hidden_b, 1, 1), 0.0).astype(BF)
    d_query_r, d_blocks = attend_back(
        info, start_row, query_t, d_mixed_t, o_t, lse, blocks, kv_heads
    )
    d_blocks = d_blocks.reshape(2 * (hops + 1), 2 * kv_heads * HD, rows)
    for_other = other_core(d_blocks[1::2])
    d_kv = d_blocks[0].astype(F32) + for_other[0].astype(F32)
    for hop in range(1, hops + 1):
        both = (d_blocks[2 * hop].astype(F32) + for_other[hop].astype(F32)).astype(BF)
        d_kv = d_kv + chips_down(both, hop).astype(F32)
    d_query = rotate_t(d_query_r * (1.0 / math.sqrt(HD)), cosine, -sine).astype(BF)
    d_keys = rotate_t(d_kv[: kv_heads * HD], cosine, -sine).astype(BF)
    d_values = d_kv[kv_heads * HD :].astype(BF)

    d_proj = jnp.concatenate([d_query, d_keys, d_values], axis=0)
    d_proj_other = other_core(d_proj)
    normed_cols, normed_cols_other = both_cores(normed)
    d_hidden_cols, d_hidden_cols_other = both_cores(d_hidden_b)
    mixed_other = other_core(mixed_t)
    grad_out = jnp.dot(mixed_t, d_hidden_cols, preferred_element_type=F32) + jnp.dot(
        mixed_other, d_hidden_cols_other, preferred_element_type=F32
    )
    grad_proj = jnp.dot(d_proj, normed_cols, preferred_element_type=F32) + jnp.dot(
        d_proj_other, normed_cols_other, preferred_element_type=F32
    )
    grad_out = scatter(grad_out.astype(BF), 1).astype(F32)
    grad_proj = scatter(grad_proj.astype(BF), 1).astype(F32)
    q_width = w_query.shape[1]
    k_width = w_key.shape[1]
    grad_query = grad_proj[:q_width].T
    grad_key = grad_proj[q_width : q_width + k_width].T
    grad_value = grad_proj[q_width + k_width :].T

    norm_one_part = dims(d_query, w_query, 0, 1) + dims(d_keys, w_key, 0, 1) + dims(
        d_values, w_value, 0, 1
    )
    norm_one_part = norm_one_part.astype(BF)
    d_norm_one = sum_pieces([rows_of(norm_one_part, d) for d in range(narrow)])
    inv_one_mine = rows_of(inv_one, 0)
    gain_one_part = jnp.sum(d_norm_one * inputs_mine * inv_one_mine, axis=0)
    input_mine = d_hidden + norm_back(d_norm_one, gain_one, inputs_mine, inv_one_mine)
    input_grad = in_order(gather_near(input_mine.astype(BF)))

    gains = lax.psum(jnp.stack([gain_one_part, gain_two_part]), ("wide", "narrow"))
    gains = lax.dynamic_slice_in_dim(gains, me_wide * part, part, 1)
    return (
        output,
        input_grad,
        gains[0],
        grad_query,
        grad_key,
        grad_value,
        grad_out,
        gains[1],
        grad_gate,
        grad_up,
        grad_down.astype(F32),
    )


def solution(mesh):
    in_specs = (
        P("wide", None),
        P(),
        P(None, "narrow"),
        P(None, "narrow"),
        P(None, "narrow"),
        P("narrow", None),
        P(),
        P(None, "narrow"),
        P(None, "narrow"),
        P("narrow", None),
        P(),
        P("wide", None),
    )
    out_specs = (
        P("wide", None),
        P("wide", None),
        P("wide"),
        P("wide", "narrow"),
        P("wide", "narrow"),
        P("wide", "narrow"),
        P("narrow", "wide"),
        P("wide"),
        P("wide", "narrow"),
        P("wide", "narrow"),
        P("narrow", "wide"),
    )
    return jax.shard_map(body, mesh=mesh, in_specs=in_specs, out_specs=out_specs, check_vma=False)
```

```python
import functools
import math

import jax
import jax.numpy as jnp
import numpy as np
from jax import lax
from jax.experimental import pallas as pl
from jax.experimental.pallas import tpu as pltpu
from jax.sharding import PartitionSpec as P

HD = 64
DOCS = 12
NORM_EPS = 1e-05
MASKED_SCORE = -1e30
LOG2E = math.log2(math.e)
SCALE2 = LOG2E / math.sqrt(HD)
KT = 256
HALVES = 2
BF = jnp.bfloat16
F32 = jnp.float32


def inverse_frequencies(head_size):
    frequency = 1.0 / 500000.0 ** (np.arange(0, head_size, 2) / head_size)
    wavelength = 2 * math.pi / frequency
    smoothing = (8192.0 / wavelength - 1.0) / 3.0
    scaled_freq = np.where(wavelength > 8192.0, frequency / 32.0, frequency)
    middle_band = (wavelength <= 8192.0) & (wavelength >= 2048.0)
    scaled_freq = np.where(
        middle_band, (1 - smoothing) * frequency / 32.0 + smoothing * frequency, scaled_freq
    )
    return scaled_freq.astype(np.float32)


def doc_offsets(doc_lengths, index):
    ends = jnp.cumsum(doc_lengths)
    passed = (index[None, :] >= ends[:, None]).astype(jnp.int32)
    start = jnp.sum(passed * doc_lengths[:, None], axis=0)
    valid = index < ends[DOCS - 2]
    return start, valid


def rotate_t(values, cosine, sine):
    heads = values.shape[0] // HD
    shaped = values.reshape(heads, 2, HD // 2, values.shape[1])
    first = shaped[:, 0]
    second = shaped[:, 1]
    return jnp.stack(
        [first * cosine - second * sine, second * cosine + first * sine], axis=1
    ).reshape(values.shape)


def dims(left, right, a, b):
    return lax.dot_general(left, right, (((a,), (b,)), ((), ())), preferred_element_type=F32)


def tile_active(info_ref, tiles, tile, q_tile, q_rows):
    key_base = info_ref[tile]
    q_base = info_ref[tiles] + q_tile * q_rows
    first_key = info_ref[tiles + 1 + q_tile]
    return (key_base <= q_base + q_rows - 1) & (key_base + KT > first_key), key_base, q_base


def tile_mask(key_base, q_base, start_row):
    q_rows = start_row.shape[1]
    keys = key_base + lax.broadcasted_iota(jnp.int32, (KT, q_rows), 0)
    queries = q_base + lax.broadcasted_iota(jnp.int32, (KT, q_rows), 1)
    return (keys <= queries) & (keys >= start_row)


def attend_kernel(slots, group, half, info_ref, start_ref, valid_ref, q_ref, *refs):
    k_refs = refs[:slots]
    v_refs = refs[slots : 2 * slots]
    o_ref, mixed_ref, lse_ref, keys_s, values_s, top_s, sum_s, acc_s = refs[2 * slots :]
    q_rows = q_ref.shape[1]
    per = k_refs[0].shape[1] // KT
    tiles = slots * per
    for slot in range(slots):
        for part in range(per):
            tile = slot * per + part
            cut = slice(part * KT, (part + 1) * KT)

            @pl.when(tile_active(info_ref, tiles, tile, half, q_rows)[0])
            def _(tile=tile, slot=slot, cut=cut):
                keys_s[tile] = k_refs[slot][:, cut].T
                values_s[tile] = v_refs[slot][:, cut]

    top_s[...] = jnp.full_like(top_s, MASKED_SCORE)
    sum_s[...] = jnp.zeros_like(sum_s)
    acc_s[...] = jnp.zeros_like(acc_s)
    start_row = start_ref[...]

    def step(tile, carry):
        active, key_base, q_base = tile_active(info_ref, tiles, tile, half, q_rows)

        @pl.when(active)
        def _():
            allowed = tile_mask(key_base, q_base, start_row)
            keys = keys_s[tile]
            values = values_s[tile]
            for head in range(group):
                scores = jnp.dot(
                    keys, q_ref[head * HD : (head + 1) * HD, :], preferred_element_type=F32
                )
                scores = jnp.where(allowed, scores, MASKED_SCORE)
                old = top_s[head : head + 1, :]
                new = jnp.maximum(old, jnp.max(scores, axis=0, keepdims=True))
                weight = jnp.exp2((scores - new) * SCALE2)
                decay = jnp.exp2((old - new) * SCALE2)
                top_s[head : head + 1, :] = new
                sum_s[head : head + 1, :] = sum_s[head : head + 1, :] * decay + jnp.sum(
                    weight, axis=0, keepdims=True
                )
                acc_s[head] = acc_s[head] * decay + jnp.dot(
                    values, weight.astype(BF), preferred_element_type=F32
                )

        return carry

    lax.fori_loop(0, tiles, step, 0)
    for head in range(group):
        h_cut = slice(head * HD, (head + 1) * HD)
        total = sum_s[head : head + 1, :]
        out = acc_s[head] / total
        o_ref[h_cut, :] = out
        mixed_ref[h_cut, :] = jnp.where(valid_ref[...] != 0, out, 0.0).astype(BF)
        lse_ref[0, head : head + 1, :] = top_s[head : head + 1, :] * SCALE2 + jnp.log(total) * LOG2E


def attend(half, info, start, valid, q_t, blocks, kv_heads):
    slots = len(blocks)
    heads = q_t.shape[0] // HD
    group = heads // kv_heads
    rows = q_t.shape[1]
    q_rows = rows // HALVES
    tiles = slots * (rows // KT)
    row_spec = pl.BlockSpec((1, q_rows), lambda g: (0, half))
    out_spec = pl.BlockSpec((group * HD, q_rows), lambda g: (g, 0))
    return pl.pallas_call(
        functools.partial(attend_kernel, slots, group, half),
        grid=(kv_heads,),
        in_specs=[
            pl.BlockSpec(memory_space=pltpu.SMEM),
            row_spec,
            row_spec,
            pl.BlockSpec((group * HD, q_rows), lambda g: (g, half)),
        ]
        + [pl.BlockSpec((HD, rows), lambda g: (g, 0))] * slots
        + [pl.BlockSpec((HD, rows), lambda g: (kv_heads + g, 0))] * slots,
        out_specs=[out_spec, out_spec, pl.BlockSpec((1, group, q_rows), lambda g: (g, 0, 0))],
        out_shape=[
            jax.ShapeDtypeStruct((heads * HD, q_rows), F32),
            jax.ShapeDtypeStruct((heads * HD, q_rows), BF),
            jax.ShapeDtypeStruct((kv_heads, group, q_rows), F32),
        ],
        scratch_shapes=[
            pltpu.VMEM((tiles, KT, HD), BF),
            pltpu.VMEM((tiles, HD, KT), BF),
            pltpu.VMEM((group, q_rows), F32),
            pltpu.VMEM((group, q_rows), F32),
            pltpu.VMEM((group, HD, q_rows), F32),
        ],
        name="attend",
        cost_estimate=pl.CostEstimate(
            flops=4 * heads * q_rows * rows * 4 * HD,
            transcendentals=heads * q_rows * rows * 4,
            bytes_accessed=8 * rows * heads * HD,
        ),
    )(info, start, valid, q_t, *blocks, *blocks)


def attend_back_kernel(slots, group, info_ref, start_ref, q_ref, do_ref, *refs):
    o_refs = refs[:HALVES]
    lse_refs = refs[HALVES : 2 * HALVES]
    refs = refs[2 * HALVES :]
    k_refs = refs[:slots]
    v_refs = refs[slots : 2 * slots]
    dq_ref, dkv_ref, keys_s, values_s, keys_t_s, dk_s, dv_s, q_s, do_s, dq_s, delta_s = refs[
        2 * slots :
    ]
    rows = q_ref.shape[1]
    q_rows = rows // HALVES
    per = rows // KT
    tiles = slots * per

    def any_active(tile):
        found = tile_active(info_ref, tiles, tile, 0, q_rows)[0]
        for half in range(1, HALVES):
            found = found | tile_active(info_ref, tiles, tile, half, q_rows)[0]
        return found

    for slot in range(slots):
        for part in range(per):
            tile = slot * per + part
            cut = slice(part * KT, (part + 1) * KT)

            @pl.when(any_active(tile))
            def _(tile=tile, slot=slot, cut=cut):
                keys_s[tile] = k_refs[slot][:, cut].T
                keys_t_s[tile] = k_refs[slot][:, cut]
                values_s[tile] = v_refs[slot][:, cut].T
                dk_s[tile] = jnp.zeros((KT, HD), F32)
                dv_s[tile] = jnp.zeros((KT, HD), F32)

    for half in range(HALVES):
        q_cut = slice(half * q_rows, (half + 1) * q_rows)
        for head in range(group):
            h_cut = slice(head * HD, (head + 1) * HD)
            q_s[head] = q_ref[h_cut, q_cut].T
            do_s[head] = do_ref[h_cut, q_cut].T
            delta_s[head : head + 1, :] = jnp.sum(
                do_ref[h_cut, q_cut].astype(F32) * o_refs[half][h_cut, :], axis=0, keepdims=True
            )
        dq_s[...] = jnp.zeros_like(dq_s)
        start_row = start_ref[:, q_cut]

        def step(tile, carry, half=half, q_cut=q_cut, start_row=start_row):
            active, key_base, q_base = tile_active(info_ref, tiles, tile, half, q_rows)

            @pl.when(active)
            def _():
                allowed = tile_mask(key_base, q_base, start_row)
                keys = keys_s[tile]
                values = values_s[tile]
                keys_t = keys_t_s[tile]
                dk = dk_s[tile]
                dv = dv_s[tile]
                for head in range(group):
                    h_cut = slice(head * HD, (head + 1) * HD)
                    scores = jnp.dot(keys, q_ref[h_cut, q_cut], preferred_element_type=F32)
                    scores = jnp.where(allowed, scores * SCALE2, MASKED_SCORE)
                    prob = jnp.exp2(scores - lse_refs[half][0, head : head + 1, :])
                    prob_grad = jnp.dot(values, do_ref[h_cut, q_cut], preferred_element_type=F32)
                    d_scores = (prob * (prob_grad - delta_s[head : head + 1, :])).astype(BF)
                    dv = dv + jnp.dot(prob.astype(BF), do_s[head], preferred_element_type=F32)
                    dk = dk + jnp.dot(d_scores, q_s[head], preferred_element_type=F32)
                    dq_s[head] += jnp.dot(keys_t, d_scores, preferred_element_type=F32)
                dk_s[tile] = dk
                dv_s[tile] = dv

            return carry

        lax.fori_loop(0, tiles, step, 0)
        for head in range(group):
            dq_ref[head * HD : (head + 1) * HD, q_cut] = dq_s[head]
    for slot in range(slots):
        for part in range(per):
            cut = slice(part * KT, (part + 1) * KT)
            tile = slot * per + part
            active = any_active(tile)

            @pl.when(active)
            def _(tile=tile, slot=slot, cut=cut):
                dkv_ref[slot, 0, :, cut] = (dk_s[tile].T * (1.0 / math.sqrt(HD))).astype(BF)
                dkv_ref[slot, 1, :, cut] = dv_s[tile].T.astype(BF)

            @pl.when(jnp.logical_not(active))
            def _(slot=slot, cut=cut):
                dkv_ref[slot, 0, :, cut] = jnp.zeros((HD, KT), BF)
                dkv_ref[slot, 1, :, cut] = jnp.zeros((HD, KT), BF)


def attend_back(info, start, q_t, do_t, outs, lses, blocks, kv_heads):
    slots = len(blocks)
    heads = q_t.shape[0] // HD
    group = heads // kv_heads
    rows = q_t.shape[1]
    q_rows = rows // HALVES
    tiles = slots * (rows // KT)
    row_spec = pl.BlockSpec((1, rows), lambda g: (0, 0))
    q_spec = pl.BlockSpec((group * HD, rows), lambda g: (g, 0))
    return pl.pallas_call(
        functools.partial(attend_back_kernel, slots, group),
        grid=(kv_heads,),
        in_specs=[pl.BlockSpec(memory_space=pltpu.SMEM), row_spec, q_spec, q_spec]
        + [pl.BlockSpec((group * HD, q_rows), lambda g: (g, 0))] * HALVES
        + [pl.BlockSpec((1, group, q_rows), lambda g: (g, 0, 0))] * HALVES
        + [pl.BlockSpec((HD, rows), lambda g: (g, 0))] * slots
        + [pl.BlockSpec((HD, rows), lambda g: (kv_heads + g, 0))] * slots,
        out_specs=[q_spec, pl.BlockSpec((slots, 2, HD, rows), lambda g: (0, 0, g, 0))],
        out_shape=[
            jax.ShapeDtypeStruct(q_t.shape, F32),
            jax.ShapeDtypeStruct((slots, 2, kv_heads * HD, rows), BF),
        ],
        scratch_shapes=[
            pltpu.VMEM((tiles, KT, HD), BF),
            pltpu.VMEM((tiles, KT, HD), BF),
            pltpu.VMEM((tiles, HD, KT), BF),
            pltpu.VMEM((tiles, KT, HD), F32),
            pltpu.VMEM((tiles, KT, HD), F32),
            pltpu.VMEM((group, q_rows, HD), BF),
            pltpu.VMEM((group, q_rows, HD), BF),
            pltpu.VMEM((group, HD, q_rows), F32),
            pltpu.VMEM((group, q_rows), F32),
        ],
        name="attend_back",
        cost_estimate=pl.CostEstimate(
            flops=10 * heads * rows * rows * 4 * HD,
            transcendentals=heads * rows * rows * 4,
            bytes_accessed=16 * rows * heads * HD,
        ),
    )(info, start, q_t, do_t, *outs, *lses, *blocks, *blocks)


def vmem_call(kernel, out_shape, name, *operands, smem=0):
    whole = pl.BlockSpec(memory_space=pltpu.VMEM)
    moved = sum(math.prod(o.shape) * o.dtype.itemsize for o in operands)
    return pl.pallas_call(
        kernel,
        in_specs=[pl.BlockSpec(memory_space=pltpu.SMEM)] * smem + [whole] * (len(operands) - smem),
        out_specs=jax.tree.map(lambda _: whole, out_shape),
        out_shape=out_shape,
        name=name,
        cost_estimate=pl.CostEstimate(flops=moved, transcendentals=0, bytes_accessed=2 * moved),
    )(*operands)


def rms_scale(values):
    return lax.rsqrt(jnp.mean(values * values, axis=-1, keepdims=True) + NORM_EPS)


def row_sum(refs):
    total = refs[0][...].astype(F32)
    for ref in refs[1:]:
        total = total + ref[...].astype(F32)
    return total


def rows_call(kernel, out_shape, name, ids, narrow, rowed, halves, *operands):
    rows, width = rowed.shape
    piece = rows // (HALVES * narrow)
    mine = [
        pl.BlockSpec((piece, width), lambda i, ids, h=h: (h * narrow + ids[0], 0)) for h in halves
    ]

    def spec(shape):
        return pl.BlockSpec(shape.shape, lambda i, ids: (0, 0))

    moved = sum(math.prod(o.shape) * o.dtype.itemsize for o in operands)
    return pl.pallas_call(
        kernel,
        grid_spec=pltpu.PrefetchScalarGridSpec(
            num_scalar_prefetch=1,
            grid=(1,),
            in_specs=mine + [spec(o) for o in operands],
            out_specs=[spec(o) for o in out_shape],
        ),
        out_shape=out_shape,
        name=name,
        cost_estimate=pl.CostEstimate(flops=moved, transcendentals=0, bytes_accessed=2 * moved),
    )(ids, *([rowed] * len(mine)), *operands)


def norm_two_kernel(ids_ref, x_ref, gain_ref, *refs):
    hidden_ref, normed_ref = refs[-2:]
    hidden = x_ref[...].astype(F32) + row_sum(refs[:-2])
    hidden_ref[...] = hidden
    normed_ref[...] = (hidden * rms_scale(hidden) * gain_ref[...]).astype(BF)


def norm_back(grad_normed, gain, values, inverse):
    scaled = grad_normed * gain
    return inverse * scaled - values * inverse**3 * jnp.mean(
        scaled * values, axis=-1, keepdims=True
    )


def norm_two_back_kernel(ids_ref, *refs):
    cots, hiddens = refs[:HALVES], refs[HALVES : 2 * HALVES]
    gain_ref, pieces = refs[2 * HALVES], refs[2 * HALVES + 1 : -3]
    sum_ref, low_ref, part_ref = refs[-3:]
    piece = cots[0].shape[0]
    parts = 0.0
    for half in range(HALVES):
        cut = slice(half * piece, (half + 1) * piece)
        grad = row_sum([r.at[cut, :] for r in pieces])
        hidden = hiddens[half][...]
        inverse = rms_scale(hidden)
        parts = parts + jnp.sum(grad * hidden * inverse, axis=0, keepdims=True)
        total = cots[half][...].astype(F32) + norm_back(grad, gain_ref[...], hidden, inverse)
        sum_ref[cut, :] = total
        low_ref[cut, :] = total.astype(BF)
    part_ref[...] = parts


def norm_one_back_kernel(ids_ref, *refs):
    tokens = refs[:HALVES]
    add_ref, gain_ref, pieces = refs[HALVES], refs[HALVES + 1], refs[HALVES + 2 : -2]
    low_ref, part_ref = refs[-2:]
    piece = tokens[0].shape[0]
    parts = 0.0
    for half in range(HALVES):
        cut = slice(half * piece, (half + 1) * piece)
        grad = row_sum([r.at[cut, :] for r in pieces])
        values = tokens[half][...].astype(F32)
        inverse = rms_scale(values)
        parts = parts + jnp.sum(grad * values * inverse, axis=0, keepdims=True)
        low_ref[cut, :] = (
            add_ref[cut, :] + norm_back(grad, gain_ref[...], values, inverse)
        ).astype(BF)
    part_ref[...] = parts


def place_rows(me, out_ref, refs):
    rows = out_ref.shape[0]
    half_rows = rows // HALVES
    count = len(refs)
    part = half_rows // count
    for distance, ref in enumerate(refs):
        owner = me ^ distance
        for half in range(HALVES):
            at = pl.multiple_of(half * half_rows + owner * part, part)
            out_ref[pl.ds(at, part), :] = ref[half * part : (half + 1) * part, :]


def columns_to(core, part, in_ref, own_ref, send_ref):
    for block in range(own_ref.shape[1] // part):
        cut = slice(block * part, (block + 1) * part)
        own_at = pl.multiple_of((2 * block + core) * part, part)
        send_at = pl.multiple_of((2 * block + 1 - core) * part, part)
        own_ref[:, cut] = in_ref[:, pl.ds(own_at, part)]
        send_ref[:, cut] = in_ref[:, pl.ds(send_at, part)]


def in_order_kernel(ids_ref, *refs):
    place_rows(ids_ref[0], refs[-1], refs[:-1])


def in_order(ids, pieces):
    rows = pieces[0].shape[0] * len(pieces)
    return vmem_call(
        in_order_kernel,
        jax.ShapeDtypeStruct((rows, pieces[0].shape[1]), pieces[0].dtype),
        "token_order",
        ids,
        *pieces,
        smem=1,
    )


def near_order_kernel(part, members, ids_ref, in_ref, near_ref, own_ref, send_ref):
    half_rows = in_ref.shape[0] // HALVES
    piece = half_rows // members
    for half in range(HALVES):
        for distance in range(members):
            at = half * half_rows + distance * piece
            source = pl.multiple_of(half * half_rows + (ids_ref[0] ^ distance) * piece, piece)
            near_ref[at : at + piece, :] = in_ref[pl.ds(source, piece), :]
    columns_to(ids_ref[1], part, near_ref, own_ref, send_ref)


def near_order(ids, members, value, part):
    rows, width = value.shape
    half = jax.ShapeDtypeStruct((rows, width // 2), value.dtype)
    return vmem_call(
        functools.partial(near_order_kernel, part, members),
        [jax.ShapeDtypeStruct(value.shape, value.dtype), half, half],
        "near_order",
        ids,
        value,
        smem=1,
    )


def split_columns_kernel(part, ids_ref, in_ref, own_ref, send_ref):
    columns_to(ids_ref[1], part, in_ref, own_ref, send_ref)


def split_columns(ids, value, part):
    half = jax.ShapeDtypeStruct((value.shape[0], value.shape[1] // 2), value.dtype)
    return vmem_call(
        functools.partial(split_columns_kernel, part), [half, half], "columns", ids, value, smem=1
    )


def d_mixed_kernel(part, ids_ref, valid_ref, w_ref, *refs):
    out_ref, own_ref, send_ref, full_s = refs[-4:]
    place_rows(ids_ref[0], full_s, refs[:-4])
    columns_to(ids_ref[1], part, full_s, own_ref, send_ref)
    grad = dims(w_ref[...], full_s[...], 1, 1)
    out_ref[...] = jnp.where(valid_ref[...] != 0, grad, 0.0).astype(BF)


def d_mixed_of(ids, valid, w_out, pieces, part):
    rows = pieces[0].shape[0] * len(pieces)
    inner, width = w_out.shape
    whole = pl.BlockSpec(memory_space=pltpu.VMEM)
    return pl.pallas_call(
        functools.partial(d_mixed_kernel, part),
        in_specs=[pl.BlockSpec(memory_space=pltpu.SMEM)] + [whole] * (2 + len(pieces)),
        out_specs=[whole] * 3,
        out_shape=[
            jax.ShapeDtypeStruct((inner, rows), BF),
            jax.ShapeDtypeStruct((rows, width // 2), BF),
            jax.ShapeDtypeStruct((rows, width // 2), BF),
        ],
        scratch_shapes=[pltpu.VMEM((rows, width), BF)],
        name="d_mixed",
        cost_estimate=pl.CostEstimate(
            flops=2 * rows * inner * width,
            transcendentals=0,
            bytes_accessed=2 * (rows + inner) * width + 4 * rows * width,
        ),
    )(ids, valid, w_out, *pieces)


def ffn_kernel(part, ids_ref, da_ref, wg_ref, wu_ref, *refs):
    act_ref, dg_ref, du_ref, own_ref, send_ref, full_s = refs[-6:]
    pieces = refs[:-6]
    count = pieces[0].shape[0]

    @pl.when(pl.program_id(0) == 0)
    def _():
        for distance, ref in enumerate(pieces):
            full_s[distance * count : (distance + 1) * count, :] = ref[...]
        columns_to(ids_ref[1], part, full_s, own_ref, send_ref)

    normed = full_s[...]
    gate = jnp.dot(normed, wg_ref[...], preferred_element_type=F32)
    up = jnp.dot(normed, wu_ref[...], preferred_element_type=F32)
    sig = jax.nn.sigmoid(gate)
    silu = gate * sig
    act_ref[...] = (silu * up).astype(BF)
    d_act = da_ref[...]
    dg_ref[...] = (d_act * up * sig * (1.0 + gate * (1.0 - sig))).astype(BF)
    du_ref[...] = (d_act * silu).astype(BF)


def ffn_forward(half, ids, pieces, d_act, w_gate, w_up, part):
    count, width = pieces[0].shape
    rows = count * len(pieces)
    units = w_gate.shape[1]
    step = min(512, units)
    tile = pl.BlockSpec((rows, step), lambda j: (0, j))
    weight = pl.BlockSpec((width, step), lambda j: (0, j))
    cols = pl.BlockSpec((rows, width // 2), lambda j: (0, 0))
    return pl.pallas_call(
        functools.partial(ffn_kernel, part),
        grid=(units // step,),
        in_specs=[
            pl.BlockSpec(memory_space=pltpu.SMEM),
            pl.BlockSpec((rows, step), lambda j: (half, j)),
            weight,
            weight,
        ]
        + [pl.BlockSpec((count, width), lambda j: (0, 0))] * len(pieces),
        out_specs=[tile, tile, tile, cols, cols],
        out_shape=[jax.ShapeDtypeStruct((rows, units), BF)] * 3
        + [jax.ShapeDtypeStruct((rows, width // 2), BF)] * 2,
        scratch_shapes=[pltpu.VMEM((rows, width), BF)],
        name="gate_up",
        cost_estimate=pl.CostEstimate(
            flops=4 * rows * width * units,
            transcendentals=rows * units,
            bytes_accessed=4 * width * units + 2 * rows * width + 10 * rows * units,
        ),
    )(ids, d_act, w_gate, w_up, *pieces)


def store_pieces(members, out_ref, halves):
    part = halves[0].shape[0] // members
    for half, value in enumerate(halves):
        low = value.astype(BF)
        for distance in range(members):
            at = (distance * len(halves) + half) * part
            out_ref[at : at + part, :] = low[distance * part : (distance + 1) * part, :]


def pair_nt_kernel(members, *refs):
    wa_ref, wb_ref, o_ref = refs[-3:]
    halves = len(refs[:-3]) // 2
    store_pieces(
        members,
        o_ref,
        [
            dims(refs[h][...], wa_ref[...], 1, 1) + dims(refs[halves + h][...], wb_ref[...], 1, 1)
            for h in range(halves)
        ],
    )


def pair_nt(members, a_halves, b_halves, w_a, w_b):
    half_rows, units = a_halves[0].shape
    rows = half_rows * len(a_halves)
    width = w_a.shape[0]
    step = min(512, width)
    full = pl.BlockSpec((half_rows, units), lambda j: (0, 0))
    weight = pl.BlockSpec((step, units), lambda j: (j, 0))
    return pl.pallas_call(
        functools.partial(pair_nt_kernel, members),
        grid=(width // step,),
        in_specs=[full] * (2 * len(a_halves)) + [weight, weight],
        out_specs=pl.BlockSpec((rows, step), lambda j: (0, j)),
        out_shape=jax.ShapeDtypeStruct((rows, width), BF),
        name="d_normed_two",
        cost_estimate=pl.CostEstimate(
            flops=4 * rows * width * units,
            transcendentals=0,
            bytes_accessed=4 * width * units + 4 * rows * units + 2 * rows * width,
        ),
    )(*a_halves, *b_halves, w_a, w_b)


def down_kernel(members, *refs):
    w_ref, o_ref = refs[-2:]
    store_pieces(
        members,
        o_ref,
        [jnp.dot(ref[...], w_ref[...], preferred_element_type=F32) for ref in refs[:-2]],
    )


def down_of(members, act_halves, w_down):
    half_rows, units = act_halves[0].shape
    rows = half_rows * len(act_halves)
    width = w_down.shape[1]
    step = min(512, width)
    return pl.pallas_call(
        functools.partial(down_kernel, members),
        grid=(width // step,),
        in_specs=[pl.BlockSpec((half_rows, units), lambda j: (0, 0))] * len(act_halves)
        + [pl.BlockSpec((units, step), lambda j: (0, j))],
        out_specs=pl.BlockSpec((rows, step), lambda j: (0, j)),
        out_shape=jax.ShapeDtypeStruct((rows, width), BF),
        name="ffn_down",
        cost_estimate=pl.CostEstimate(
            flops=2 * rows * width * units,
            transcendentals=0,
            bytes_accessed=2 * width * units + 2 * rows * units + 2 * rows * width,
        ),
    )(*act_halves, w_down)


def contract_groups(lefts, rights):
    total = None
    for left, right in zip(lefts, rights, strict=True):
        term = dims(left, right, 0, 0)
        total = term if total is None else total + term
    return total.astype(BF)


def grad_down_kernel(groups, *refs):
    o_ref = refs[-1]
    o_ref[...] = contract_groups(
        [r[...] for r in refs[:groups]], [r[...] for r in refs[groups : 2 * groups]]
    )


def grad_down_of(acts, cots):
    rows, units = acts[0].shape
    width = cots[0].shape[1]
    step = min(512, units)
    groups = len(acts)
    return pl.pallas_call(
        functools.partial(grad_down_kernel, groups),
        grid=(units // step,),
        in_specs=[pl.BlockSpec((rows, step), lambda j: (0, j))] * groups
        + [pl.BlockSpec((rows, width), lambda j: (0, 0))] * groups,
        out_specs=pl.BlockSpec((step, width), lambda j: (j, 0)),
        out_shape=jax.ShapeDtypeStruct((units, width), BF),
        name="grad_down",
        cost_estimate=pl.CostEstimate(
            flops=2 * groups * rows * width * units,
            transcendentals=0,
            bytes_accessed=2 * groups * rows * (units + width) + 2 * width * units,
        ),
    )(*acts, *cots)


def grad_in_kernel(groups, half, *refs):
    o_ref = refs[-1]
    lefts = refs[:groups]

    def of(rights):
        o_ref[...] = contract_groups([r[...] for r in lefts], [r[...] for r in rights])

    pl.when(pl.program_id(0) < half)(lambda: of(refs[groups : 2 * groups]))
    pl.when(pl.program_id(0) >= half)(lambda: of(refs[2 * groups : 3 * groups]))


def grad_in_of(normeds, d_gates, d_ups):
    rows, width = normeds[0].shape
    units = d_gates[0].shape[1]
    step = min(512, units)
    half = units // step
    groups = len(normeds)
    full = pl.BlockSpec((rows, width), lambda j: (0, 0))
    first = pl.BlockSpec((rows, step), lambda j: (0, jnp.minimum(j, half - 1)))
    second = pl.BlockSpec((rows, step), lambda j: (0, jnp.maximum(j - half, 0)))
    return pl.pallas_call(
        functools.partial(grad_in_kernel, groups, half),
        grid=(2 * half,),
        in_specs=[full] * groups + [first] * groups + [second] * groups,
        out_specs=pl.BlockSpec((width, step), lambda j: (0, j)),
        out_shape=jax.ShapeDtypeStruct((width, 2 * units), BF),
        name="grad_gate_up",
        cost_estimate=pl.CostEstimate(
            flops=4 * groups * rows * width * units,
            transcendentals=0,
            bytes_accessed=2 * groups * rows * (2 * units + width) + 4 * width * units,
        ),
    )(*normeds, *d_gates, *d_ups)


def after(value, *others):
    return lax.optimization_barrier((value, *others))[0]


def body(
    tokens,
    attn_gain,
    w_query,
    w_key,
    w_value,
    w_out,
    ffn_gain,
    w_gate,
    w_up,
    w_down,
    doc_lengths,
    cotangent,
):
    rows, width = tokens.shape
    wide = lax.axis_size("wide")
    narrow = lax.axis_size("narrow")
    me_wide = lax.axis_index("wide")
    me = lax.axis_index("narrow")
    core = me_wide % 2
    kv_heads = w_key.shape[1] // HD
    half_rows = rows // HALVES
    piece = half_rows // narrow
    part = width // wide
    hops = wide // 4
    units = w_gate.shape[1]
    q_width = w_query.shape[1]
    k_width = w_key.shape[1]
    chip_groups = [list(range(0, wide, 2)), list(range(1, wide, 2))]
    ids = jnp.stack([me, core]).astype(jnp.int32)

    def other_core(value):
        return lax.ppermute(value, "wide", [(i, i ^ 1) for i in range(wide)])

    def chips_up(value, hop):
        return lax.ppermute(value, "wide", [(i, i + 2 * hop) for i in range(wide - 2 * hop)])

    def chips_down(value, hop):
        return lax.ppermute(value, "wide", [(i + 2 * hop, i) for i in range(wide - 2 * hop)])

    def swap(value, distance):
        return lax.ppermute(value, "narrow", [(i, i ^ distance) for i in range(narrow)])

    def half_piece(value, half, distance):
        return lax.dynamic_slice_in_dim(
            value, half * half_rows + (me ^ distance) * piece, piece, 0
        )

    def rows_of(value, distance):
        return jnp.concatenate([half_piece(value, h, distance) for h in range(HALVES)], axis=0)

    def exchange(pieces):
        return [pieces[0]] + [swap(pieces[d], d) for d in range(1, narrow)]

    def gather_near(value):
        return [value] + [swap(value, d) for d in range(1, narrow)]

    def split_pieces(value):
        size = value.shape[0] // narrow
        return [value[d * size : (d + 1) * size] for d in range(narrow)]

    def columns_of(value, which):
        return jnp.concatenate(
            [
                lax.dynamic_slice_in_dim(value, (2 * chip + which) * part, part, 1)
                for chip in range(wide // 2)
            ],
            axis=1,
        )

    def both_cores(value):
        return columns_of(value, core), other_core(columns_of(value, 1 - core))

    def scatter(value, dimension):
        return lax.psum_scatter(
            value,
            "wide",
            scatter_dimension=dimension,
            axis_index_groups=chip_groups,
            tiled=True,
        )

    gain_one = attn_gain.astype(F32)[None, :]
    gain_two = ffn_gain.astype(F32)[None, :]

    base = me_wide * rows
    index = base + jnp.arange(rows, dtype=jnp.int32)
    start, valid = doc_offsets(doc_lengths, index)
    angle = jnp.asarray(inverse_frequencies(HD))[:, None] * (index - start).astype(F32)[None, :]
    cosine = jnp.cos(angle)
    sine = jnp.sin(angle)
    first_key = jnp.where(valid, start, index)
    key_tiles = []
    for hop in range(hops + 1):
        for side in range(2):
            block = ((me_wide // 2 - hop) * 2 + (core ^ side)) * rows
            key_tiles += [block + tile * KT for tile in range(rows // KT)]
    info = jnp.concatenate(
        [
            jnp.stack(key_tiles).astype(jnp.int32),
            base[None].astype(jnp.int32),
            first_key[::half_rows],
        ]
    )
    start_row = first_key[None, :]
    valid_row = valid.astype(jnp.int32)[None, :]

    inputs = tokens.astype(F32)
    normed = (inputs * rms_scale(inputs) * gain_one).astype(BF)
    keys_t = rotate_t(dims(w_key, normed, 0, 1), cosine, sine).astype(BF)
    values_t = dims(w_value, normed, 0, 1).astype(BF)
    packed = jnp.concatenate([keys_t, values_t], axis=0)
    blocks = [packed, other_core(packed)]
    for hop in range(1, hops + 1):
        near = chips_up(packed, hop)
        blocks += [near, other_core(near)]
    query_t = rotate_t(dims(w_query, normed, 0, 1), cosine, sine).astype(BF)

    cot_near, cot_own, cot_send = near_order(ids, narrow, cotangent, part)
    cot_other = other_core(cot_send)
    query_t, start_row, valid_row, info, cot_own = lax.optimization_barrier(
        (query_t, start_row, valid_row, info, cot_own)
    )

    outs, mixes, lses, hiddens, normed_two = [], [], [], [], []

    def out_pieces(mixed):
        attn_part = dims(mixed, w_out, 0, 0).astype(BF)
        return [
            lax.dynamic_slice_in_dim(attn_part, (me ^ d) * piece, piece, 0) for d in range(narrow)
        ]

    def norm_two(half, pieces):
        return rows_call(
            norm_two_kernel,
            [
                jax.ShapeDtypeStruct((piece, width), F32),
                jax.ShapeDtypeStruct((piece, width), BF),
            ],
            "norm_two",
            ids,
            narrow,
            tokens,
            [half],
            gain_two,
            *pieces,
        )

    received = None
    for half in range(HALVES):
        out, mixed, lse = attend(half, info, start_row, valid_row, query_t, blocks, kv_heads)
        if received is not None:
            received, mixed = lax.optimization_barrier((received, mixed))
            hidden, low = norm_two(half - 1, received)
            hiddens.append(hidden)
            normed_two.append(gather_near(low))
            mixed, low = lax.optimization_barrier((mixed, low))
        outs.append(out)
        mixes.append(mixed)
        lses.append(lse)
        pieces = out_pieces(mixed)
        query_t, cot_near, pieces = lax.optimization_barrier((query_t, cot_near, pieces))
        received = exchange(pieces)
    d_act = dims(cot_near, w_down, 1, 1)
    received, d_act = lax.optimization_barrier((received, d_act))
    hidden, low = norm_two(HALVES - 1, received)
    hiddens.append(hidden)
    d_act, low = lax.optimization_barrier((d_act, low))
    normed_two.append(gather_near(low))

    acts, d_gates, d_ups, n_owns, n_sends = [], [], [], [], []
    for half in range(HALVES):
        act, d_gate, d_up, own, send = ffn_forward(
            half, ids, normed_two[half], d_act, w_gate, w_up, part
        )
        acts.append(act)
        d_gates.append(d_gate)
        d_ups.append(d_up)
        n_owns.append(own)
        n_sends.append(send)
    cots = [c[h * half_rows : (h + 1) * half_rows] for c in (cot_own, cot_other) for h in range(HALVES)]
    acts_all = acts + [other_core(a) for a in acts]
    d_gates_all = d_gates + [other_core(a) for a in d_gates]
    d_ups_all = d_ups + [other_core(a) for a in d_ups]
    n_all = n_owns + [other_core(a) for a in n_sends]

    normed_own, normed_send = split_columns(ids, normed, part)
    acts_all, normed_own, d_gates = lax.optimization_barrier((acts_all, normed_own, d_gates))
    grad_down = grad_down_of(acts_all, cots)
    d_gates_then, _ = lax.optimization_barrier((d_gates, grad_down))
    d_norm_part = pair_nt(narrow, d_gates_then, d_ups, w_gate, w_up)
    n_all, d_norm_part = lax.optimization_barrier((n_all, d_norm_part))
    d_norm_pieces = exchange(split_pieces(d_norm_part))
    grad_gate_up = grad_in_of(n_all, d_gates_all, d_ups_all)
    d_norm_pieces, _ = lax.optimization_barrier((d_norm_pieces, grad_gate_up))
    grad_down = scatter(grad_down, 1)

    shard = HALVES * piece
    d_hidden, d_hidden_b, gain_two_part = rows_call(
        norm_two_back_kernel,
        [
            jax.ShapeDtypeStruct((shard, width), F32),
            jax.ShapeDtypeStruct((shard, width), BF),
            jax.ShapeDtypeStruct((1, width), F32),
        ],
        "norm_two_back",
        ids,
        narrow,
        cotangent,
        range(HALVES),
        *hiddens,
        gain_two,
        *d_norm_pieces,
    )
    d_hidden_pieces = gather_near(d_hidden_b)
    ffn_part = down_of(narrow, acts, w_down)
    d_hidden_pieces, ffn_part = lax.optimization_barrier((d_hidden_pieces, ffn_part))
    grad_gate_up = scatter(grad_gate_up, 0)
    ffn_pieces = exchange(split_pieces(ffn_part))

    d_mixed_t, dh_own, dh_send = d_mixed_of(ids, valid_row, w_out, d_hidden_pieces, part)
    d_query_r, d_blocks = attend_back(
        info, start_row, query_t, d_mixed_t, outs, lses, blocks, kv_heads
    )
    d_blocks = d_blocks.reshape(2 * (hops + 1), 2 * k_width, rows)
    for_other = other_core(d_blocks[1::2])
    d_kv = d_blocks[0].astype(F32) + for_other[0].astype(F32)
    down = []
    for hop in range(1, hops + 1):
        both = (d_blocks[2 * hop].astype(F32) + for_other[hop].astype(F32)).astype(BF)
        down.append(chips_down(both, hop))
    d_query = rotate_t(d_query_r * (1.0 / math.sqrt(HD)), cosine, -sine).astype(BF)

    ffn_pieces, d_query = lax.optimization_barrier((ffn_pieces, d_query))
    ffn_sum = ffn_pieces[0].astype(F32)
    for other in ffn_pieces[1:]:
        ffn_sum = ffn_sum + other.astype(F32)
    output_pieces = gather_near((jnp.concatenate(hiddens, axis=0) + ffn_sum).astype(BF))
    normed_other = other_core(normed_send)
    dh_other = other_core(dh_send)
    mixed_others = [other_core(m) for m in mixes]
    d_query_other = other_core(d_query)
    grad_out = None
    for half in range(HALVES):
        cut = slice(half * half_rows, (half + 1) * half_rows)
        term = jnp.dot(mixes[half], dh_own[cut], preferred_element_type=F32) + jnp.dot(
            mixed_others[half], dh_other[cut], preferred_element_type=F32
        )
        grad_out = term if grad_out is None else grad_out + term
    grad_query = jnp.dot(d_query, normed_own, preferred_element_type=F32) + jnp.dot(
        d_query_other, normed_other, preferred_element_type=F32
    )
    grad_out, grad_query = grad_out.astype(BF), grad_query.astype(BF)

    down, grad_out, grad_query, grad_down = lax.optimization_barrier(
        (down, grad_out, grad_query, grad_down)
    )
    for value in down:
        d_kv = d_kv + value.astype(F32)
    d_keys = rotate_t(d_kv[:k_width], cosine, -sine).astype(BF)
    d_values = d_kv[k_width:].astype(BF)
    norm_one_part = (
        dims(d_query, w_query, 0, 1) + dims(d_keys, w_key, 0, 1) + dims(d_values, w_value, 0, 1)
    ).astype(BF)
    norm_one_pieces = exchange([rows_of(norm_one_part, d) for d in range(narrow)])
    d_pair = jnp.concatenate([d_keys, d_values], axis=0)
    d_pair_other = other_core(d_pair)
    grad_pair = jnp.dot(d_pair, normed_own, preferred_element_type=F32) + jnp.dot(
        d_pair_other, normed_other, preferred_element_type=F32
    )
    grad_pair = grad_pair.astype(BF)
    output = in_order(ids, output_pieces)

    input_mine, gain_one_part = rows_call(
        norm_one_back_kernel,
        [jax.ShapeDtypeStruct((shard, width), BF), jax.ShapeDtypeStruct((1, width), F32)],
        "norm_one_back",
        ids,
        narrow,
        tokens,
        range(HALVES),
        d_hidden,
        gain_one,
        *norm_one_pieces,
    )
    input_pieces = gather_near(input_mine)
    gains = jnp.concatenate([gain_one_part, gain_two_part], axis=0)
    gains = sum(gather_near(gains)[1:], gains)
    gains_own, gains_other = both_cores(gains)
    gain_rows = jnp.pad((gains_own + gains_other).astype(BF), ((0, 14), (0, 0)))
    grads = jnp.concatenate([grad_out, grad_query, grad_pair, gain_rows], axis=0)
    grads, grad_gate_up = lax.optimization_barrier((grads, grad_gate_up))
    grads = scatter(grads, 1)
    grad_gate = grad_gate_up[:, :units].astype(F32)
    grad_up = grad_gate_up[:, units:].astype(F32)
    grad_down = grad_down.astype(F32)
    grads, grad_gate, grad_up, grad_down = lax.optimization_barrier(
        (grads, grad_gate, grad_up, grad_down)
    )
    grads = grads.astype(F32)
    input_grad = in_order(ids, input_pieces)
    cuts = np.cumsum([0, w_out.shape[0], q_width, k_width, k_width])
    return (
        output,
        input_grad,
        grads[cuts[4]],
        grads[cuts[1] : cuts[2]].T,
        grads[cuts[2] : cuts[3]].T,
        grads[cuts[3] : cuts[4]].T,
        grads[: cuts[1]],
        grads[cuts[4] + 1],
        grad_gate,
        grad_up,
        grad_down,
    )


def solution(mesh):
    in_specs = (
        P("wide", None),
        P(),
        P(None, "narrow"),
        P(None, "narrow"),
        P(None, "narrow"),
        P("narrow", None),
        P(),
        P(None, "narrow"),
        P(None, "narrow"),
        P("narrow", None),
        P(),
        P("wide", None),
    )
    out_specs = (
        P("wide", None),
        P("wide", None),
        P("wide"),
        P("wide", "narrow"),
        P("wide", "narrow"),
        P("wide", "narrow"),
        P("narrow", "wide"),
        P("wide"),
        P("wide", "narrow"),
        P("wide", "narrow"),
        P("narrow", "wide"),
    )
    return jax.shard_map(body, mesh=mesh, in_specs=in_specs, out_specs=out_specs, check_vma=False)
```

```python
import functools
import math

import jax
import jax.numpy as jnp
import numpy as np
from jax import lax
from jax.experimental import pallas as pl
from jax.experimental.pallas import tpu as pltpu
from jax.sharding import PartitionSpec as P

HD = 64
DOCS = 12
NORM_EPS = 1e-05
MASKED_SCORE = -1e30
LOG2E = math.log2(math.e)
SCALE2 = LOG2E / math.sqrt(HD)
KT = 256
HALVES = 2
BF = jnp.bfloat16
F32 = jnp.float32


def inverse_frequencies(head_size):
    frequency = 1.0 / 500000.0 ** (np.arange(0, head_size, 2) / head_size)
    wavelength = 2 * math.pi / frequency
    smoothing = (8192.0 / wavelength - 1.0) / 3.0
    scaled_freq = np.where(wavelength > 8192.0, frequency / 32.0, frequency)
    middle_band = (wavelength <= 8192.0) & (wavelength >= 2048.0)
    scaled_freq = np.where(
        middle_band, (1 - smoothing) * frequency / 32.0 + smoothing * frequency, scaled_freq
    )
    return scaled_freq.astype(np.float32)


def doc_offsets(doc_lengths, index):
    ends = jnp.cumsum(doc_lengths)
    passed = (index[None, :] >= ends[:, None]).astype(jnp.int32)
    return jnp.sum(passed * doc_lengths[:, None], axis=0)


def rotate_t(values, cosine, sine):
    heads = values.shape[0] // HD
    shaped = values.reshape(heads, 2, HD // 2, values.shape[1])
    first = shaped[:, 0]
    second = shaped[:, 1]
    return jnp.stack(
        [first * cosine - second * sine, second * cosine + first * sine], axis=1
    ).reshape(values.shape)


def dims(left, right, a, b):
    return lax.dot_general(left, right, (((a,), (b,)), ((), ())), preferred_element_type=F32)


def vmem_spec():
    return pl.BlockSpec(memory_space=pltpu.VMEM)


def smem_spec():
    return pl.BlockSpec(memory_space=pltpu.SMEM)


def any_spec():
    return pl.BlockSpec(memory_space=pl.ANY)


def cost(flops, moved, exps=0):
    return pl.CostEstimate(flops=int(flops), transcendentals=int(exps), bytes_accessed=int(moved))


def rms_scale(values):
    return lax.rsqrt(jnp.mean(values * values, axis=-1, keepdims=True) + NORM_EPS)


def keys_values_kernel(x_ref, gain_ref, wk_ref, wv_ref, cos_ref, sin_ref, normed_ref, packed_ref):
    rows = x_ref.shape[0]
    step = min(128, rows)
    for at in range(0, rows, step):
        values = x_ref[at : at + step, :].astype(F32)
        normed_ref[at : at + step, :] = (values * rms_scale(values) * gain_ref[...]).astype(BF)
    normed = normed_ref[...]
    keys = jnp.dot(normed, wk_ref[...], preferred_element_type=F32).T
    width = keys.shape[0]
    half = HD // 2
    for head in range(width // HD):
        first = keys[head * HD : head * HD + half]
        second = keys[head * HD + half : (head + 1) * HD]
        cosine, sine = cos_ref[...], sin_ref[...]
        packed_ref[head * HD : head * HD + half, :] = (first * cosine - second * sine).astype(BF)
        packed_ref[head * HD + half : (head + 1) * HD, :] = (
            second * cosine + first * sine
        ).astype(BF)
    packed_ref[width:, :] = jnp.dot(normed, wv_ref[...], preferred_element_type=F32).T.astype(BF)


def keys_values(tokens, gain, w_key, w_value, cosine, sine):
    rows, width = tokens.shape
    kv = w_key.shape[1]
    return pl.pallas_call(
        keys_values_kernel,
        in_specs=[vmem_spec()] * 6,
        out_specs=[vmem_spec()] * 2,
        out_shape=[
            jax.ShapeDtypeStruct((rows, width), BF),
            jax.ShapeDtypeStruct((2 * kv, rows), BF),
        ],
        name="keys_values",
        cost_estimate=cost(4 * rows * width * kv, 4 * rows * width + 4 * width * kv),
    )(tokens, gain, w_key, w_value, cosine, sine)


def window(lengths_ref, index):
    end = lengths_ref[0]
    start = jnp.zeros_like(index)
    for doc in range(1, DOCS):
        start = jnp.where(index >= end, end, start)
        if doc == DOCS - 1:
            last = end
        end = end + lengths_ref[doc]
    valid = index < last
    return jnp.where(valid, start, index), valid


def tile_state(ids_ref, edges, tile, half, q_rows, rows):
    me_wide = ids_ref[2]
    slot = tile // (rows // KT)
    block = (me_wide // 2 - slot // 2) * 2 + (ids_ref[1] ^ (slot % 2))
    key_base = block * rows + (tile % (rows // KT)) * KT
    q_base = me_wide * rows + half * q_rows
    low, high = edges[half]
    active = (key_base <= q_base + q_rows - 1) & (key_base + KT > low)
    whole = (key_base + KT - 1 <= q_base) & (key_base >= high)
    return active, active & whole, key_base, q_base


def window_edges(ids_ref, lengths_ref, rows):
    base = ids_ref[2] * rows
    step = rows // HALVES
    return [
        (
            window(lengths_ref, base + half * step)[0],
            window(lengths_ref, base + (half + 1) * step - 1)[0],
        )
        for half in range(HALVES)
    ]


def query_row(ids_ref, rows, half):
    step = rows // HALVES
    return ids_ref[2] * rows + half * step + lax.broadcasted_iota(jnp.int32, (1, step), 1)


def tile_mask(key_base, q_base, start_row):
    q_rows = start_row.shape[1]
    keys = key_base + lax.broadcasted_iota(jnp.int32, (KT, q_rows), 0)
    queries = q_base + lax.broadcasted_iota(jnp.int32, (KT, q_rows), 1)
    return (keys <= queries) & (keys >= start_row)


def both_ways(active, whole, run):
    pl.when(whole)(lambda: run(False))
    pl.when(active & jnp.logical_not(whole))(lambda: run(True))


def attend_kernel(slots, group, half, ids_ref, lengths_ref, q_ref, *refs):
    k_refs = refs[:slots]
    v_refs = refs[slots : 2 * slots]
    o_ref, mixed_ref, lse_ref, keys_s, values_s, top_s, sum_s, acc_s = refs[2 * slots :]
    q_rows = q_ref.shape[1]
    rows = k_refs[0].shape[1]
    per = rows // KT
    tiles = slots * per
    edges = window_edges(ids_ref, lengths_ref, rows)
    start_row, valid_row = window(lengths_ref, query_row(ids_ref, rows, half))
    for slot in range(slots):
        for part in range(per):
            tile = slot * per + part
            cut = slice(part * KT, (part + 1) * KT)

            @pl.when(tile_state(ids_ref, edges, tile, half, q_rows, rows)[0])
            def _(tile=tile, slot=slot, cut=cut):
                keys_s[tile] = k_refs[slot][:, cut].T
                values_s[tile] = v_refs[slot][:, cut]

    top_s[...] = jnp.full_like(top_s, MASKED_SCORE)
    sum_s[...] = jnp.zeros_like(sum_s)
    acc_s[...] = jnp.zeros_like(acc_s)
    heads = range(group)

    def step(tile, carry):
        active, whole, key_base, q_base = tile_state(ids_ref, edges, tile, half, q_rows, rows)

        def run(masked):
            keys = keys_s[tile]
            values = values_s[tile]
            scores = [
                jnp.dot(keys, q_ref[h * HD : (h + 1) * HD, :], preferred_element_type=F32)
                for h in heads
            ]
            if masked:
                allowed = tile_mask(key_base, q_base, start_row)
                scores = [jnp.where(allowed, s, MASKED_SCORE) for s in scores]
            tops, decays = [], []
            for h in heads:
                old = top_s[h : h + 1, :]
                new = jnp.maximum(old, jnp.max(scores[h], axis=0, keepdims=True))
                top_s[h : h + 1, :] = new
                tops.append(new)
                decays.append(jnp.exp2((old - new) * SCALE2))
            for h in heads:
                weight = jnp.exp2((scores[h] - tops[h]) * SCALE2)
                sum_s[h : h + 1, :] = sum_s[h : h + 1, :] * decays[h] + jnp.sum(
                    weight, axis=0, keepdims=True
                )
                acc_s[h] = acc_s[h] * decays[h] + jnp.dot(
                    values, weight.astype(BF), preferred_element_type=F32
                )

        both_ways(active, whole, run)
        return carry

    lax.fori_loop(0, tiles, step, 0)
    for h in heads:
        h_cut = slice(h * HD, (h + 1) * HD)
        total = sum_s[h : h + 1, :]
        out = acc_s[h] / total
        o_ref[h_cut, :] = out
        mixed_ref[h_cut, :] = jnp.where(valid_row, out, 0.0).astype(BF)
        lse_ref[0, h : h + 1, :] = top_s[h : h + 1, :] * SCALE2 + jnp.log(total) * LOG2E


def attend(half, ids, lengths, q_t, blocks, kv_heads):
    slots = len(blocks)
    heads = q_t.shape[0] // HD
    group = heads // kv_heads
    rows = q_t.shape[1]
    q_rows = rows // HALVES
    tiles = slots * (rows // KT)
    out_spec = pl.BlockSpec((group * HD, q_rows), lambda g: (g, 0))
    return pl.pallas_call(
        functools.partial(attend_kernel, slots, group, half),
        grid=(kv_heads,),
        in_specs=[
            smem_spec(),
            smem_spec(),
            pl.BlockSpec((group * HD, q_rows), lambda g: (g, half)),
        ]
        + [pl.BlockSpec((HD, rows), lambda g: (g, 0))] * slots
        + [pl.BlockSpec((HD, rows), lambda g: (kv_heads + g, 0))] * slots,
        out_specs=[out_spec, out_spec, pl.BlockSpec((1, group, q_rows), lambda g: (g, 0, 0))],
        out_shape=[
            jax.ShapeDtypeStruct((heads * HD, q_rows), F32),
            jax.ShapeDtypeStruct((heads * HD, q_rows), BF),
            jax.ShapeDtypeStruct((kv_heads, group, q_rows), F32),
        ],
        scratch_shapes=[
            pltpu.VMEM((tiles, KT, HD), BF),
            pltpu.VMEM((tiles, HD, KT), BF),
            pltpu.VMEM((group, q_rows), F32),
            pltpu.VMEM((group, q_rows), F32),
            pltpu.VMEM((group, HD, q_rows), F32),
        ],
        name="attend",
        cost_estimate=cost(
            16 * heads * q_rows * rows * HD, 8 * rows * heads * HD, heads * q_rows * rows * 4
        ),
    )(ids, lengths, q_t, *blocks, *blocks)


def attend_back_kernel(slots, group, members, ids_ref, lengths_ref, q_ref, *refs):
    do_refs, refs = refs[:members], refs[members:]
    o_refs, lse_refs, refs = refs[:HALVES], refs[HALVES : 2 * HALVES], refs[2 * HALVES :]
    k_refs, v_refs, refs = refs[:slots], refs[slots : 2 * slots], refs[2 * slots :]
    dq_ref, dkv_ref = refs[:2]
    keys_s, values_s, keys_t_s, dk_s, dv_s, q_s, do_s, do_t_s, dq_s, delta_s = refs[2:]
    rows = q_ref.shape[1]
    q_rows = rows // HALVES
    per = rows // KT
    tiles = slots * per
    heads = range(group)
    edges = window_edges(ids_ref, lengths_ref, rows)

    def any_active(tile):
        found = tile_state(ids_ref, edges, tile, 0, q_rows, rows)[0]
        for half in range(1, HALVES):
            found = found | tile_state(ids_ref, edges, tile, half, q_rows, rows)[0]
        return found

    for slot in range(slots):
        for part in range(per):
            tile = slot * per + part
            cut = slice(part * KT, (part + 1) * KT)

            @pl.when(any_active(tile))
            def _(tile=tile, slot=slot, cut=cut):
                keys_s[tile] = k_refs[slot][:, cut].T
                keys_t_s[tile] = k_refs[slot][:, cut]
                values_s[tile] = v_refs[slot][:, cut].T
                dk_s[tile] = jnp.zeros((KT, HD), F32)
                dv_s[tile] = jnp.zeros((KT, HD), F32)

    shard = do_refs[0].shape[0]
    for distance in range(members):
        at = pl.multiple_of((ids_ref[0] ^ distance) * shard, shard)
        do_s[pl.ds(at, shard), :] = do_refs[distance][...]
    do_t_s[...] = do_s[...].T

    for half in range(HALVES):
        q_cut = slice(half * q_rows, (half + 1) * q_rows)
        for h in heads:
            h_cut = slice(h * HD, (h + 1) * HD)
            q_s[h] = q_ref[h_cut, q_cut].T
            delta_s[h : h + 1, :] = jnp.sum(
                do_t_s[h_cut, q_cut].astype(F32) * o_refs[half][h_cut, :], axis=0, keepdims=True
            )
        dq_s[...] = jnp.zeros_like(dq_s)
        start_row = window(lengths_ref, query_row(ids_ref, rows, half))[0]

        def step(tile, carry, half=half, q_cut=q_cut, start_row=start_row):
            active, whole, key_base, q_base = tile_state(ids_ref, edges, tile, half, q_rows, rows)

            def run(masked):
                keys = keys_s[tile]
                values = values_s[tile]
                keys_t = keys_t_s[tile]
                scores = [
                    jnp.dot(keys, q_ref[h * HD : (h + 1) * HD, q_cut], preferred_element_type=F32)
                    for h in heads
                ]
                prob_grads = [
                    jnp.dot(values, do_t_s[h * HD : (h + 1) * HD, q_cut], preferred_element_type=F32)
                    for h in heads
                ]
                if masked:
                    allowed = tile_mask(key_base, q_base, start_row)
                probs, d_scores = [], []
                for h in heads:
                    scaled = scores[h] * SCALE2 - lse_refs[half][0, h : h + 1, :]
                    if masked:
                        scaled = jnp.where(allowed, scaled, MASKED_SCORE)
                    prob = jnp.exp2(scaled)
                    probs.append(prob.astype(BF))
                    d_scores.append((prob * (prob_grads[h] - delta_s[h : h + 1, :])).astype(BF))
                dk = dk_s[tile]
                dv = dv_s[tile]
                for h in heads:
                    dv = dv + jnp.dot(
                        probs[h],
                        do_s[q_cut, h * HD : (h + 1) * HD],
                        preferred_element_type=F32,
                    )
                    dk = dk + jnp.dot(d_scores[h], q_s[h], preferred_element_type=F32)
                    dq_s[h] += jnp.dot(keys_t, d_scores[h], preferred_element_type=F32)
                dk_s[tile] = dk
                dv_s[tile] = dv

            both_ways(active, whole, run)
            return carry

        lax.fori_loop(0, tiles, step, 0)
        for h in heads:
            dq_ref[h * HD : (h + 1) * HD, q_cut] = dq_s[h]
    for slot in range(slots):
        for part in range(per):
            cut = slice(part * KT, (part + 1) * KT)
            tile = slot * per + part
            active = any_active(tile)

            @pl.when(active)
            def _(tile=tile, slot=slot, cut=cut):
                dkv_ref[slot, 0, :, cut] = (dk_s[tile].T * (1.0 / math.sqrt(HD))).astype(BF)
                dkv_ref[slot, 1, :, cut] = dv_s[tile].T.astype(BF)

            @pl.when(jnp.logical_not(active))
            def _(slot=slot, cut=cut):
                dkv_ref[slot, 0, :, cut] = jnp.zeros((HD, KT), BF)
                dkv_ref[slot, 1, :, cut] = jnp.zeros((HD, KT), BF)


def attend_back(ids, lengths, q_t, do_pieces, outs, lses, blocks, kv_heads):
    slots = len(blocks)
    heads = q_t.shape[0] // HD
    group = heads // kv_heads
    rows = q_t.shape[1]
    q_rows = rows // HALVES
    tiles = slots * (rows // KT)
    members = len(do_pieces)
    wide = group * HD
    q_spec = pl.BlockSpec((wide, rows), lambda g: (g, 0))
    return pl.pallas_call(
        functools.partial(attend_back_kernel, slots, group, members),
        grid=(kv_heads,),
        in_specs=[smem_spec(), smem_spec(), q_spec]
        + [pl.BlockSpec((rows // members, wide), lambda g: (0, g))] * members
        + [pl.BlockSpec((wide, q_rows), lambda g: (g, 0))] * HALVES
        + [pl.BlockSpec((1, group, q_rows), lambda g: (g, 0, 0))] * HALVES
        + [pl.BlockSpec((HD, rows), lambda g: (g, 0))] * slots
        + [pl.BlockSpec((HD, rows), lambda g: (kv_heads + g, 0))] * slots,
        out_specs=[q_spec, pl.BlockSpec((slots, 2, HD, rows), lambda g: (0, 0, g, 0))],
        out_shape=[
            jax.ShapeDtypeStruct(q_t.shape, F32),
            jax.ShapeDtypeStruct((slots, 2, kv_heads * HD, rows), BF),
        ],
        scratch_shapes=[
            pltpu.VMEM((tiles, KT, HD), BF),
            pltpu.VMEM((tiles, KT, HD), BF),
            pltpu.VMEM((tiles, HD, KT), BF),
            pltpu.VMEM((tiles, KT, HD), F32),
            pltpu.VMEM((tiles, KT, HD), F32),
            pltpu.VMEM((group, q_rows, HD), BF),
            pltpu.VMEM((rows, wide), BF),
            pltpu.VMEM((wide, rows), BF),
            pltpu.VMEM((group, HD, q_rows), F32),
            pltpu.VMEM((group, q_rows), F32),
        ],
        name="attend_back",
        cost_estimate=cost(
            40 * heads * rows * rows * HD, 16 * rows * heads * HD, heads * rows * rows * 4
        ),
    )(ids, lengths, q_t, *do_pieces, *outs, *lses, *blocks, *blocks)


def fetch_weights(members, ids_ref, weights, held, sems):
    size = held.shape[0] // (2 * members)
    copies = []
    for distance in range(members):
        for other in range(2):
            index = 2 * distance + other
            source = pl.multiple_of((ids_ref[0] ^ distance) * size, size)
            copy = pltpu.make_async_copy(
                weights[other].at[pl.ds(source, size), :],
                held.at[index * size : (index + 1) * size, :],
                sems.at[index],
            )
            copy.start()
            first = pl.multiple_of((ids_ref[1] ^ other) * size, size)
            copies.append((copy, distance, index * size, first))
    return copies, size


def attn_out_kernel(members, ids_ref, x_ref, gain_ref, *refs):
    mixes, weights = refs[:members], refs[members : members + 2]
    hidden_ref, normed_ref, held, sems = refs[-4:]
    copies, size = fetch_weights(members, ids_ref, weights, held, sems)
    hidden_ref[...] = x_ref[...].astype(F32)
    for copy, distance, at, first in copies:
        copy.wait()
        hidden_ref[...] += dims(
            mixes[distance][pl.ds(first, size), :], held[at : at + size, :], 0, 0
        )
    rows = hidden_ref.shape[0]
    step = min(64, rows)
    for at in range(0, rows, step):
        hidden = hidden_ref[at : at + step, :]
        normed_ref[at : at + step, :] = (hidden * rms_scale(hidden) * gain_ref[...]).astype(BF)


def attn_out(half, ids, tokens, gain, mixes, weights, filled):
    rows, width = tokens.shape
    half_rows = rows // HALVES
    inner = sum(w.shape[0] for w in weights)
    out_spec = pl.BlockSpec((half_rows, width), lambda i: (half, 0))
    operands = [ids, tokens, gain, *mixes, *weights]
    extra = [] if filled is None else list(filled)
    return pl.pallas_call(
        functools.partial(attn_out_kernel, len(mixes)),
        grid=(1,),
        in_specs=[smem_spec(), out_spec, vmem_spec()]
        + [vmem_spec()] * len(mixes)
        + [any_spec()] * (len(weights) + len(extra)),
        out_specs=[out_spec, out_spec],
        out_shape=[
            jax.ShapeDtypeStruct((rows, width), F32),
            jax.ShapeDtypeStruct((rows, width), BF),
        ],
        scratch_shapes=[
            pltpu.VMEM((inner, width), BF),
            pltpu.SemaphoreType.DMA((2 * len(mixes),)),
        ],
        input_output_aliases={len(operands) + i: i for i in range(len(extra))},
        name="attn_out",
        cost_estimate=cost(
            2 * half_rows * inner * width, 2 * inner * width + 12 * half_rows * width
        ),
    )(*operands, *extra)


def row_sum(refs):
    total = refs[0][...].astype(F32)
    for ref in refs[1:]:
        total = total + ref[...].astype(F32)
    return total


def norm_back(grad_normed, gain, values, inverse):
    scaled = grad_normed * gain
    return inverse * scaled - values * inverse**3 * jnp.mean(
        scaled * values, axis=-1, keepdims=True
    )


def norm_two_back_kernel(members, ids_ref, lengths_ref, hidden_ref, cot_ref, gain_ref, *refs):
    pieces, refs = refs[:members], refs[members:]
    weights, refs = refs[:2], refs[2:]
    refs = refs[members - 1 :]
    sum_ref, low_ref, part_ref = refs[:3]
    d_mixed, refs = refs[3 : 3 + members], refs[3 + members :]
    sent, (held, sems) = refs[:-2], refs[-2:]
    copies, size = fetch_weights(members, ids_ref, weights, held, sems)
    grad = row_sum(pieces)
    hidden = hidden_ref[...]
    inverse = rms_scale(hidden)
    part_ref[...] = jnp.sum(grad * hidden * inverse, axis=0, keepdims=True)
    total = cot_ref[...].astype(F32) + norm_back(grad, gain_ref[...], hidden, inverse)
    sum_ref[...] = total
    low = total.astype(BF)
    low_ref[...] = low
    for ref in sent:
        ref[...] = low
    shard = hidden.shape[0]
    begin = (ids_ref[2] * members + ids_ref[0]) * shard
    keep = window(lengths_ref, begin + lax.broadcasted_iota(jnp.int32, (shard, 1), 0))[1]
    for copy, distance, at, first in copies:
        copy.wait()
        out = jnp.where(keep, dims(low, held[at : at + size, :], 1, 1), 0.0)
        d_mixed[distance][:, pl.ds(first, size)] = out.astype(BF)


def norm_two_back(ids, lengths, hidden, cotangent, gain, pieces, weights, travel):
    members = len(pieces)
    shard, width = pieces[0].shape
    inner = sum(w.shape[0] for w in weights)
    mine = pl.BlockSpec((shard, width), lambda i, ids, lengths: (ids[0], 0))
    whole = pl.BlockSpec((shard, width), lambda i, ids, lengths: (0, 0))
    line = pl.BlockSpec((1, width), lambda i, ids, lengths: (0, 0))
    head_spec = pl.BlockSpec((shard, inner // members), lambda i, ids, lengths: (0, 0))
    return pl.pallas_call(
        functools.partial(norm_two_back_kernel, members),
        grid_spec=pltpu.PrefetchScalarGridSpec(
            num_scalar_prefetch=2,
            grid=(1,),
            in_specs=[mine, mine, line]
            + [whole] * members
            + [any_spec()] * (len(weights) + len(travel)),
            out_specs=[whole, whole, line] + [head_spec] * members + [whole] * len(travel),
            scratch_shapes=[
                pltpu.VMEM((inner, width), BF),
                pltpu.SemaphoreType.DMA((2 * members,)),
            ],
        ),
        out_shape=[
            jax.ShapeDtypeStruct((shard, width), F32),
            jax.ShapeDtypeStruct((shard, width), BF),
            jax.ShapeDtypeStruct((1, width), F32),
        ]
        + [jax.ShapeDtypeStruct((shard, inner // members), BF)] * members
        + [jax.ShapeDtypeStruct(t.shape, BF) for t in travel],
        input_output_aliases={
            5 + members + len(weights) + i: 3 + members + i for i in range(len(travel))
        },
        name="norm_two_back",
        cost_estimate=cost(2 * shard * inner * width, 2 * inner * width + 24 * shard * width),
    )(ids, lengths, hidden, cotangent, gain, *pieces, *weights, *travel)


def last_rows_kernel(members, ids_ref, x_ref, hidden_ref, add_ref, gain_ref, *refs):
    pieces, ffn, (low_ref, part_ref) = refs[:members], refs[members:-2], refs[-2:]
    grad = row_sum(pieces)
    values = x_ref[...].astype(F32)
    shard = values.shape[0]
    inverse = rms_scale(values)
    part_ref[...] = jnp.sum(grad * values * inverse, axis=0, keepdims=True)
    low_ref[:shard, :] = (
        add_ref[...] + norm_back(grad, gain_ref[...], values, inverse)
    ).astype(BF)
    low_ref[shard:, :] = (hidden_ref[...] + row_sum(ffn)).astype(BF)


def last_rows(ids, tokens, hidden, add, gain, pieces, ffn_pieces):
    shard, width = pieces[0].shape
    mine = pl.BlockSpec((shard, width), lambda i, ids: (ids[0], 0))
    first = pl.BlockSpec((shard, width), lambda i, ids: (0, 0))
    second = pl.BlockSpec((shard, width), lambda i, ids: (1, 0))
    line = pl.BlockSpec((1, width), lambda i, ids: (0, 0))
    both = pl.BlockSpec((2 * shard, width), lambda i, ids: (0, 0))
    return pl.pallas_call(
        functools.partial(last_rows_kernel, len(pieces)),
        grid_spec=pltpu.PrefetchScalarGridSpec(
            num_scalar_prefetch=1,
            grid=(1,),
            in_specs=[mine, mine, first, line]
            + [first] * (len(pieces) + 1)
            + [second] * (len(ffn_pieces) - 1),
            out_specs=[both, line],
        ),
        out_shape=[
            jax.ShapeDtypeStruct((2 * shard, width), BF),
            jax.ShapeDtypeStruct((1, width), F32),
        ],
        name="last_rows",
        cost_estimate=cost(30 * shard * width, 32 * shard * width),
    )(ids, tokens, hidden, add, gain, *pieces, *ffn_pieces)


def in_order_kernel(shard, outs, ids_ref, *refs):
    pieces, out_refs = refs[:-outs], refs[-outs:]
    for distance, ref in enumerate(pieces):
        at = pl.multiple_of((ids_ref[0] ^ distance) * shard, shard)
        for index, out_ref in enumerate(out_refs):
            out_ref[pl.ds(at, shard), :] = ref[index * shard : (index + 1) * shard, :]


def in_order(ids, pieces, outs):
    width = pieces[0].shape[1]
    shard = pieces[0].shape[0] // outs if outs > 1 else pieces[0].shape[0]
    rows = shard * len(pieces)
    return pl.pallas_call(
        functools.partial(in_order_kernel, shard, outs),
        in_specs=[smem_spec()] + [vmem_spec()] * len(pieces),
        out_specs=[vmem_spec()] * outs,
        out_shape=[jax.ShapeDtypeStruct((rows, width), pieces[0].dtype)] * outs,
        name="token_order",
        cost_estimate=cost(0, 4 * rows * outs * width),
    )(ids, *pieces)


def ffn_kernel(n_ref, da_ref, wg_ref, wu_ref, act_ref, dg_ref, du_ref):
    normed = n_ref[...]
    gate = jnp.dot(normed, wg_ref[...], preferred_element_type=F32)
    up = jnp.dot(normed, wu_ref[...], preferred_element_type=F32)
    sig = jax.nn.sigmoid(gate)
    silu = gate * sig
    act_ref[...] = (silu * up).astype(BF)
    d_act = da_ref[...]
    dg_ref[...] = (d_act * up * sig * (1.0 + gate * (1.0 - sig))).astype(BF)
    du_ref[...] = (d_act * silu).astype(BF)


def ffn_forward(normed, d_act, w_gate, w_up):
    rows, width = normed.shape
    units = w_gate.shape[1]
    step = min(512, units)
    tile = pl.BlockSpec((rows, step), lambda j: (0, j))
    weight = pl.BlockSpec((width, step), lambda j: (0, j))
    return pl.pallas_call(
        ffn_kernel,
        grid=(units // step,),
        in_specs=[pl.BlockSpec((rows, width), lambda j: (0, 0)), tile, weight, weight],
        out_specs=[tile, tile, tile],
        out_shape=[jax.ShapeDtypeStruct((rows, units), BF)] * 3,
        name="gate_up",
        cost_estimate=cost(
            4 * rows * width * units,
            4 * width * units + 2 * rows * width + 10 * rows * units,
            rows * units,
        ),
    )(normed, d_act, w_gate, w_up)


def store_by_distance(ids_ref, out_refs, held, value):
    shard = value.shape[0] // len(out_refs)
    held[...] = value.astype(BF)
    for distance, out_ref in enumerate(out_refs):
        at = pl.multiple_of((ids_ref[0] ^ distance) * shard, shard)
        out_ref[...] = held[pl.ds(at, shard), :]


def pair_nt_kernel(ids_ref, a_ref, b_ref, wa_ref, wb_ref, *refs):
    value = dims(a_ref[...], wa_ref[...], 1, 1) + dims(b_ref[...], wb_ref[...], 1, 1)
    store_by_distance(ids_ref, refs[:-1], refs[-1], value)


def pair_nt(members, ids, a, b, w_a, w_b):
    rows, units = a.shape
    width = w_a.shape[0]
    step = min(512, width)
    full = pl.BlockSpec((rows, units), lambda j: (0, 0))
    weight = pl.BlockSpec((step, units), lambda j: (j, 0))
    return pl.pallas_call(
        pair_nt_kernel,
        grid=(width // step,),
        in_specs=[smem_spec(), full, full, weight, weight],
        out_specs=[pl.BlockSpec((rows // members, step), lambda j: (0, j))] * members,
        out_shape=[jax.ShapeDtypeStruct((rows // members, width), BF)] * members,
        scratch_shapes=[pltpu.VMEM((rows, step), BF)],
        name="d_normed_two",
        cost_estimate=cost(
            4 * rows * width * units, 4 * width * units + 4 * rows * units + 2 * rows * width
        ),
    )(ids, a, b, w_a, w_b)


def down_kernel(ids_ref, a_ref, w_ref, *refs):
    value = jnp.dot(a_ref[...], w_ref[...], preferred_element_type=F32)
    store_by_distance(ids_ref, refs[:-1], refs[-1], value)


def down_of(members, ids, act, w_down):
    rows, units = act.shape
    shard = rows // members
    width = w_down.shape[1]
    step = min(512, width)
    return pl.pallas_call(
        down_kernel,
        grid=(width // step,),
        in_specs=[
            smem_spec(),
            pl.BlockSpec((rows, units), lambda j: (0, 0)),
            pl.BlockSpec((units, step), lambda j: (0, j)),
        ],
        out_specs=[pl.BlockSpec((shard, step), lambda j: (0, j))]
        + [pl.BlockSpec((shard, step), lambda j: (1, j))] * (members - 1),
        out_shape=[jax.ShapeDtypeStruct((shard, width), BF)]
        + [jax.ShapeDtypeStruct((2 * shard, width), BF)] * (members - 1),
        scratch_shapes=[pltpu.VMEM((rows, step), BF)],
        name="ffn_down",
        cost_estimate=cost(
            2 * rows * width * units, 2 * width * units + 2 * rows * units + 2 * rows * width
        ),
    )(ids, act, w_down)


def column_specs(rows, part, count):
    return [
        pl.BlockSpec((rows, part), lambda j, ids, k=k: (0, 2 * k + ids[1])) for k in range(count)
    ]


def fill_columns(held, refs):
    count = len(refs) // 2
    rows, part = refs[0].shape
    for index, ref in enumerate(refs):
        top = (index // count) * rows
        left = (index % count) * part
        held[top : top + rows, left : left + part] = ref[...]


def grad_down_kernel(blocks, ids_ref, own_ref, other_ref, *refs):
    cots, (o_ref, held) = refs[: 2 * blocks], refs[2 * blocks :]

    @pl.when(pl.program_id(0) == 0)
    def _():
        fill_columns(held, cots)

    rows = own_ref.shape[0]
    o_ref[...] = (
        dims(own_ref[...], held[:rows, :], 0, 0) + dims(other_ref[...], held[rows:, :], 0, 0)
    ).astype(BF)


def grad_down_of(ids, act, act_other, cot, cot_other, part):
    rows, units = act.shape
    width = cot.shape[1]
    blocks = width // (2 * part)
    step = min(512, units)
    tile = pl.BlockSpec((rows, step), lambda j, ids: (0, j))
    columns = column_specs(rows, part, blocks)
    return pl.pallas_call(
        functools.partial(grad_down_kernel, blocks),
        grid_spec=pltpu.PrefetchScalarGridSpec(
            num_scalar_prefetch=1,
            grid=(units // step,),
            in_specs=[tile, tile] + columns + columns,
            out_specs=pl.BlockSpec((step, width // 2), lambda j, ids: (j, 0)),
            scratch_shapes=[pltpu.VMEM((2 * rows, width // 2), BF)],
        ),
        out_shape=jax.ShapeDtypeStruct((units, width // 2), BF),
        name="grad_down",
        cost_estimate=cost(
            2 * rows * width * units, 4 * rows * units + 2 * rows * width + width * units
        ),
    )(ids, act, act_other, *([cot] * blocks), *([cot_other] * blocks))


def grad_in_kernel(blocks, half, ids_ref, *refs):
    normeds, refs = refs[: 2 * blocks], refs[2 * blocks :]
    gates, ups, (o_ref, held) = refs[:2], refs[2:4], refs[4:]

    @pl.when(pl.program_id(0) == 0)
    def _():
        fill_columns(held, normeds)

    rows = gates[0].shape[0]

    def of(pair):
        o_ref[...] = (
            dims(held[:rows, :], pair[0][...], 0, 0) + dims(held[rows:, :], pair[1][...], 0, 0)
        ).astype(BF)

    pl.when(pl.program_id(0) < half)(lambda: of(gates))
    pl.when(pl.program_id(0) >= half)(lambda: of(ups))


def grad_in_of(ids, normed, normed_other, d_gates, d_ups, part):
    rows, width = normed.shape
    units = d_gates[0].shape[1]
    blocks = width // (2 * part)
    step = min(512, units)
    half = units // step
    columns = column_specs(rows, part, blocks)
    first = pl.BlockSpec((rows, step), lambda j, ids: (0, jnp.minimum(j, half - 1)))
    second = pl.BlockSpec((rows, step), lambda j, ids: (0, jnp.maximum(j - half, 0)))
    return pl.pallas_call(
        functools.partial(grad_in_kernel, blocks, half),
        grid_spec=pltpu.PrefetchScalarGridSpec(
            num_scalar_prefetch=1,
            grid=(2 * half,),
            in_specs=columns + columns + [first] * 2 + [second] * 2,
            out_specs=pl.BlockSpec((width // 2, step), lambda j, ids: (0, j)),
            scratch_shapes=[pltpu.VMEM((2 * rows, width // 2), BF)],
        ),
        out_shape=jax.ShapeDtypeStruct((width // 2, 2 * units), BF),
        name="grad_gate_up",
        cost_estimate=cost(
            4 * rows * width * units, 8 * rows * units + 2 * rows * width + 2 * width * units
        ),
    )(ids, *([normed] * blocks), *([normed_other] * blocks), *d_gates, *d_ups)


def grad_proj_kernel(lefts, ids_ref, *refs):
    own, other = refs[:lefts], refs[lefts : 2 * lefts]
    right_ref, right_other_ref, o_ref = refs[2 * lefts :]
    at = 0
    rows = right_ref.shape[0]
    part = rows // lefts
    total = 0.0
    for group, right in ((own, right_ref), (other, right_other_ref)):
        for index, left in enumerate(group):
            total = total + jnp.dot(
                left[...],
                right[index * part : (index + 1) * part, :],
                preferred_element_type=F32,
            )
    o_ref[...] = total.astype(BF)


def grad_proj_of(ids, lefts, lefts_other, right, right_other, part, name):
    inner = lefts[0].shape[0]
    rows, width = right.shape
    blocks = width // (2 * part)
    left_spec = pl.BlockSpec(lefts[0].shape, lambda k, ids: (0, 0))
    right_spec = pl.BlockSpec((rows, part), lambda k, ids: (0, 2 * k + ids[1]))
    return pl.pallas_call(
        functools.partial(grad_proj_kernel, len(lefts)),
        grid_spec=pltpu.PrefetchScalarGridSpec(
            num_scalar_prefetch=1,
            grid=(blocks,),
            in_specs=[left_spec] * (2 * len(lefts)) + [right_spec] * 2,
            out_specs=pl.BlockSpec((inner, part), lambda k, ids: (0, k)),
        ),
        out_shape=jax.ShapeDtypeStruct((inner, width // 2), BF),
        name=name,
        cost_estimate=cost(
            2 * rows * width * inner, 4 * inner * rows + 2 * rows * width + inner * width
        ),
    )(ids, *lefts, *lefts_other, right, right_other)


def finish_kernel(in_ref, out_ref, *refs):
    at = out_ref.shape[0]
    out_ref[...] = in_ref[:at, :].astype(F32)
    for ref in refs:
        count = ref.shape[1]
        ref[...] = in_ref[at : at + count, :].astype(F32).T
        at += count


def finish(grads, sizes):
    part = grads.shape[1]
    return pl.pallas_call(
        finish_kernel,
        in_specs=[vmem_spec()],
        out_specs=[vmem_spec()] * len(sizes),
        out_shape=[jax.ShapeDtypeStruct((sizes[0], part), F32)]
        + [jax.ShapeDtypeStruct((part, size), F32) for size in sizes[1:]],
        name="finish",
        cost_estimate=cost(0, 6 * sum(sizes) * part),
    )(grads)


def together(*values):
    return lax.optimization_barrier(values)


def body(
    tokens,
    attn_gain,
    w_query,
    w_key,
    w_value,
    w_out,
    ffn_gain,
    w_gate,
    w_up,
    w_down,
    doc_lengths,
    cotangent,
):
    rows, width = tokens.shape
    wide = lax.axis_size("wide")
    narrow = lax.axis_size("narrow")
    me_wide = lax.axis_index("wide")
    me = lax.axis_index("narrow")
    core = me_wide % 2
    kv_heads = w_key.shape[1] // HD
    half_rows = rows // HALVES
    shard = rows // narrow
    part = width // wide
    hops = wide // 4
    units = w_gate.shape[1]
    q_width = w_query.shape[1]
    k_width = w_key.shape[1]
    chip_groups = [list(range(0, wide, 2)), list(range(1, wide, 2))]
    ids = jnp.stack([me, core, me_wide]).astype(jnp.int32)

    def other_core(value):
        return lax.ppermute(value, "wide", [(i, i ^ 1) for i in range(wide)])

    def chips_up(value, hop):
        return lax.ppermute(value, "wide", [(i, i + 2 * hop) for i in range(wide - 2 * hop)])

    def chips_down(value, hop):
        return lax.ppermute(value, "wide", [(i + 2 * hop, i) for i in range(wide - 2 * hop)])

    def swap(value, distance):
        return lax.ppermute(value, "narrow", [(i, i ^ distance) for i in range(narrow)])

    def rows_of(value, distance):
        return lax.dynamic_slice_in_dim(value, (me ^ distance) * shard, shard, 0)

    def exchange(pieces):
        return [pieces[0]] + [swap(pieces[d], d) for d in range(1, narrow)]

    def gather_near(value):
        return [value] + [swap(value, d) for d in range(1, narrow)]

    def scatter(value, dimension):
        return lax.psum_scatter(
            value,
            "wide",
            scatter_dimension=dimension,
            axis_index_groups=chip_groups,
            tiled=True,
        )

    gain_one = attn_gain.astype(F32)[None, :]
    gain_two = ffn_gain.astype(F32)[None, :]

    w_half = w_out.shape[0] // 2
    w_mine = lax.dynamic_slice_in_dim(w_out, core * w_half, w_half, 0)
    w_all = lax.all_gather(w_mine, "narrow", axis=0, tiled=True)

    base = me_wide * rows
    index = base + jnp.arange(rows, dtype=jnp.int32)
    start = doc_offsets(doc_lengths, index)
    angle = jnp.asarray(inverse_frequencies(HD))[:, None] * (index - start).astype(F32)[None, :]
    cosine = jnp.cos(angle)
    sine = jnp.sin(angle)
    normed, packed = keys_values(tokens, gain_one, w_key, w_value, cosine, sine)
    ups = [chips_up(packed, hop) for hop in range(1, hops + 1)]
    beside = other_core(packed)
    query_t = rotate_t(dims(w_query, normed, 0, 1), cosine, sine).astype(BF)
    d_act = dims(cotangent, w_down, 1, 1)
    cot_other = other_core(cotangent)
    normed_other = other_core(normed)
    ups, query_t, d_act = together(ups, query_t, d_act)
    blocks = [packed, beside]
    for near in ups:
        blocks += [near, other_core(near)]

    outs, mixes, lses = [], [], []
    filled = None
    gathered = None
    for half in range(HALVES):
        out, mixed, lse = attend(half, ids, doc_lengths, query_t, blocks, kv_heads)
        outs.append(out)
        mixes.append(mixed)
        lses.append(lse)
        waiting = gathered
        if waiting is not None:
            waiting, mixed, w_all = together(waiting, mixed, w_all)
            out_weights = [w_all, other_core(w_all)]
        query_t, mixed = together(query_t, mixed)
        gathered = gather_near(mixed)
        if waiting is not None:
            filled = attn_out(half - 1, ids, tokens, gain_two, waiting, out_weights, filled)
            gathered, filled = together(gathered, filled)
    hidden_one, normed_two = attn_out(
        HALVES - 1, ids, tokens, gain_two, gathered, out_weights, filled
    )

    act, d_gate, d_up = ffn_forward(normed_two, d_act, w_gate, w_up)
    act_other = other_core(act)
    d_gates = [d_gate, other_core(d_gate)]
    d_ups = [d_up, other_core(d_up)]
    normed_two_other = other_core(normed_two)
    grad_down = grad_down_of(ids, act, act_other, cotangent, cot_other, part)
    d_gate_then, _ = together(d_gate, grad_down)
    grad_down = scatter(grad_down, 1)
    d_norm_pieces = pair_nt(narrow, ids, d_gate_then, d_up, w_gate, w_up)
    normed_two_then, d_norm_pieces = together(normed_two, d_norm_pieces)
    d_norm_pieces = exchange(d_norm_pieces)
    grad_gate_up = grad_in_of(ids, normed_two_then, normed_two_other, d_gates, d_ups, part)
    act_then, _ = together(act, grad_gate_up)
    ffn_pieces = down_of(narrow, ids, act_then, w_down)
    mixed_others = [other_core(m) for m in mixes]
    d_norm_pieces, ffn_pieces, mixed_others = together(d_norm_pieces, ffn_pieces, mixed_others)
    grad_gate_up = scatter(grad_gate_up, 0)

    d_hidden, d_hidden_b, gain_two_part, *made = norm_two_back(
        ids,
        doc_lengths,
        hidden_one,
        cotangent,
        gain_two,
        d_norm_pieces,
        out_weights,
        ffn_pieces[1:],
    )
    d_mixed, travel = made[:narrow], made[narrow:]
    d_mixed = exchange(d_mixed)
    d_mixed, travel = together(d_mixed, travel)
    travel = [swap(value, d + 1) for d, value in enumerate(travel)]

    d_query_r, d_blocks = attend_back(
        ids, doc_lengths, query_t, d_mixed, outs, lses, blocks, kv_heads
    )
    d_query_r, d_blocks, travel[:-1] = together(d_query_r, d_blocks, travel[:-1])
    d_blocks = d_blocks.reshape(2 * (hops + 1), 2 * k_width, rows)
    for_other = other_core(d_blocks[1::2])
    both = [
        d_blocks[2 * hop].astype(F32) + for_other[hop].astype(F32) for hop in range(hops + 1)
    ]
    down = chips_down(both[hops].astype(BF), 1)
    for hop in range(hops - 1, 0, -1):
        down = chips_down((both[hop] + down.astype(F32)).astype(BF), 1)
    d_kv = both[0]

    d_query = rotate_t(d_query_r * (1.0 / math.sqrt(HD)), cosine, -sine).astype(BF)
    (d_hidden_full,) = in_order(ids, [d_hidden_b, *travel], 1)
    grad_query = grad_proj_of(
        ids, [d_query], [other_core(d_query)], normed, normed_other, part, "grad_query"
    )
    grad_out = grad_proj_of(
        ids, mixes, mixed_others, d_hidden_full, other_core(d_hidden_full), part, "grad_out"
    )
    down, grad_out, grad_query, grad_down = together(down, grad_out, grad_query, grad_down)
    d_kv = d_kv + down.astype(F32)
    d_keys = rotate_t(d_kv[:k_width], cosine, -sine).astype(BF)
    d_values = d_kv[k_width:].astype(BF)
    norm_one_part = (
        dims(d_query, w_query, 0, 1) + dims(d_keys, w_key, 0, 1) + dims(d_values, w_value, 0, 1)
    ).astype(BF)
    norm_one_pieces = [rows_of(norm_one_part, d) for d in range(narrow)]
    d_pair = jnp.concatenate([d_keys, d_values], axis=0)
    d_pair, norm_one_pieces = together(d_pair, norm_one_pieces)
    norm_one_pieces = exchange(norm_one_pieces)
    grad_pair = grad_proj_of(
        ids, [d_pair], [other_core(d_pair)], normed, normed_other, part, "grad_key_value"
    )
    grads = jnp.concatenate([grad_out, grad_query, grad_pair], axis=0)
    norm_one_pieces, grads = together(norm_one_pieces, grads)
    last, gain_one_part = last_rows(
        ids,
        tokens,
        hidden_one,
        d_hidden,
        gain_one,
        norm_one_pieces,
        [ffn_pieces[0], *travel],
    )
    last_pieces = gather_near(last)
    gains = jnp.concatenate([gain_one_part, gain_two_part], axis=0)
    grads, grad_gate_up, last_pieces[1:-1] = together(grads, grad_gate_up, last_pieces[1:-1])
    grads = scatter(grads, 1)
    input_grad, output = in_order(ids, last_pieces, 2)
    gains, output = together(gains, output)
    gains = sum(gather_near(gains)[1:], gains)
    gains = gains + other_core(gains)
    gain_sum = 0.0
    for hop in range(wide // 2):
        target = lax.rem(me_wide + 2 * hop, wide)
        piece = lax.dynamic_slice_in_dim(gains, target * part, part, 1)
        if hop:
            piece = lax.ppermute(piece, "wide", [(i, (i + 2 * hop) % wide) for i in range(wide)])
        gain_sum = gain_sum + piece
    gains = gain_sum
    grad_gate = grad_gate_up[:, :units].astype(F32)
    grad_up = grad_gate_up[:, units:].astype(F32)
    grad_down = grad_down.astype(F32)
    grads, gains, input_grad, output, grad_gate, grad_up, grad_down = together(
        grads, gains, input_grad, output, grad_gate, grad_up, grad_down
    )
    grad_out, grad_query, grad_key, grad_value = finish(
        grads, (w_out.shape[0], q_width, k_width, k_width)
    )
    return (
        output,
        input_grad,
        gains[0],
        grad_query,
        grad_key,
        grad_value,
        grad_out,
        gains[1],
        grad_gate,
        grad_up,
        grad_down,
    )


def solution(mesh):
    in_specs = (
        P("wide", None),
        P(),
        P(None, "narrow"),
        P(None, "narrow"),
        P(None, "narrow"),
        P("narrow", None),
        P(),
        P(None, "narrow"),
        P(None, "narrow"),
        P("narrow", None),
        P(),
        P("wide", None),
    )
    out_specs = (
        P("wide", None),
        P("wide", None),
        P("wide"),
        P("wide", "narrow"),
        P("wide", "narrow"),
        P("wide", "narrow"),
        P("narrow", "wide"),
        P("wide"),
        P("wide", "narrow"),
        P("wide", "narrow"),
        P("narrow", "wide"),
    )
    return jax.shard_map(body, mesh=mesh, in_specs=in_specs, out_specs=out_specs, check_vma=False)
```

```python
import functools
import math

import jax
import jax.numpy as jnp
import numpy as np
from jax import lax
from jax.experimental import pallas as pl
from jax.experimental.pallas import tpu as pltpu
from jax.sharding import PartitionSpec as P

HD = 64
DOCS = 12
NORM_EPS = 1e-05
MASKED_SCORE = -1e30
LOG2E = math.log2(math.e)
SCALE2 = LOG2E / math.sqrt(HD)
KT = 256
HALVES = 2
BF = jnp.bfloat16
F32 = jnp.float32


def inverse_frequencies(head_size):
    frequency = 1.0 / 500000.0 ** (np.arange(0, head_size, 2) / head_size)
    wavelength = 2 * math.pi / frequency
    smoothing = (8192.0 / wavelength - 1.0) / 3.0
    scaled_freq = np.where(wavelength > 8192.0, frequency / 32.0, frequency)
    middle_band = (wavelength <= 8192.0) & (wavelength >= 2048.0)
    scaled_freq = np.where(
        middle_band, (1 - smoothing) * frequency / 32.0 + smoothing * frequency, scaled_freq
    )
    return scaled_freq.astype(np.float32)


def doc_offsets(doc_lengths, index):
    ends = jnp.cumsum(doc_lengths)
    passed = (index[None, :] >= ends[:, None]).astype(jnp.int32)
    return jnp.sum(passed * doc_lengths[:, None], axis=0)


def rotate_t(values, cosine, sine):
    heads = values.shape[0] // HD
    shaped = values.reshape(heads, 2, HD // 2, values.shape[1])
    first = shaped[:, 0]
    second = shaped[:, 1]
    return jnp.stack(
        [first * cosine - second * sine, second * cosine + first * sine], axis=1
    ).reshape(values.shape)


def dims(left, right, a, b):
    return lax.dot_general(left, right, (((a,), (b,)), ((), ())), preferred_element_type=F32)


def vmem_spec():
    return pl.BlockSpec(memory_space=pltpu.VMEM)


def smem_spec():
    return pl.BlockSpec(memory_space=pltpu.SMEM)


def any_spec():
    return pl.BlockSpec(memory_space=pl.ANY)


def cost(flops, moved, exps=0):
    return pl.CostEstimate(flops=int(flops), transcendentals=int(exps), bytes_accessed=int(moved))


def rms_scale(values):
    return lax.rsqrt(jnp.mean(values * values, axis=-1, keepdims=True) + NORM_EPS)


def keys_values_kernel(x_ref, gain_ref, wk_ref, wv_ref, cos_ref, sin_ref, normed_ref, packed_ref):
    rows = x_ref.shape[0]
    step = min(128, rows)
    for at in range(0, rows, step):
        values = x_ref[at : at + step, :].astype(F32)
        normed_ref[at : at + step, :] = (values * rms_scale(values) * gain_ref[...]).astype(BF)
    normed = normed_ref[...]
    keys = jnp.dot(normed, wk_ref[...], preferred_element_type=F32).T
    width = keys.shape[0]
    half = HD // 2
    for head in range(width // HD):
        first = keys[head * HD : head * HD + half]
        second = keys[head * HD + half : (head + 1) * HD]
        cosine, sine = cos_ref[...], sin_ref[...]
        packed_ref[head * HD : head * HD + half, :] = (first * cosine - second * sine).astype(BF)
        packed_ref[head * HD + half : (head + 1) * HD, :] = (
            second * cosine + first * sine
        ).astype(BF)
    packed_ref[width:, :] = jnp.dot(normed, wv_ref[...], preferred_element_type=F32).T.astype(BF)


def keys_values(tokens, gain, w_key, w_value, cosine, sine):
    rows, width = tokens.shape
    kv = w_key.shape[1]
    return pl.pallas_call(
        keys_values_kernel,
        in_specs=[vmem_spec()] * 6,
        out_specs=[vmem_spec()] * 2,
        out_shape=[
            jax.ShapeDtypeStruct((rows, width), BF),
            jax.ShapeDtypeStruct((2 * kv, rows), BF),
        ],
        name="keys_values",
        cost_estimate=cost(4 * rows * width * kv, 4 * rows * width + 4 * width * kv),
    )(tokens, gain, w_key, w_value, cosine, sine)


def window(lengths_ref, index):
    end = lengths_ref[0]
    start = jnp.zeros_like(index)
    for doc in range(1, DOCS):
        start = jnp.where(index >= end, end, start)
        if doc == DOCS - 1:
            last = end
        end = end + lengths_ref[doc]
    valid = index < last
    return jnp.where(valid, start, index), valid


def tile_state(ids_ref, edges, tile, half, q_rows, rows):
    me_wide = ids_ref[2]
    slot = tile // (rows // KT)
    block = (me_wide // 2 - slot // 2) * 2 + (ids_ref[1] ^ (slot % 2))
    key_base = block * rows + (tile % (rows // KT)) * KT
    q_base = me_wide * rows + half * q_rows
    low, high = edges[half]
    active = (key_base <= q_base + q_rows - 1) & (key_base + KT > low)
    whole = (key_base + KT - 1 <= q_base) & (key_base >= high)
    return active, active & whole, key_base, q_base


def window_edges(ids_ref, lengths_ref, rows):
    base = ids_ref[2] * rows
    step = rows // HALVES
    return [
        (
            window(lengths_ref, base + half * step)[0],
            window(lengths_ref, base + (half + 1) * step - 1)[0],
        )
        for half in range(HALVES)
    ]


def query_row(ids_ref, rows, half):
    step = rows // HALVES
    return ids_ref[2] * rows + half * step + lax.broadcasted_iota(jnp.int32, (1, step), 1)


def tile_mask(key_base, q_base, start_row):
    q_rows = start_row.shape[1]
    keys = key_base + lax.broadcasted_iota(jnp.int32, (KT, q_rows), 0)
    queries = q_base + lax.broadcasted_iota(jnp.int32, (KT, q_rows), 1)
    return (keys <= queries) & (keys >= start_row)


def both_ways(active, whole, run):
    pl.when(whole)(lambda: run(False))
    pl.when(active & jnp.logical_not(whole))(lambda: run(True))


def attend_kernel(slots, group, half, ids_ref, lengths_ref, q_ref, *refs):
    k_refs = refs[:slots]
    v_refs = refs[slots : 2 * slots]
    o_ref, mixed_ref, lse_ref, keys_s, values_s, top_s, sum_s, acc_s = refs[2 * slots :]
    q_rows = q_ref.shape[1]
    rows = k_refs[0].shape[1]
    per = rows // KT
    tiles = slots * per
    edges = window_edges(ids_ref, lengths_ref, rows)
    start_row, valid_row = window(lengths_ref, query_row(ids_ref, rows, half))
    for slot in range(slots):
        for part in range(per):
            tile = slot * per + part
            cut = slice(part * KT, (part + 1) * KT)

            @pl.when(tile_state(ids_ref, edges, tile, half, q_rows, rows)[0])
            def _(tile=tile, slot=slot, cut=cut):
                keys_s[tile] = k_refs[slot][:, cut].T
                values_s[tile] = v_refs[slot][:, cut]

    top_s[...] = jnp.full_like(top_s, MASKED_SCORE)
    sum_s[...] = jnp.zeros_like(sum_s)
    acc_s[...] = jnp.zeros_like(acc_s)
    heads = range(group)

    def step(tile, carry):
        active, whole, key_base, q_base = tile_state(ids_ref, edges, tile, half, q_rows, rows)

        def run(masked):
            keys = keys_s[tile]
            values = values_s[tile]
            scores = [
                jnp.dot(keys, q_ref[h * HD : (h + 1) * HD, :], preferred_element_type=F32)
                for h in heads
            ]
            if masked:
                allowed = tile_mask(key_base, q_base, start_row)
                scores = [jnp.where(allowed, s, MASKED_SCORE) for s in scores]
            tops, decays = [], []
            for h in heads:
                old = top_s[h : h + 1, :]
                new = jnp.maximum(old, jnp.max(scores[h], axis=0, keepdims=True))
                top_s[h : h + 1, :] = new
                tops.append(new)
                decays.append(jnp.exp2((old - new) * SCALE2))
            for h in heads:
                weight = jnp.exp2((scores[h] - tops[h]) * SCALE2)
                sum_s[h : h + 1, :] = sum_s[h : h + 1, :] * decays[h] + jnp.sum(
                    weight, axis=0, keepdims=True
                )
                acc_s[h] = acc_s[h] * decays[h] + jnp.dot(
                    values, weight.astype(BF), preferred_element_type=F32
                )

        both_ways(active, whole, run)
        return carry

    lax.fori_loop(0, tiles, step, 0)
    for h in heads:
        h_cut = slice(h * HD, (h + 1) * HD)
        total = sum_s[h : h + 1, :]
        out = acc_s[h] / total
        o_ref[h_cut, :] = out
        mixed_ref[h_cut, :] = jnp.where(valid_row, out, 0.0).astype(BF)
        lse_ref[0, h : h + 1, :] = top_s[h : h + 1, :] * SCALE2 + jnp.log(total) * LOG2E


def attend(half, ids, lengths, q_t, blocks, kv_heads):
    slots = len(blocks)
    heads = q_t.shape[0] // HD
    group = heads // kv_heads
    rows = q_t.shape[1]
    q_rows = rows // HALVES
    tiles = slots * (rows // KT)
    out_spec = pl.BlockSpec((group * HD, q_rows), lambda g: (g, 0))
    return pl.pallas_call(
        functools.partial(attend_kernel, slots, group, half),
        grid=(kv_heads,),
        in_specs=[
            smem_spec(),
            smem_spec(),
            pl.BlockSpec((group * HD, q_rows), lambda g: (g, half)),
        ]
        + [pl.BlockSpec((HD, rows), lambda g: (g, 0))] * slots
        + [pl.BlockSpec((HD, rows), lambda g: (kv_heads + g, 0))] * slots,
        out_specs=[out_spec, out_spec, pl.BlockSpec((1, group, q_rows), lambda g: (g, 0, 0))],
        out_shape=[
            jax.ShapeDtypeStruct((heads * HD, q_rows), F32),
            jax.ShapeDtypeStruct((heads * HD, q_rows), BF),
            jax.ShapeDtypeStruct((kv_heads, group, q_rows), F32),
        ],
        scratch_shapes=[
            pltpu.VMEM((tiles, KT, HD), BF),
            pltpu.VMEM((tiles, HD, KT), BF),
            pltpu.VMEM((group, q_rows), F32),
            pltpu.VMEM((group, q_rows), F32),
            pltpu.VMEM((group, HD, q_rows), F32),
        ],
        name="attend",
        cost_estimate=cost(
            16 * heads * q_rows * rows * HD, 8 * rows * heads * HD, heads * q_rows * rows * 4
        ),
    )(ids, lengths, q_t, *blocks, *blocks)


def attend_back_kernel(slots, group, members, ids_ref, lengths_ref, q_ref, *refs):
    do_refs, refs = refs[:members], refs[members:]
    o_refs, lse_refs, refs = refs[:HALVES], refs[HALVES : 2 * HALVES], refs[2 * HALVES :]
    k_refs, v_refs, refs = refs[:slots], refs[slots : 2 * slots], refs[2 * slots :]
    dq_ref, dkv_ref = refs[:2]
    keys_s, values_s, keys_t_s, dk_s, dv_s, q_s, do_s, do_t_s, dq_s, delta_s = refs[2:]
    rows = q_ref.shape[1]
    q_rows = rows // HALVES
    per = rows // KT
    tiles = slots * per
    heads = range(group)
    edges = window_edges(ids_ref, lengths_ref, rows)

    def any_active(tile):
        found = tile_state(ids_ref, edges, tile, 0, q_rows, rows)[0]
        for half in range(1, HALVES):
            found = found | tile_state(ids_ref, edges, tile, half, q_rows, rows)[0]
        return found

    for slot in range(slots):
        for part in range(per):
            tile = slot * per + part
            cut = slice(part * KT, (part + 1) * KT)

            @pl.when(any_active(tile))
            def _(tile=tile, slot=slot, cut=cut):
                keys_s[tile] = k_refs[slot][:, cut].T
                keys_t_s[tile] = k_refs[slot][:, cut]
                values_s[tile] = v_refs[slot][:, cut].T
                dk_s[tile] = jnp.zeros((KT, HD), F32)
                dv_s[tile] = jnp.zeros((KT, HD), F32)

    shard = do_refs[0].shape[0]
    for distance in range(members):
        at = pl.multiple_of((ids_ref[0] ^ distance) * shard, shard)
        do_s[pl.ds(at, shard), :] = do_refs[distance][...]
    do_t_s[...] = do_s[...].T

    for half in range(HALVES):
        q_cut = slice(half * q_rows, (half + 1) * q_rows)
        for h in heads:
            h_cut = slice(h * HD, (h + 1) * HD)
            q_s[h] = q_ref[h_cut, q_cut].T
            delta_s[h : h + 1, :] = jnp.sum(
                do_t_s[h_cut, q_cut].astype(F32) * o_refs[half][h_cut, :], axis=0, keepdims=True
            )
        dq_s[...] = jnp.zeros_like(dq_s)
        start_row = window(lengths_ref, query_row(ids_ref, rows, half))[0]

        def step(tile, carry, half=half, q_cut=q_cut, start_row=start_row):
            active, whole, key_base, q_base = tile_state(ids_ref, edges, tile, half, q_rows, rows)

            def run(masked):
                keys = keys_s[tile]
                values = values_s[tile]
                keys_t = keys_t_s[tile]
                scores = [
                    jnp.dot(keys, q_ref[h * HD : (h + 1) * HD, q_cut], preferred_element_type=F32)
                    for h in heads
                ]
                prob_grads = [
                    jnp.dot(values, do_t_s[h * HD : (h + 1) * HD, q_cut], preferred_element_type=F32)
                    for h in heads
                ]
                if masked:
                    allowed = tile_mask(key_base, q_base, start_row)
                probs, d_scores = [], []
                for h in heads:
                    scaled = scores[h] * SCALE2 - lse_refs[half][0, h : h + 1, :]
                    if masked:
                        scaled = jnp.where(allowed, scaled, MASKED_SCORE)
                    prob = jnp.exp2(scaled)
                    probs.append(prob.astype(BF))
                    d_scores.append((prob * (prob_grads[h] - delta_s[h : h + 1, :])).astype(BF))
                dk = dk_s[tile]
                dv = dv_s[tile]
                for h in heads:
                    dv = dv + jnp.dot(
                        probs[h],
                        do_s[q_cut, h * HD : (h + 1) * HD],
                        preferred_element_type=F32,
                    )
                    dk = dk + jnp.dot(d_scores[h], q_s[h], preferred_element_type=F32)
                    dq_s[h] += jnp.dot(keys_t, d_scores[h], preferred_element_type=F32)
                dk_s[tile] = dk
                dv_s[tile] = dv

            both_ways(active, whole, run)
            return carry

        lax.fori_loop(0, tiles, step, 0)
        for h in heads:
            dq_ref[h * HD : (h + 1) * HD, q_cut] = dq_s[h]
    for slot in range(slots):
        for part in range(per):
            cut = slice(part * KT, (part + 1) * KT)
            tile = slot * per + part
            active = any_active(tile)

            @pl.when(active)
            def _(tile=tile, slot=slot, cut=cut):
                dkv_ref[slot, 0, :, cut] = (dk_s[tile].T * (1.0 / math.sqrt(HD))).astype(BF)
                dkv_ref[slot, 1, :, cut] = dv_s[tile].T.astype(BF)

            @pl.when(jnp.logical_not(active))
            def _(slot=slot, cut=cut):
                dkv_ref[slot, 0, :, cut] = jnp.zeros((HD, KT), BF)
                dkv_ref[slot, 1, :, cut] = jnp.zeros((HD, KT), BF)


def attend_back(ids, lengths, q_t, do_pieces, outs, lses, blocks, kv_heads):
    slots = len(blocks)
    heads = q_t.shape[0] // HD
    group = heads // kv_heads
    rows = q_t.shape[1]
    q_rows = rows // HALVES
    tiles = slots * (rows // KT)
    members = len(do_pieces)
    wide = group * HD
    q_spec = pl.BlockSpec((wide, rows), lambda g: (g, 0))
    return pl.pallas_call(
        functools.partial(attend_back_kernel, slots, group, members),
        grid=(kv_heads,),
        in_specs=[smem_spec(), smem_spec(), q_spec]
        + [pl.BlockSpec((rows // members, wide), lambda g: (0, g))] * members
        + [pl.BlockSpec((wide, q_rows), lambda g: (g, 0))] * HALVES
        + [pl.BlockSpec((1, group, q_rows), lambda g: (g, 0, 0))] * HALVES
        + [pl.BlockSpec((HD, rows), lambda g: (g, 0))] * slots
        + [pl.BlockSpec((HD, rows), lambda g: (kv_heads + g, 0))] * slots,
        out_specs=[q_spec, pl.BlockSpec((slots, 2, HD, rows), lambda g: (0, 0, g, 0))],
        out_shape=[
            jax.ShapeDtypeStruct(q_t.shape, F32),
            jax.ShapeDtypeStruct((slots, 2, kv_heads * HD, rows), BF),
        ],
        scratch_shapes=[
            pltpu.VMEM((tiles, KT, HD), BF),
            pltpu.VMEM((tiles, KT, HD), BF),
            pltpu.VMEM((tiles, HD, KT), BF),
            pltpu.VMEM((tiles, KT, HD), F32),
            pltpu.VMEM((tiles, KT, HD), F32),
            pltpu.VMEM((group, q_rows, HD), BF),
            pltpu.VMEM((rows, wide), BF),
            pltpu.VMEM((wide, rows), BF),
            pltpu.VMEM((group, HD, q_rows), F32),
            pltpu.VMEM((group, q_rows), F32),
        ],
        name="attend_back",
        cost_estimate=cost(
            40 * heads * rows * rows * HD, 16 * rows * heads * HD, heads * rows * rows * 4
        ),
    )(ids, lengths, q_t, *do_pieces, *outs, *lses, *blocks, *blocks)


def fetch_weights(members, ids_ref, weights, held, sems):
    size = held.shape[0] // (2 * members)
    copies = []
    for distance in range(members):
        for other in range(2):
            index = 2 * distance + other
            source = pl.multiple_of((ids_ref[0] ^ distance) * size, size)
            copy = pltpu.make_async_copy(
                weights[other].at[pl.ds(source, size), :],
                held.at[index * size : (index + 1) * size, :],
                sems.at[index],
            )
            copy.start()
            first = pl.multiple_of((ids_ref[1] ^ other) * size, size)
            copies.append((copy, distance, index * size, first))
    return copies, size


def attn_out_kernel(members, ids_ref, x_ref, gain_ref, *refs):
    mixes, weights = refs[:members], refs[members : members + 2]
    hidden_ref, normed_ref, held, sems = refs[-4:]
    copies, size = fetch_weights(members, ids_ref, weights, held, sems)
    hidden_ref[...] = x_ref[...].astype(F32)
    for copy, distance, at, first in copies:
        copy.wait()
        hidden_ref[...] += dims(
            mixes[distance][pl.ds(first, size), :], held[at : at + size, :], 0, 0
        )
    rows = hidden_ref.shape[0]
    step = min(64, rows)
    for at in range(0, rows, step):
        hidden = hidden_ref[at : at + step, :]
        normed_ref[at : at + step, :] = (hidden * rms_scale(hidden) * gain_ref[...]).astype(BF)


def attn_out(half, ids, tokens, gain, mixes, weights, filled):
    rows, width = tokens.shape
    half_rows = rows // HALVES
    inner = sum(w.shape[0] for w in weights)
    out_spec = pl.BlockSpec((half_rows, width), lambda i: (half, 0))
    operands = [ids, tokens, gain, *mixes, *weights]
    extra = [] if filled is None else list(filled)
    return pl.pallas_call(
        functools.partial(attn_out_kernel, len(mixes)),
        grid=(1,),
        in_specs=[smem_spec(), out_spec, vmem_spec()]
        + [vmem_spec()] * len(mixes)
        + [any_spec()] * (len(weights) + len(extra)),
        out_specs=[out_spec, out_spec],
        out_shape=[
            jax.ShapeDtypeStruct((rows, width), F32),
            jax.ShapeDtypeStruct((rows, width), BF),
        ],
        scratch_shapes=[
            pltpu.VMEM((inner, width), BF),
            pltpu.SemaphoreType.DMA((2 * len(mixes),)),
        ],
        input_output_aliases={len(operands) + i: i for i in range(len(extra))},
        name="attn_out",
        cost_estimate=cost(
            2 * half_rows * inner * width, 2 * inner * width + 12 * half_rows * width
        ),
    )(*operands, *extra)


def row_sum(refs):
    total = refs[0][...].astype(F32)
    for ref in refs[1:]:
        total = total + ref[...].astype(F32)
    return total


def norm_back(grad_normed, gain, values, inverse):
    scaled = grad_normed * gain
    return inverse * scaled - values * inverse**3 * jnp.mean(
        scaled * values, axis=-1, keepdims=True
    )


def norm_two_back_kernel(members, ids_ref, lengths_ref, hidden_ref, cot_ref, gain_ref, *refs):
    pieces, refs = refs[:members], refs[members:]
    weights, refs = refs[:2], refs[2:]
    refs = refs[members - 1 :]
    sum_ref, low_ref, part_ref = refs[:3]
    d_mixed, refs = refs[3 : 3 + members], refs[3 + members :]
    sent, (held, sems) = refs[:-2], refs[-2:]
    copies, size = fetch_weights(members, ids_ref, weights, held, sems)
    grad = row_sum(pieces)
    hidden = hidden_ref[...]
    inverse = rms_scale(hidden)
    part_ref[...] = jnp.sum(grad * hidden * inverse, axis=0, keepdims=True)
    total = cot_ref[...].astype(F32) + norm_back(grad, gain_ref[...], hidden, inverse)
    sum_ref[...] = total
    low = total.astype(BF)
    low_ref[...] = low
    for ref in sent:
        ref[...] = low
    shard = hidden.shape[0]
    begin = (ids_ref[2] * members + ids_ref[0]) * shard
    keep = window(lengths_ref, begin + lax.broadcasted_iota(jnp.int32, (shard, 1), 0))[1]
    for copy, distance, at, first in copies:
        copy.wait()
        out = jnp.where(keep, dims(low, held[at : at + size, :], 1, 1), 0.0)
        d_mixed[distance][:, pl.ds(first, size)] = out.astype(BF)


def norm_two_back(ids, lengths, hidden, cotangent, gain, pieces, weights, travel):
    members = len(pieces)
    shard, width = pieces[0].shape
    inner = sum(w.shape[0] for w in weights)
    mine = pl.BlockSpec((shard, width), lambda i, ids, lengths: (ids[0], 0))
    whole = pl.BlockSpec((shard, width), lambda i, ids, lengths: (0, 0))
    line = pl.BlockSpec((1, width), lambda i, ids, lengths: (0, 0))
    head_spec = pl.BlockSpec((shard, inner // members), lambda i, ids, lengths: (0, 0))
    return pl.pallas_call(
        functools.partial(norm_two_back_kernel, members),
        grid_spec=pltpu.PrefetchScalarGridSpec(
            num_scalar_prefetch=2,
            grid=(1,),
            in_specs=[mine, mine, line]
            + [whole] * members
            + [any_spec()] * (len(weights) + len(travel)),
            out_specs=[whole, whole, line] + [head_spec] * members + [whole] * len(travel),
            scratch_shapes=[
                pltpu.VMEM((inner, width), BF),
                pltpu.SemaphoreType.DMA((2 * members,)),
            ],
        ),
        out_shape=[
            jax.ShapeDtypeStruct((shard, width), F32),
            jax.ShapeDtypeStruct((shard, width), BF),
            jax.ShapeDtypeStruct((1, width), F32),
        ]
        + [jax.ShapeDtypeStruct((shard, inner // members), BF)] * members
        + [jax.ShapeDtypeStruct(t.shape, BF) for t in travel],
        input_output_aliases={
            5 + members + len(weights) + i: 3 + members + i for i in range(len(travel))
        },
        name="norm_two_back",
        cost_estimate=cost(2 * shard * inner * width, 2 * inner * width + 24 * shard * width),
    )(ids, lengths, hidden, cotangent, gain, *pieces, *weights, *travel)


def last_rows_kernel(members, ids_ref, x_ref, hidden_ref, add_ref, gain_ref, *refs):
    pieces, ffn, (low_ref, part_ref) = refs[:members], refs[members:-2], refs[-2:]
    grad = row_sum(pieces)
    values = x_ref[...].astype(F32)
    shard = values.shape[0]
    inverse = rms_scale(values)
    part_ref[...] = jnp.sum(grad * values * inverse, axis=0, keepdims=True)
    low_ref[:shard, :] = (
        add_ref[...] + norm_back(grad, gain_ref[...], values, inverse)
    ).astype(BF)
    low_ref[shard:, :] = (hidden_ref[...] + row_sum(ffn)).astype(BF)


def last_rows(ids, tokens, hidden, add, gain, pieces, ffn_pieces):
    shard, width = pieces[0].shape
    mine = pl.BlockSpec((shard, width), lambda i, ids: (ids[0], 0))
    first = pl.BlockSpec((shard, width), lambda i, ids: (0, 0))
    second = pl.BlockSpec((shard, width), lambda i, ids: (1, 0))
    line = pl.BlockSpec((1, width), lambda i, ids: (0, 0))
    both = pl.BlockSpec((2 * shard, width), lambda i, ids: (0, 0))
    return pl.pallas_call(
        functools.partial(last_rows_kernel, len(pieces)),
        grid_spec=pltpu.PrefetchScalarGridSpec(
            num_scalar_prefetch=1,
            grid=(1,),
            in_specs=[mine, mine, first, line]
            + [first] * (len(pieces) + 1)
            + [second] * (len(ffn_pieces) - 1),
            out_specs=[both, line],
        ),
        out_shape=[
            jax.ShapeDtypeStruct((2 * shard, width), BF),
            jax.ShapeDtypeStruct((1, width), F32),
        ],
        name="last_rows",
        cost_estimate=cost(30 * shard * width, 32 * shard * width),
    )(ids, tokens, hidden, add, gain, *pieces, *ffn_pieces)


def in_order_kernel(shard, outs, ids_ref, *refs):
    pieces, out_refs = refs[:-outs], refs[-outs:]
    for distance, ref in enumerate(pieces):
        at = pl.multiple_of((ids_ref[0] ^ distance) * shard, shard)
        for index, out_ref in enumerate(out_refs):
            out_ref[pl.ds(at, shard), :] = ref[index * shard : (index + 1) * shard, :]


def in_order(ids, pieces, outs):
    width = pieces[0].shape[1]
    shard = pieces[0].shape[0] // outs if outs > 1 else pieces[0].shape[0]
    rows = shard * len(pieces)
    return pl.pallas_call(
        functools.partial(in_order_kernel, shard, outs),
        in_specs=[smem_spec()] + [vmem_spec()] * len(pieces),
        out_specs=[vmem_spec()] * outs,
        out_shape=[jax.ShapeDtypeStruct((rows, width), pieces[0].dtype)] * outs,
        name="token_order",
        cost_estimate=cost(0, 4 * rows * outs * width),
    )(ids, *pieces)


def ffn_kernel(n_ref, da_ref, wg_ref, wu_ref, act_ref, dg_ref, du_ref):
    normed = n_ref[...]
    gate = jnp.dot(normed, wg_ref[...], preferred_element_type=F32)
    up = jnp.dot(normed, wu_ref[...], preferred_element_type=F32)
    sig = jax.nn.sigmoid(gate)
    silu = gate * sig
    act_ref[...] = (silu * up).astype(BF)
    d_act = da_ref[...]
    dg_ref[...] = (d_act * up * sig * (1.0 + gate * (1.0 - sig))).astype(BF)
    du_ref[...] = (d_act * silu).astype(BF)


def ffn_forward(normed, d_act, w_gate, w_up):
    rows, width = normed.shape
    units = w_gate.shape[1]
    step = min(512, units)
    tile = pl.BlockSpec((rows, step), lambda j: (0, j))
    weight = pl.BlockSpec((width, step), lambda j: (0, j))
    return pl.pallas_call(
        ffn_kernel,
        grid=(units // step,),
        in_specs=[pl.BlockSpec((rows, width), lambda j: (0, 0)), tile, weight, weight],
        out_specs=[tile, tile, tile],
        out_shape=[jax.ShapeDtypeStruct((rows, units), BF)] * 3,
        name="gate_up",
        cost_estimate=cost(
            4 * rows * width * units,
            4 * width * units + 2 * rows * width + 10 * rows * units,
            rows * units,
        ),
    )(normed, d_act, w_gate, w_up)


def store_by_distance(ids_ref, out_refs, held, value):
    shard = value.shape[0] // len(out_refs)
    held[...] = value.astype(BF)
    for distance, out_ref in enumerate(out_refs):
        at = pl.multiple_of((ids_ref[0] ^ distance) * shard, shard)
        out_ref[...] = held[pl.ds(at, shard), :]


def pair_nt_kernel(ids_ref, a_ref, b_ref, wa_ref, wb_ref, *refs):
    value = dims(a_ref[...], wa_ref[...], 1, 1) + dims(b_ref[...], wb_ref[...], 1, 1)
    store_by_distance(ids_ref, refs[:-1], refs[-1], value)


def pair_nt(members, ids, a, b, w_a, w_b):
    rows, units = a.shape
    width = w_a.shape[0]
    step = min(512, width)
    full = pl.BlockSpec((rows, units), lambda j: (0, 0))
    weight = pl.BlockSpec((step, units), lambda j: (j, 0))
    return pl.pallas_call(
        pair_nt_kernel,
        grid=(width // step,),
        in_specs=[smem_spec(), full, full, weight, weight],
        out_specs=[pl.BlockSpec((rows // members, step), lambda j: (0, j))] * members,
        out_shape=[jax.ShapeDtypeStruct((rows // members, width), BF)] * members,
        scratch_shapes=[pltpu.VMEM((rows, step), BF)],
        name="d_normed_two",
        cost_estimate=cost(
            4 * rows * width * units, 4 * width * units + 4 * rows * units + 2 * rows * width
        ),
    )(ids, a, b, w_a, w_b)


def down_kernel(ids_ref, a_ref, w_ref, *refs):
    value = jnp.dot(a_ref[...], w_ref[...], preferred_element_type=F32)
    store_by_distance(ids_ref, refs[:-1], refs[-1], value)


def down_of(members, ids, act, w_down):
    rows, units = act.shape
    shard = rows // members
    width = w_down.shape[1]
    step = min(512, width)
    return pl.pallas_call(
        down_kernel,
        grid=(width // step,),
        in_specs=[
            smem_spec(),
            pl.BlockSpec((rows, units), lambda j: (0, 0)),
            pl.BlockSpec((units, step), lambda j: (0, j)),
        ],
        out_specs=[pl.BlockSpec((shard, step), lambda j: (0, j))]
        + [pl.BlockSpec((shard, step), lambda j: (1, j))] * (members - 1),
        out_shape=[jax.ShapeDtypeStruct((shard, width), BF)]
        + [jax.ShapeDtypeStruct((2 * shard, width), BF)] * (members - 1),
        scratch_shapes=[pltpu.VMEM((rows, step), BF)],
        name="ffn_down",
        cost_estimate=cost(
            2 * rows * width * units, 2 * width * units + 2 * rows * units + 2 * rows * width
        ),
    )(ids, act, w_down)


def column_specs(rows, part, count):
    return [
        pl.BlockSpec((rows, part), lambda j, ids, k=k: (0, 2 * k + ids[1])) for k in range(count)
    ]


def fill_columns(held, refs):
    count = len(refs) // 2
    rows, part = refs[0].shape
    for index, ref in enumerate(refs):
        top = (index // count) * rows
        left = (index % count) * part
        held[top : top + rows, left : left + part] = ref[...]


def grad_down_kernel(blocks, ids_ref, own_ref, other_ref, *refs):
    cots, (o_ref, held) = refs[: 2 * blocks], refs[2 * blocks :]

    @pl.when(pl.program_id(0) == 0)
    def _():
        fill_columns(held, cots)

    rows = own_ref.shape[0]
    o_ref[...] = (
        dims(own_ref[...], held[:rows, :], 0, 0) + dims(other_ref[...], held[rows:, :], 0, 0)
    ).astype(BF)


def grad_down_of(ids, act, act_other, cot, cot_other, part):
    rows, units = act.shape
    width = cot.shape[1]
    blocks = width // (2 * part)
    step = min(512, units)
    tile = pl.BlockSpec((rows, step), lambda j, ids: (0, j))
    columns = column_specs(rows, part, blocks)
    return pl.pallas_call(
        functools.partial(grad_down_kernel, blocks),
        grid_spec=pltpu.PrefetchScalarGridSpec(
            num_scalar_prefetch=1,
            grid=(units // step,),
            in_specs=[tile, tile] + columns + columns,
            out_specs=pl.BlockSpec((step, width // 2), lambda j, ids: (j, 0)),
            scratch_shapes=[pltpu.VMEM((2 * rows, width // 2), BF)],
        ),
        out_shape=jax.ShapeDtypeStruct((units, width // 2), BF),
        name="grad_down",
        cost_estimate=cost(
            2 * rows * width * units, 4 * rows * units + 2 * rows * width + width * units
        ),
    )(ids, act, act_other, *([cot] * blocks), *([cot_other] * blocks))


def grad_in_kernel(blocks, half, ids_ref, *refs):
    normeds, refs = refs[: 2 * blocks], refs[2 * blocks :]
    gates, ups, (o_ref, held) = refs[:2], refs[2:4], refs[4:]

    @pl.when(pl.program_id(0) == 0)
    def _():
        fill_columns(held, normeds)

    rows = gates[0].shape[0]

    def of(pair):
        o_ref[...] = (
            dims(held[:rows, :], pair[0][...], 0, 0) + dims(held[rows:, :], pair[1][...], 0, 0)
        ).astype(BF)

    pl.when(pl.program_id(0) < half)(lambda: of(gates))
    pl.when(pl.program_id(0) >= half)(lambda: of(ups))


def grad_in_of(ids, normed, normed_other, d_gates, d_ups, part):
    rows, width = normed.shape
    units = d_gates[0].shape[1]
    blocks = width // (2 * part)
    step = min(512, units)
    half = units // step
    columns = column_specs(rows, part, blocks)
    first = pl.BlockSpec((rows, step), lambda j, ids: (0, jnp.minimum(j, half - 1)))
    second = pl.BlockSpec((rows, step), lambda j, ids: (0, jnp.maximum(j - half, 0)))
    return pl.pallas_call(
        functools.partial(grad_in_kernel, blocks, half),
        grid_spec=pltpu.PrefetchScalarGridSpec(
            num_scalar_prefetch=1,
            grid=(2 * half,),
            in_specs=columns + columns + [first] * 2 + [second] * 2,
            out_specs=pl.BlockSpec((width // 2, step), lambda j, ids: (0, j)),
            scratch_shapes=[pltpu.VMEM((2 * rows, width // 2), BF)],
        ),
        out_shape=jax.ShapeDtypeStruct((width // 2, 2 * units), BF),
        name="grad_gate_up",
        cost_estimate=cost(
            4 * rows * width * units, 8 * rows * units + 2 * rows * width + 2 * width * units
        ),
    )(ids, *([normed] * blocks), *([normed_other] * blocks), *d_gates, *d_ups)


def grad_proj_kernel(lefts, ids_ref, *refs):
    own, other = refs[:lefts], refs[lefts : 2 * lefts]
    right_ref, right_other_ref, o_ref = refs[2 * lefts :]
    at = 0
    rows = right_ref.shape[0]
    part = rows // lefts
    total = 0.0
    for group, right in ((own, right_ref), (other, right_other_ref)):
        for index, left in enumerate(group):
            total = total + jnp.dot(
                left[...],
                right[index * part : (index + 1) * part, :],
                preferred_element_type=F32,
            )
    o_ref[...] = total.astype(BF)


def grad_proj_of(ids, lefts, lefts_other, right, right_other, part, name):
    inner = lefts[0].shape[0]
    rows, width = right.shape
    blocks = width // (2 * part)
    left_spec = pl.BlockSpec(lefts[0].shape, lambda k, ids: (0, 0))
    right_spec = pl.BlockSpec((rows, part), lambda k, ids: (0, 2 * k + ids[1]))
    return pl.pallas_call(
        functools.partial(grad_proj_kernel, len(lefts)),
        grid_spec=pltpu.PrefetchScalarGridSpec(
            num_scalar_prefetch=1,
            grid=(blocks,),
            in_specs=[left_spec] * (2 * len(lefts)) + [right_spec] * 2,
            out_specs=pl.BlockSpec((inner, part), lambda k, ids: (0, k)),
        ),
        out_shape=jax.ShapeDtypeStruct((inner, width // 2), BF),
        name=name,
        cost_estimate=cost(
            2 * rows * width * inner, 4 * inner * rows + 2 * rows * width + inner * width
        ),
    )(ids, *lefts, *lefts_other, right, right_other)


def finish_kernel(in_ref, out_ref, *refs):
    at = out_ref.shape[0]
    out_ref[...] = in_ref[:at, :].astype(F32)
    for ref in refs:
        count = ref.shape[1]
        ref[...] = in_ref[at : at + count, :].astype(F32).T
        at += count


def finish(grads, sizes):
    part = grads.shape[1]
    return pl.pallas_call(
        finish_kernel,
        in_specs=[vmem_spec()],
        out_specs=[vmem_spec()] * len(sizes),
        out_shape=[jax.ShapeDtypeStruct((sizes[0], part), F32)]
        + [jax.ShapeDtypeStruct((part, size), F32) for size in sizes[1:]],
        name="finish",
        cost_estimate=cost(0, 6 * sum(sizes) * part),
    )(grads)


def together(*values):
    return lax.optimization_barrier(values)


def body(
    tokens,
    attn_gain,
    w_query,
    w_key,
    w_value,
    w_out,
    ffn_gain,
    w_gate,
    w_up,
    w_down,
    doc_lengths,
    cotangent,
):
    rows, width = tokens.shape
    wide = lax.axis_size("wide")
    narrow = lax.axis_size("narrow")
    me_wide = lax.axis_index("wide")
    me = lax.axis_index("narrow")
    core = me_wide % 2
    kv_heads = w_key.shape[1] // HD
    half_rows = rows // HALVES
    shard = rows // narrow
    part = width // wide
    hops = wide // 4
    units = w_gate.shape[1]
    q_width = w_query.shape[1]
    k_width = w_key.shape[1]
    chip_groups = [list(range(0, wide, 2)), list(range(1, wide, 2))]
    ids = jnp.stack([me, core, me_wide]).astype(jnp.int32)

    def other_core(value):
        return lax.ppermute(value, "wide", [(i, i ^ 1) for i in range(wide)])

    def chips_up(value, hop):
        return lax.ppermute(value, "wide", [(i, i + 2 * hop) for i in range(wide - 2 * hop)])

    def chips_down(value, hop):
        return lax.ppermute(value, "wide", [(i + 2 * hop, i) for i in range(wide - 2 * hop)])

    def swap(value, distance):
        return lax.ppermute(value, "narrow", [(i, i ^ distance) for i in range(narrow)])

    def rows_of(value, distance):
        return lax.dynamic_slice_in_dim(value, (me ^ distance) * shard, shard, 0)

    def exchange(pieces):
        return [pieces[0]] + [swap(pieces[d], d) for d in range(1, narrow)]

    def gather_near(value):
        return [value] + [swap(value, d) for d in range(1, narrow)]

    def scatter(value, dimension):
        return lax.psum_scatter(
            value,
            "wide",
            scatter_dimension=dimension,
            axis_index_groups=chip_groups,
            tiled=True,
        )

    gain_one = attn_gain.astype(F32)[None, :]
    gain_two = ffn_gain.astype(F32)[None, :]

    w_half = w_out.shape[0] // 2
    w_mine = lax.dynamic_slice_in_dim(w_out, core * w_half, w_half, 0)
    w_all = lax.all_gather(w_mine, "narrow", axis=0, tiled=True)

    base = me_wide * rows
    index = base + jnp.arange(rows, dtype=jnp.int32)
    start = doc_offsets(doc_lengths, index)
    angle = jnp.asarray(inverse_frequencies(HD))[:, None] * (index - start).astype(F32)[None, :]
    cosine = jnp.cos(angle)
    sine = jnp.sin(angle)
    normed, packed = keys_values(tokens, gain_one, w_key, w_value, cosine, sine)
    ups = [chips_up(packed, hop) for hop in range(1, hops + 1)]
    beside = other_core(packed)
    query_t = rotate_t(dims(w_query, normed, 0, 1), cosine, sine).astype(BF)
    d_act = dims(cotangent, w_down, 1, 1)
    cot_other = other_core(cotangent)
    normed_other = other_core(normed)
    ups, query_t, d_act = together(ups, query_t, d_act)
    blocks = [packed, beside]
    for near in ups:
        blocks += [near, other_core(near)]

    outs, mixes, lses = [], [], []
    filled = None
    gathered = None
    for half in range(HALVES):
        out, mixed, lse = attend(half, ids, doc_lengths, query_t, blocks, kv_heads)
        outs.append(out)
        mixes.append(mixed)
        lses.append(lse)
        waiting = gathered
        if waiting is not None:
            waiting, mixed, w_all, normed_other = together(waiting, mixed, w_all, normed_other)
            out_weights = [w_all, other_core(w_all)]
        query_t, mixed = together(query_t, mixed)
        gathered = gather_near(mixed)
        if waiting is not None:
            filled = attn_out(half - 1, ids, tokens, gain_two, waiting, out_weights, filled)
            gathered, filled = together(gathered, filled)
    hidden_one, normed_two = attn_out(
        HALVES - 1, ids, tokens, gain_two, gathered, out_weights, filled
    )

    act, d_gate, d_up = ffn_forward(normed_two, d_act, w_gate, w_up)
    act_other = other_core(act)
    d_gates = [d_gate, other_core(d_gate)]
    d_ups = [d_up, other_core(d_up)]
    normed_two_other = other_core(normed_two)
    grad_down = grad_down_of(ids, act, act_other, cotangent, cot_other, part)
    d_gate_then, _ = together(d_gate, grad_down)
    grad_down = scatter(grad_down, 1)
    d_norm_pieces = pair_nt(narrow, ids, d_gate_then, d_up, w_gate, w_up)
    mixed_others = [other_core(m) for m in mixes]
    act_then, d_norm_pieces, d_gates, d_ups, normed_two_other, mixed_others = together(
        act, d_norm_pieces, d_gates, d_ups, normed_two_other, mixed_others
    )
    d_norm_pieces = exchange(d_norm_pieces)
    ffn_pieces = down_of(narrow, ids, act_then, w_down)
    d_norm_pieces[1], ffn_pieces, normed_two_then = together(
        d_norm_pieces[1], ffn_pieces, normed_two
    )
    grad_gate_up = grad_in_of(ids, normed_two_then, normed_two_other, d_gates, d_ups, part)
    d_norm_pieces, ffn_pieces, _ = together(d_norm_pieces, ffn_pieces, grad_gate_up)

    d_hidden, d_hidden_b, gain_two_part, *made = norm_two_back(
        ids,
        doc_lengths,
        hidden_one,
        cotangent,
        gain_two,
        d_norm_pieces,
        out_weights,
        ffn_pieces[1:],
    )
    d_mixed, travel = made[:narrow], made[narrow:]
    grad_gate_up, _ = together(grad_gate_up, d_hidden_b)
    grad_gate_up = scatter(grad_gate_up, 0)
    d_mixed = exchange(d_mixed)
    d_mixed, travel = together(d_mixed, travel)
    travel = [swap(value, d + 1) for d, value in enumerate(travel)]

    d_query_r, d_blocks = attend_back(
        ids, doc_lengths, query_t, d_mixed, outs, lses, blocks, kv_heads
    )
    d_query_r, d_blocks, travel[0] = together(d_query_r, d_blocks, travel[0])
    d_blocks = d_blocks.reshape(2 * (hops + 1), 2 * k_width, rows)
    for_other = other_core(d_blocks[1::2])
    both = [
        d_blocks[2 * hop].astype(F32) + for_other[hop].astype(F32) for hop in range(hops + 1)
    ]
    down = chips_down(both[hops].astype(BF), 1)
    for hop in range(hops - 1, 0, -1):
        down = chips_down((both[hop] + down.astype(F32)).astype(BF), 1)
    d_kv = both[0]

    d_query = rotate_t(d_query_r * (1.0 / math.sqrt(HD)), cosine, -sine).astype(BF)
    (d_hidden_full,) = in_order(ids, [d_hidden_b, *travel], 1)
    grad_query = grad_proj_of(
        ids, [d_query], [other_core(d_query)], normed, normed_other, part, "grad_query"
    )
    grad_out = grad_proj_of(
        ids, mixes, mixed_others, d_hidden_full, other_core(d_hidden_full), part, "grad_out"
    )
    down, grad_out, grad_query, grad_down = together(down, grad_out, grad_query, grad_down)
    d_kv = d_kv + down.astype(F32)
    d_keys = rotate_t(d_kv[:k_width], cosine, -sine).astype(BF)
    d_values = d_kv[k_width:].astype(BF)
    norm_one_part = (
        dims(d_query, w_query, 0, 1) + dims(d_keys, w_key, 0, 1) + dims(d_values, w_value, 0, 1)
    ).astype(BF)
    norm_one_pieces = [rows_of(norm_one_part, d) for d in range(narrow)]
    d_pair = jnp.concatenate([d_keys, d_values], axis=0)
    d_pair, norm_one_pieces = together(d_pair, norm_one_pieces)
    norm_one_pieces = exchange(norm_one_pieces)
    grad_pair = grad_proj_of(
        ids, [d_pair], [other_core(d_pair)], normed, normed_other, part, "grad_key_value"
    )
    grads = jnp.concatenate([grad_out, grad_query, grad_pair], axis=0)
    norm_one_pieces, grads = together(norm_one_pieces, grads)
    last, gain_one_part = last_rows(
        ids,
        tokens,
        hidden_one,
        d_hidden,
        gain_one,
        norm_one_pieces,
        [ffn_pieces[0], *travel],
    )
    last_pieces = gather_near(last)
    gains = jnp.concatenate([gain_one_part, gain_two_part], axis=0)
    grads, grad_gate_up, last_pieces[1:-1] = together(grads, grad_gate_up, last_pieces[1:-1])
    grads = scatter(grads, 1)
    input_grad, output = in_order(ids, last_pieces, 2)
    gains, output = together(gains, output)
    gains = sum(gather_near(gains)[1:], gains)
    gains = gains + other_core(gains)
    gain_sum = 0.0
    for hop in range(wide // 2):
        target = lax.rem(me_wide + 2 * hop, wide)
        piece = lax.dynamic_slice_in_dim(gains, target * part, part, 1)
        if hop:
            piece = lax.ppermute(piece, "wide", [(i, (i + 2 * hop) % wide) for i in range(wide)])
        gain_sum = gain_sum + piece
    gains = gain_sum
    grad_gate = grad_gate_up[:, :units].astype(F32)
    grad_up = grad_gate_up[:, units:].astype(F32)
    grad_down = grad_down.astype(F32)
    grads, gains, input_grad, output, grad_gate, grad_up, grad_down = together(
        grads, gains, input_grad, output, grad_gate, grad_up, grad_down
    )
    grad_out, grad_query, grad_key, grad_value = finish(
        grads, (w_out.shape[0], q_width, k_width, k_width)
    )
    return (
        output,
        input_grad,
        gains[0],
        grad_query,
        grad_key,
        grad_value,
        grad_out,
        gains[1],
        grad_gate,
        grad_up,
        grad_down,
    )


def solution(mesh):
    in_specs = (
        P("wide", None),
        P(),
        P(None, "narrow"),
        P(None, "narrow"),
        P(None, "narrow"),
        P("narrow", None),
        P(),
        P(None, "narrow"),
        P(None, "narrow"),
        P("narrow", None),
        P(),
        P("wide", None),
    )
    out_specs = (
        P("wide", None),
        P("wide", None),
        P("wide"),
        P("wide", "narrow"),
        P("wide", "narrow"),
        P("wide", "narrow"),
        P("narrow", "wide"),
        P("wide"),
        P("wide", "narrow"),
        P("wide", "narrow"),
        P("narrow", "wide"),
    )
    return jax.shard_map(body, mesh=mesh, in_specs=in_specs, out_specs=out_specs, check_vma=False)
```

```python
import functools
import math

import jax
import jax.numpy as jnp
import numpy as np
from jax import lax
from jax.experimental import pallas as pl
from jax.experimental.pallas import tpu as pltpu
from jax.sharding import PartitionSpec as P

HD = 64
DOCS = 12
NORM_EPS = 1e-05
MASKED_SCORE = -1e30
LOG2E = math.log2(math.e)
SCALE2 = LOG2E / math.sqrt(HD)
KT = 256
HALVES = 2
BF = jnp.bfloat16
F32 = jnp.float32


def inverse_frequencies(head_size):
    frequency = 1.0 / 500000.0 ** (np.arange(0, head_size, 2) / head_size)
    wavelength = 2 * math.pi / frequency
    smoothing = (8192.0 / wavelength - 1.0) / 3.0
    scaled_freq = np.where(wavelength > 8192.0, frequency / 32.0, frequency)
    middle_band = (wavelength <= 8192.0) & (wavelength >= 2048.0)
    scaled_freq = np.where(
        middle_band, (1 - smoothing) * frequency / 32.0 + smoothing * frequency, scaled_freq
    )
    return scaled_freq.astype(np.float32)


def doc_offsets(doc_lengths, index):
    ends = jnp.cumsum(doc_lengths)
    passed = (index[None, :] >= ends[:, None]).astype(jnp.int32)
    return jnp.sum(passed * doc_lengths[:, None], axis=0)


def rotate_t(values, cosine, sine):
    heads = values.shape[0] // HD
    shaped = values.reshape(heads, 2, HD // 2, values.shape[1])
    first = shaped[:, 0]
    second = shaped[:, 1]
    return jnp.stack(
        [first * cosine - second * sine, second * cosine + first * sine], axis=1
    ).reshape(values.shape)


def dims(left, right, a, b):
    return lax.dot_general(left, right, (((a,), (b,)), ((), ())), preferred_element_type=F32)


def vmem_spec():
    return pl.BlockSpec(memory_space=pltpu.VMEM)


def smem_spec():
    return pl.BlockSpec(memory_space=pltpu.SMEM)


def any_spec():
    return pl.BlockSpec(memory_space=pl.ANY)


def cost(flops, moved, exps=0):
    return pl.CostEstimate(flops=int(flops), transcendentals=int(exps), bytes_accessed=int(moved))


def rms_scale(values):
    return lax.rsqrt(jnp.mean(values * values, axis=-1, keepdims=True) + NORM_EPS)


def keys_values_kernel(x_ref, gain_ref, wk_ref, wv_ref, cos_ref, sin_ref, normed_ref, packed_ref):
    rows = x_ref.shape[0]
    step = min(128, rows)
    for at in range(0, rows, step):
        values = x_ref[at : at + step, :].astype(F32)
        normed_ref[at : at + step, :] = (values * rms_scale(values) * gain_ref[...]).astype(BF)
    normed = normed_ref[...]
    keys = jnp.dot(normed, wk_ref[...], preferred_element_type=F32).T
    width = keys.shape[0]
    half = HD // 2
    for head in range(width // HD):
        first = keys[head * HD : head * HD + half]
        second = keys[head * HD + half : (head + 1) * HD]
        cosine, sine = cos_ref[...], sin_ref[...]
        packed_ref[head * HD : head * HD + half, :] = (first * cosine - second * sine).astype(BF)
        packed_ref[head * HD + half : (head + 1) * HD, :] = (
            second * cosine + first * sine
        ).astype(BF)
    packed_ref[width:, :] = jnp.dot(normed, wv_ref[...], preferred_element_type=F32).T.astype(BF)


def keys_values(tokens, gain, w_key, w_value, cosine, sine):
    rows, width = tokens.shape
    kv = w_key.shape[1]
    return pl.pallas_call(
        keys_values_kernel,
        in_specs=[vmem_spec()] * 6,
        out_specs=[vmem_spec()] * 2,
        out_shape=[
            jax.ShapeDtypeStruct((rows, width), BF),
            jax.ShapeDtypeStruct((2 * kv, rows), BF),
        ],
        name="keys_values",
        cost_estimate=cost(4 * rows * width * kv, 4 * rows * width + 4 * width * kv),
    )(tokens, gain, w_key, w_value, cosine, sine)


def window(lengths_ref, index):
    end = lengths_ref[0]
    start = jnp.zeros_like(index)
    for doc in range(1, DOCS):
        start = jnp.where(index >= end, end, start)
        if doc == DOCS - 1:
            last = end
        end = end + lengths_ref[doc]
    valid = index < last
    return jnp.where(valid, start, index), valid


def tile_state(ids_ref, edge, tile, half, q_rows, rows):
    me_wide = ids_ref[2]
    slot = tile // (rows // KT)
    block = (me_wide // 2 - slot // 2) * 2 + (ids_ref[1] ^ (slot % 2))
    key_base = block * rows + (tile % (rows // KT)) * KT
    q_base = me_wide * rows + half * q_rows
    low, high = edge
    active = (key_base <= q_base + q_rows - 1) & (key_base + KT > low)
    whole = (key_base + KT - 1 <= q_base) & (key_base >= high)
    return active, active & whole, key_base, q_base


def window_edge(ids_ref, lengths_ref, rows, half):
    base = ids_ref[2] * rows
    step = rows // HALVES
    return (
        window(lengths_ref, base + half * step)[0],
        window(lengths_ref, base + (half + 1) * step - 1)[0],
    )


def query_row(ids_ref, rows, half):
    step = rows // HALVES
    return ids_ref[2] * rows + half * step + lax.broadcasted_iota(jnp.int32, (1, step), 1)


def tile_mask(key_base, q_base, start_row):
    q_rows = start_row.shape[1]
    keys = key_base + lax.broadcasted_iota(jnp.int32, (KT, q_rows), 0)
    queries = q_base + lax.broadcasted_iota(jnp.int32, (KT, q_rows), 1)
    return (keys <= queries) & (keys >= start_row)


def both_ways(active, whole, run):
    pl.when(whole)(lambda: run(False))
    pl.when(active & jnp.logical_not(whole))(lambda: run(True))


def attend_kernel(slots, group, half, ids_ref, lengths_ref, q_ref, *refs):
    k_refs = refs[:slots]
    v_refs = refs[slots : 2 * slots]
    o_ref, mixed_ref, lse_ref, keys_s, values_s, top_s, sum_s, acc_s = refs[2 * slots :]
    q_rows = q_ref.shape[1]
    rows = k_refs[0].shape[1]
    per = rows // KT
    tiles = slots * per
    edge = window_edge(ids_ref, lengths_ref, rows, half)
    start_row, valid_row = window(lengths_ref, query_row(ids_ref, rows, half))
    for slot in range(slots):
        for part in range(per):
            tile = slot * per + part
            cut = slice(part * KT, (part + 1) * KT)

            @pl.when(tile_state(ids_ref, edge, tile, half, q_rows, rows)[0])
            def _(tile=tile, slot=slot, cut=cut):
                keys_s[tile] = k_refs[slot][:, cut].T
                values_s[tile] = v_refs[slot][:, cut]

    top_s[...] = jnp.full_like(top_s, MASKED_SCORE)
    sum_s[...] = jnp.zeros_like(sum_s)
    acc_s[...] = jnp.zeros_like(acc_s)
    heads = range(group)

    def step(tile, carry):
        active, whole, key_base, q_base = tile_state(ids_ref, edge, tile, half, q_rows, rows)

        def run(masked):
            keys = keys_s[tile]
            values = values_s[tile]
            scores = [
                jnp.dot(keys, q_ref[h * HD : (h + 1) * HD, :], preferred_element_type=F32)
                for h in heads
            ]
            if masked:
                allowed = tile_mask(key_base, q_base, start_row)
                scores = [jnp.where(allowed, s, MASKED_SCORE) for s in scores]
            tops, decays = [], []
            for h in heads:
                old = top_s[h : h + 1, :]
                new = jnp.maximum(old, jnp.max(scores[h], axis=0, keepdims=True))
                top_s[h : h + 1, :] = new
                tops.append(new)
                decays.append(jnp.exp2((old - new) * SCALE2))
            for h in heads:
                weight = jnp.exp2((scores[h] - tops[h]) * SCALE2)
                sum_s[h : h + 1, :] = sum_s[h : h + 1, :] * decays[h] + jnp.sum(
                    weight, axis=0, keepdims=True
                )
                acc_s[h] = acc_s[h] * decays[h] + jnp.dot(
                    values, weight.astype(BF), preferred_element_type=F32
                )

        both_ways(active, whole, run)
        return carry

    lax.fori_loop(0, tiles, step, 0)
    for h in heads:
        h_cut = slice(h * HD, (h + 1) * HD)
        total = sum_s[h : h + 1, :]
        out = acc_s[h] / total
        o_ref[h_cut, :] = out
        mixed_ref[h_cut, :] = jnp.where(valid_row, out, 0.0).astype(BF)
        lse_ref[0, h : h + 1, :] = top_s[h : h + 1, :] * SCALE2 + jnp.log(total) * LOG2E


def attend(half, ids, lengths, q_t, blocks, kv_heads):
    slots = len(blocks)
    heads = q_t.shape[0] // HD
    group = heads // kv_heads
    rows = q_t.shape[1]
    q_rows = rows // HALVES
    tiles = slots * (rows // KT)
    out_spec = pl.BlockSpec((group * HD, q_rows), lambda g: (g, 0))
    return pl.pallas_call(
        functools.partial(attend_kernel, slots, group, half),
        grid=(kv_heads,),
        in_specs=[
            smem_spec(),
            smem_spec(),
            pl.BlockSpec((group * HD, q_rows), lambda g: (g, half)),
        ]
        + [pl.BlockSpec((HD, rows), lambda g: (g, 0))] * slots
        + [pl.BlockSpec((HD, rows), lambda g: (kv_heads + g, 0))] * slots,
        out_specs=[out_spec, out_spec, pl.BlockSpec((1, group, q_rows), lambda g: (g, 0, 0))],
        out_shape=[
            jax.ShapeDtypeStruct((heads * HD, q_rows), F32),
            jax.ShapeDtypeStruct((heads * HD, q_rows), BF),
            jax.ShapeDtypeStruct((kv_heads, group, q_rows), F32),
        ],
        scratch_shapes=[
            pltpu.VMEM((tiles, KT, HD), BF),
            pltpu.VMEM((tiles, HD, KT), BF),
            pltpu.VMEM((group, q_rows), F32),
            pltpu.VMEM((group, q_rows), F32),
            pltpu.VMEM((group, HD, q_rows), F32),
        ],
        name="attend",
        cost_estimate=cost(
            16 * heads * q_rows * rows * HD, 8 * rows * heads * HD, heads * q_rows * rows * 4
        ),
    )(ids, lengths, q_t, *blocks, *blocks)


def attend_back_kernel(slots, group, members, ids_ref, lengths_ref, q_ref, *refs):
    do_refs, refs = refs[:members], refs[members:]
    o_refs, lse_refs, refs = refs[:HALVES], refs[HALVES : 2 * HALVES], refs[2 * HALVES :]
    k_refs, v_refs, refs = refs[:slots], refs[slots : 2 * slots], refs[2 * slots :]
    dq_ref, dkv_ref = refs[:2]
    keys_s, values_s, keys_t_s, dk_s, dv_s, q_s, do_s, do_t_s, dq_s, delta_s, lse_s = refs[2:]
    rows = q_ref.shape[1]
    q_rows = rows // HALVES
    per = rows // KT
    tiles = slots * per
    heads = range(group)
    edges = [window_edge(ids_ref, lengths_ref, rows, half) for half in range(HALVES)]

    def any_active(tile):
        found = tile_state(ids_ref, edges[0], tile, 0, q_rows, rows)[0]
        for half in range(1, HALVES):
            found = found | tile_state(ids_ref, edges[half], tile, half, q_rows, rows)[0]
        return found

    for slot in range(slots):
        for part in range(per):
            tile = slot * per + part
            cut = slice(part * KT, (part + 1) * KT)

            @pl.when(any_active(tile))
            def _(tile=tile, slot=slot, cut=cut):
                keys_s[tile] = k_refs[slot][:, cut].T
                keys_t_s[tile] = k_refs[slot][:, cut]
                values_s[tile] = v_refs[slot][:, cut].T
                dk_s[tile] = jnp.zeros((KT, HD), F32)
                dv_s[tile] = jnp.zeros((KT, HD), F32)

    shard = do_refs[0].shape[0]
    for distance in range(members):
        at = pl.multiple_of((ids_ref[0] ^ distance) * shard, shard)
        do_s[pl.ds(at, shard), :] = do_refs[distance][...]
    do_t_s[...] = do_s[...].T

    for half in range(HALVES):
        for h in heads:
            h_cut = slice(h * HD, (h + 1) * HD)
            do_h = do_t_s[h_cut, half * q_rows : (half + 1) * q_rows].astype(F32)
            delta_s[half, h : h + 1, :] = jnp.sum(
                do_h * o_refs[half][h_cut, :], axis=0, keepdims=True
            )
            lse_s[half, h : h + 1, :] = lse_refs[half][0, h : h + 1, :]

    def half_step(half, carry):
        q_cut = pl.ds(pl.multiple_of(half * q_rows, q_rows), q_rows)
        edge = window_edge(ids_ref, lengths_ref, rows, half)
        for h in heads:
            q_s[h] = q_ref[h * HD : (h + 1) * HD, q_cut].T
        dq_s[...] = jnp.zeros_like(dq_s)
        start_row = window(lengths_ref, query_row(ids_ref, rows, half))[0]

        def step(tile, carry):
            active, whole, key_base, q_base = tile_state(ids_ref, edge, tile, half, q_rows, rows)

            def run(masked):
                keys = keys_s[tile]
                values = values_s[tile]
                keys_t = keys_t_s[tile]
                scores = [
                    jnp.dot(keys, q_ref[h * HD : (h + 1) * HD, q_cut], preferred_element_type=F32)
                    for h in heads
                ]
                prob_grads = [
                    jnp.dot(values, do_t_s[h * HD : (h + 1) * HD, q_cut], preferred_element_type=F32)
                    for h in heads
                ]
                if masked:
                    allowed = tile_mask(key_base, q_base, start_row)
                probs, d_scores = [], []
                for h in heads:
                    scaled = scores[h] * SCALE2 - lse_s[half, h : h + 1, :]
                    if masked:
                        scaled = jnp.where(allowed, scaled, MASKED_SCORE)
                    prob = jnp.exp2(scaled)
                    probs.append(prob.astype(BF))
                    d_scores.append(
                        (prob * (prob_grads[h] - delta_s[half, h : h + 1, :])).astype(BF)
                    )
                dk = dk_s[tile]
                dv = dv_s[tile]
                for h in heads:
                    dv = dv + jnp.dot(
                        probs[h],
                        do_s[q_cut, h * HD : (h + 1) * HD],
                        preferred_element_type=F32,
                    )
                    dk = dk + jnp.dot(d_scores[h], q_s[h], preferred_element_type=F32)
                    dq_s[h] += jnp.dot(keys_t, d_scores[h], preferred_element_type=F32)
                dk_s[tile] = dk
                dv_s[tile] = dv

            both_ways(active, whole, run)
            return carry

        lax.fori_loop(0, tiles, step, 0)
        for h in heads:
            dq_ref[h * HD : (h + 1) * HD, q_cut] = dq_s[h]
        return carry

    lax.fori_loop(0, HALVES, half_step, 0)
    for slot in range(slots):
        for part in range(per):
            cut = slice(part * KT, (part + 1) * KT)
            tile = slot * per + part
            active = any_active(tile)

            @pl.when(active)
            def _(tile=tile, slot=slot, cut=cut):
                dkv_ref[slot, 0, :, cut] = (dk_s[tile].T * (1.0 / math.sqrt(HD))).astype(BF)
                dkv_ref[slot, 1, :, cut] = dv_s[tile].T.astype(BF)

            @pl.when(jnp.logical_not(active))
            def _(slot=slot, cut=cut):
                dkv_ref[slot, 0, :, cut] = jnp.zeros((HD, KT), BF)
                dkv_ref[slot, 1, :, cut] = jnp.zeros((HD, KT), BF)


def attend_back(ids, lengths, q_t, do_pieces, outs, lses, blocks, kv_heads):
    slots = len(blocks)
    heads = q_t.shape[0] // HD
    group = heads // kv_heads
    rows = q_t.shape[1]
    q_rows = rows // HALVES
    tiles = slots * (rows // KT)
    members = len(do_pieces)
    wide = group * HD
    q_spec = pl.BlockSpec((wide, rows), lambda g: (g, 0))
    return pl.pallas_call(
        functools.partial(attend_back_kernel, slots, group, members),
        grid=(kv_heads,),
        in_specs=[smem_spec(), smem_spec(), q_spec]
        + [pl.BlockSpec((rows // members, wide), lambda g: (0, g))] * members
        + [pl.BlockSpec((wide, q_rows), lambda g: (g, 0))] * HALVES
        + [pl.BlockSpec((1, group, q_rows), lambda g: (g, 0, 0))] * HALVES
        + [pl.BlockSpec((HD, rows), lambda g: (g, 0))] * slots
        + [pl.BlockSpec((HD, rows), lambda g: (kv_heads + g, 0))] * slots,
        out_specs=[q_spec, pl.BlockSpec((slots, 2, HD, rows), lambda g: (0, 0, g, 0))],
        out_shape=[
            jax.ShapeDtypeStruct(q_t.shape, F32),
            jax.ShapeDtypeStruct((slots, 2, kv_heads * HD, rows), BF),
        ],
        scratch_shapes=[
            pltpu.VMEM((tiles, KT, HD), BF),
            pltpu.VMEM((tiles, KT, HD), BF),
            pltpu.VMEM((tiles, HD, KT), BF),
            pltpu.VMEM((tiles, KT, HD), F32),
            pltpu.VMEM((tiles, KT, HD), F32),
            pltpu.VMEM((group, q_rows, HD), BF),
            pltpu.VMEM((rows, wide), BF),
            pltpu.VMEM((wide, rows), BF),
            pltpu.VMEM((group, HD, q_rows), F32),
            pltpu.VMEM((HALVES, group, q_rows), F32),
            pltpu.VMEM((HALVES, group, q_rows), F32),
        ],
        name="attend_back",
        cost_estimate=cost(
            40 * heads * rows * rows * HD, 16 * rows * heads * HD, heads * rows * rows * 4
        ),
    )(ids, lengths, q_t, *do_pieces, *outs, *lses, *blocks, *blocks)


def weight_copies(members, ids_ref, weights, held, sems, distance):
    size = held.shape[0] // (2 * members)
    copies = []
    for other in range(2):
        index = 2 * distance + other
        source = pl.multiple_of((ids_ref[0] ^ distance) * size, size)
        at = pl.multiple_of(index * size, size)
        copy = pltpu.make_async_copy(
            weights[other].at[pl.ds(source, size), :], held.at[pl.ds(at, size), :], sems.at[index]
        )
        copies.append((copy, at, pl.multiple_of((ids_ref[1] ^ other) * size, size)))
    return copies


def project(members, ids_ref, x_ref, gain_ref, mixes, weights, hidden_ref, normed_ref, scratch):
    held, left, sems = scratch
    size = held.shape[0] // (2 * members)
    for distance in range(members):
        for copy, _, _ in weight_copies(members, ids_ref, weights, held, sems, distance):
            copy.start()
    for distance in range(members):
        for other in range(2):
            at = (2 * distance + other) * size
            first = pl.multiple_of((ids_ref[1] ^ other) * size, size)
            left[at : at + size, :] = mixes[distance][pl.ds(first, size), :]
    hidden_ref[...] = x_ref[...].astype(F32)

    def add(distance, carry):
        for copy, _, _ in weight_copies(members, ids_ref, weights, held, sems, distance):
            copy.wait()
        at = pl.ds(pl.multiple_of(2 * distance * size, size), 2 * size)
        hidden_ref[...] += dims(left[at, :], held[at, :], 0, 0)
        return carry

    lax.fori_loop(0, members, add, 0)
    rows = hidden_ref.shape[0]
    step = min(64, rows)

    def norm(index, carry):
        at = pl.ds(pl.multiple_of(index * step, step), step)
        hidden = hidden_ref[at, :]
        normed_ref[at, :] = (hidden * rms_scale(hidden) * gain_ref[...]).astype(BF)
        return carry

    lax.fori_loop(0, rows // step, norm, 0)


def project_scratch(inner, width, half_rows, members):
    return [
        pltpu.VMEM((inner, width), BF),
        pltpu.VMEM((inner, half_rows), BF),
        pltpu.SemaphoreType.DMA((2 * members,)),
    ]


def attn_out_kernel(members, ids_ref, x_ref, gain_ref, *refs):
    mixes, weights, refs = refs[:members], refs[members : members + 2], refs[members + 2 :]
    hidden_ref, normed_ref = refs[:2]
    project(members, ids_ref, x_ref, gain_ref, mixes, weights, hidden_ref, normed_ref, refs[2:])


def attn_out(half, ids, tokens, gain, mixes, weights):
    rows, width = tokens.shape
    half_rows = rows // HALVES
    members = len(mixes)
    inner = 2 * weights[0].shape[0]
    return pl.pallas_call(
        functools.partial(attn_out_kernel, members),
        grid=(1,),
        in_specs=[
            smem_spec(),
            pl.BlockSpec((half_rows, width), lambda i: (half, 0)),
            vmem_spec(),
        ]
        + [vmem_spec()] * members
        + [any_spec()] * len(weights),
        out_specs=[vmem_spec()] * 2,
        out_shape=[
            jax.ShapeDtypeStruct((half_rows, width), F32),
            jax.ShapeDtypeStruct((half_rows, width), BF),
        ],
        scratch_shapes=project_scratch(inner, width, half_rows, members),
        name="attn_out",
        cost_estimate=cost(
            2 * half_rows * inner * width, 2 * inner * width + 12 * half_rows * width
        ),
    )(ids, tokens, gain, *mixes, *weights)


def row_sum(refs):
    total = refs[0][...].astype(F32)
    for ref in refs[1:]:
        total = total + ref[...].astype(F32)
    return total


def norm_back(grad_normed, gain, values, inverse):
    scaled = grad_normed * gain
    return inverse * scaled - values * inverse**3 * jnp.mean(
        scaled * values, axis=-1, keepdims=True
    )


def pick_half(members, ids_ref, refs, at):
    per = members // HALVES
    value = refs[0][at, :]
    for half in range(1, HALVES):
        value = jnp.where(ids_ref[0] // per == half, refs[half][at, :], value)
    return value


def norm_two_back_kernel(members, ids_ref, lengths_ref, *refs):
    hiddens, (cot_ref, gain_ref), refs = refs[:HALVES], refs[HALVES : HALVES + 2], refs[HALVES + 2 :]
    pieces, refs = refs[:members], refs[members:]
    weights, refs = refs[:2], refs[2:]
    refs = refs[members - 1 :]
    sum_ref, low_ref, part_ref = refs[:3]
    d_mixed, refs = refs[3 : 3 + members], refs[3 + members :]
    sent, (held, made, sems) = refs[:-3], refs[-3:]
    for distance in range(members):
        for copy, _, _ in weight_copies(members, ids_ref, weights, held, sems, distance):
            copy.start()
    shard = low_ref.shape[0]
    step = min(32, shard)
    part_ref[...] = jnp.zeros_like(part_ref)

    def rows_at(index, carry):
        at = pl.ds(pl.multiple_of(index * step, step), step)
        grad = row_sum([r.at[at, :] for r in pieces])
        hidden = pick_half(members, ids_ref, hiddens, at)
        inverse = rms_scale(hidden)
        part_ref[...] += jnp.sum(grad * hidden * inverse, axis=0, keepdims=True)
        total = cot_ref[at, :].astype(F32) + norm_back(grad, gain_ref[...], hidden, inverse)
        sum_ref[at, :] = total
        low = total.astype(BF)
        low_ref[at, :] = low
        for ref in sent:
            ref[at, :] = low
        return carry

    lax.fori_loop(0, shard // step, rows_at, 0)
    begin = (ids_ref[2] * members + ids_ref[0]) * shard
    keep = window(lengths_ref, begin + lax.broadcasted_iota(jnp.int32, (shard, 1), 0))[1]
    size = held.shape[0] // (2 * members)

    def heads_of(distance, carry):
        for copy, at, first in weight_copies(members, ids_ref, weights, held, sems, distance):
            copy.wait()
            out = dims(low_ref[...], held[pl.ds(at, size), :], 1, 1)
            made[distance, :, pl.ds(first, size)] = jnp.where(keep, out, 0.0).astype(BF)
        return carry

    lax.fori_loop(0, members, heads_of, 0)
    for distance, ref in enumerate(d_mixed):
        ref[...] = made[distance]


def norm_two_back(ids, lengths, hiddens, cotangent, gain, pieces, weights, travel):
    members = len(pieces)
    shard, width = pieces[0].shape
    inner = sum(w.shape[0] for w in weights)
    per = members // HALVES
    mine = pl.BlockSpec((shard, width), lambda i, ids, lengths: (ids[0], 0))
    mine_half = pl.BlockSpec((shard, width), lambda i, ids, lengths: (ids[0] % per, 0))
    whole = pl.BlockSpec((shard, width), lambda i, ids, lengths: (0, 0))
    line = pl.BlockSpec((1, width), lambda i, ids, lengths: (0, 0))
    head_spec = pl.BlockSpec((shard, inner // members), lambda i, ids, lengths: (0, 0))
    return pl.pallas_call(
        functools.partial(norm_two_back_kernel, members),
        grid_spec=pltpu.PrefetchScalarGridSpec(
            num_scalar_prefetch=2,
            grid=(1,),
            in_specs=[mine_half] * HALVES
            + [mine, line]
            + [whole] * members
            + [any_spec()] * (len(weights) + len(travel)),
            out_specs=[whole, whole, line] + [head_spec] * members + [whole] * len(travel),
            scratch_shapes=[
                pltpu.VMEM((inner, width), BF),
                pltpu.VMEM((members, shard, inner // members), BF),
                pltpu.SemaphoreType.DMA((2 * members,)),
            ],
        ),
        out_shape=[
            jax.ShapeDtypeStruct((shard, width), F32),
            jax.ShapeDtypeStruct((shard, width), BF),
            jax.ShapeDtypeStruct((1, width), F32),
        ]
        + [jax.ShapeDtypeStruct((shard, inner // members), BF)] * members
        + [jax.ShapeDtypeStruct(t.shape, BF) for t in travel],
        input_output_aliases={
            4 + HALVES + members + len(weights) + i: 3 + members + i for i in range(len(travel))
        },
        name="norm_two_back",
        cost_estimate=cost(2 * shard * inner * width, 2 * inner * width + 24 * shard * width),
    )(ids, lengths, *hiddens, cotangent, gain, *pieces, *weights, *travel)


def last_rows_kernel(members, ids_ref, x_ref, *refs):
    hiddens, (add_ref, gain_ref), refs = refs[:HALVES], refs[HALVES : HALVES + 2], refs[HALVES + 2 :]
    pieces, ffn, (low_ref, part_ref) = refs[:members], refs[members:-2], refs[-2:]
    shard = x_ref.shape[0]
    step = min(32, shard)
    part_ref[...] = jnp.zeros_like(part_ref)

    def rows_at(index, carry):
        first = pl.multiple_of(index * step, step)
        at = pl.ds(first, step)
        grad = row_sum([r.at[at, :] for r in pieces])
        values = x_ref[at, :].astype(F32)
        inverse = rms_scale(values)
        part_ref[...] += jnp.sum(grad * values * inverse, axis=0, keepdims=True)
        low_ref[at, :] = (
            add_ref[at, :] + norm_back(grad, gain_ref[...], values, inverse)
        ).astype(BF)
        hidden = pick_half(members, ids_ref, hiddens, at)
        low_ref[pl.ds(shard + first, step), :] = (
            hidden + row_sum([r.at[at, :] for r in ffn])
        ).astype(BF)
        return carry

    lax.fori_loop(0, shard // step, rows_at, 0)


def last_rows(ids, tokens, hiddens, add, gain, pieces, ffn_pieces):
    shard, width = pieces[0].shape
    per = len(pieces) // HALVES
    mine = pl.BlockSpec((shard, width), lambda i, ids: (ids[0], 0))
    mine_half = pl.BlockSpec((shard, width), lambda i, ids: (ids[0] % per, 0))
    first = pl.BlockSpec((shard, width), lambda i, ids: (0, 0))
    second = pl.BlockSpec((shard, width), lambda i, ids: (1, 0))
    line = pl.BlockSpec((1, width), lambda i, ids: (0, 0))
    both = pl.BlockSpec((2 * shard, width), lambda i, ids: (0, 0))
    return pl.pallas_call(
        functools.partial(last_rows_kernel, len(pieces)),
        grid_spec=pltpu.PrefetchScalarGridSpec(
            num_scalar_prefetch=1,
            grid=(1,),
            in_specs=[mine] + [mine_half] * HALVES + [first, line]
            + [first] * (len(pieces) + 1)
            + [second] * (len(ffn_pieces) - 1),
            out_specs=[both, line],
        ),
        out_shape=[
            jax.ShapeDtypeStruct((2 * shard, width), BF),
            jax.ShapeDtypeStruct((1, width), F32),
        ],
        name="last_rows",
        cost_estimate=cost(30 * shard * width, 32 * shard * width),
    )(ids, tokens, *hiddens, add, gain, *pieces, *ffn_pieces)


def in_order_kernel(shard, outs, ids_ref, *refs):
    pieces, out_refs = refs[:-outs], refs[-outs:]
    for distance, ref in enumerate(pieces):
        at = pl.multiple_of((ids_ref[0] ^ distance) * shard, shard)
        for index, out_ref in enumerate(out_refs):
            out_ref[pl.ds(at, shard), :] = ref[index * shard : (index + 1) * shard, :]


def in_order(ids, pieces, outs):
    width = pieces[0].shape[1]
    shard = pieces[0].shape[0] // outs if outs > 1 else pieces[0].shape[0]
    rows = shard * len(pieces)
    return pl.pallas_call(
        functools.partial(in_order_kernel, shard, outs),
        in_specs=[smem_spec()] + [vmem_spec()] * len(pieces),
        out_specs=[vmem_spec()] * outs,
        out_shape=[jax.ShapeDtypeStruct((rows, width), pieces[0].dtype)] * outs,
        name="token_order",
        cost_estimate=cost(0, 4 * rows * outs * width),
    )(ids, *pieces)


def ffn_kernel(members, ids_ref, x_ref, gain_ref, before_ref, da_ref, wg_ref, wu_ref, *refs):
    mixes, refs = refs[:members], refs[members:]
    weights, refs = refs[:2], refs[2:]
    hidden_ref, normed_ref, act_ref, dg_ref, du_ref, full_s = refs[:6]
    half_rows = before_ref.shape[0]

    @pl.when(pl.program_id(0) == 0)
    def _():
        full_s[:half_rows, :] = before_ref[...]
        project(
            members, ids_ref, x_ref, gain_ref, mixes, weights, hidden_ref, normed_ref, refs[6:]
        )
        full_s[half_rows:, :] = normed_ref[...]

    normed = full_s[...]
    gate = jnp.dot(normed, wg_ref[...], preferred_element_type=F32)
    up = jnp.dot(normed, wu_ref[...], preferred_element_type=F32)
    sig = jax.nn.sigmoid(gate)
    silu = gate * sig
    act_ref[...] = (silu * up).astype(BF)
    d_act = da_ref[...]
    dg_ref[...] = (d_act * up * sig * (1.0 + gate * (1.0 - sig))).astype(BF)
    du_ref[...] = (d_act * silu).astype(BF)


def ffn_forward(ids, tokens, gain, mixes, weights, before, d_act, w_gate, w_up):
    rows, width = tokens.shape
    half_rows = rows // HALVES
    members = len(mixes)
    inner = 2 * weights[0].shape[0]
    units = w_gate.shape[1]
    step = min(512, units)
    tile = pl.BlockSpec((rows, step), lambda j: (0, j))
    weight = pl.BlockSpec((width, step), lambda j: (0, j))
    half_spec = pl.BlockSpec((half_rows, width), lambda j: (0, 0))
    return pl.pallas_call(
        functools.partial(ffn_kernel, members),
        grid=(units // step,),
        in_specs=[
            smem_spec(),
            pl.BlockSpec((half_rows, width), lambda j: (HALVES - 1, 0)),
            pl.BlockSpec((1, width), lambda j: (0, 0)),
            half_spec,
            tile,
            weight,
            weight,
        ]
        + [pl.BlockSpec(m.shape, lambda j: (0, 0)) for m in mixes]
        + [any_spec()] * len(weights),
        out_specs=[half_spec, half_spec, tile, tile, tile],
        out_shape=[
            jax.ShapeDtypeStruct((half_rows, width), F32),
            jax.ShapeDtypeStruct((half_rows, width), BF),
        ]
        + [jax.ShapeDtypeStruct((rows, units), BF)] * 3,
        scratch_shapes=[pltpu.VMEM((rows, width), BF)]
        + project_scratch(inner, width, half_rows, members),
        name="gate_up",
        cost_estimate=cost(
            4 * rows * width * units + 2 * half_rows * inner * width,
            4 * width * units + 2 * rows * width + 10 * rows * units + 2 * inner * width,
            rows * units,
        ),
    )(ids, tokens, gain, before, d_act, w_gate, w_up, *mixes, *weights)


def store_by_distance(ids_ref, out_refs, held, value):
    shard = value.shape[0] // len(out_refs)
    held[...] = value.astype(BF)
    for distance, out_ref in enumerate(out_refs):
        at = pl.multiple_of((ids_ref[0] ^ distance) * shard, shard)
        out_ref[...] = held[pl.ds(at, shard), :]


def pair_nt_kernel(ids_ref, a_ref, b_ref, wa_ref, wb_ref, *refs):
    value = dims(a_ref[...], wa_ref[...], 1, 1) + dims(b_ref[...], wb_ref[...], 1, 1)
    store_by_distance(ids_ref, refs[:-1], refs[-1], value)


def pair_nt(members, ids, a, b, w_a, w_b):
    rows, units = a.shape
    width = w_a.shape[0]
    step = min(512, width)
    full = pl.BlockSpec((rows, units), lambda j: (0, 0))
    weight = pl.BlockSpec((step, units), lambda j: (j, 0))
    return pl.pallas_call(
        pair_nt_kernel,
        grid=(width // step,),
        in_specs=[smem_spec(), full, full, weight, weight],
        out_specs=[pl.BlockSpec((rows // members, step), lambda j: (0, j))] * members,
        out_shape=[jax.ShapeDtypeStruct((rows // members, width), BF)] * members,
        scratch_shapes=[pltpu.VMEM((rows, step), BF)],
        name="d_normed_two",
        cost_estimate=cost(
            4 * rows * width * units, 4 * width * units + 4 * rows * units + 2 * rows * width
        ),
    )(ids, a, b, w_a, w_b)


def down_kernel(ids_ref, a_ref, w_ref, *refs):
    value = jnp.dot(a_ref[...], w_ref[...], preferred_element_type=F32)
    store_by_distance(ids_ref, refs[:-1], refs[-1], value)


def down_of(members, ids, act, w_down):
    rows, units = act.shape
    shard = rows // members
    width = w_down.shape[1]
    step = min(512, width)
    return pl.pallas_call(
        down_kernel,
        grid=(width // step,),
        in_specs=[
            smem_spec(),
            pl.BlockSpec((rows, units), lambda j: (0, 0)),
            pl.BlockSpec((units, step), lambda j: (0, j)),
        ],
        out_specs=[pl.BlockSpec((shard, step), lambda j: (0, j))]
        + [pl.BlockSpec((shard, step), lambda j: (1, j))] * (members - 1),
        out_shape=[jax.ShapeDtypeStruct((shard, width), BF)]
        + [jax.ShapeDtypeStruct((2 * shard, width), BF)] * (members - 1),
        scratch_shapes=[pltpu.VMEM((rows, step), BF)],
        name="ffn_down",
        cost_estimate=cost(
            2 * rows * width * units, 2 * width * units + 2 * rows * units + 2 * rows * width
        ),
    )(ids, act, w_down)


def column_specs(rows, part, count):
    return [
        pl.BlockSpec((rows, part), lambda j, ids, k=k: (0, 2 * k + ids[1])) for k in range(count)
    ]


def fill_columns(held, refs, groups):
    count = len(refs) // groups
    rows, part = refs[0].shape
    for index, ref in enumerate(refs):
        top = (index // count) * rows
        left = (index % count) * part
        held[top : top + rows, left : left + part] = ref[...]


def grad_down_kernel(blocks, ids_ref, own_ref, other_ref, *refs):
    cots, (o_ref, held) = refs[: 2 * blocks], refs[2 * blocks :]

    @pl.when(pl.program_id(0) == 0)
    def _():
        fill_columns(held, cots, 2)

    rows = own_ref.shape[0]
    o_ref[...] = (
        dims(own_ref[...], held[:rows, :], 0, 0) + dims(other_ref[...], held[rows:, :], 0, 0)
    ).astype(BF)


def grad_down_of(ids, act, act_other, cot, cot_other, part):
    rows, units = act.shape
    width = cot.shape[1]
    blocks = width // (2 * part)
    step = min(512, units)
    tile = pl.BlockSpec((rows, step), lambda j, ids: (0, j))
    columns = column_specs(rows, part, blocks)
    return pl.pallas_call(
        functools.partial(grad_down_kernel, blocks),
        grid_spec=pltpu.PrefetchScalarGridSpec(
            num_scalar_prefetch=1,
            grid=(units // step,),
            in_specs=[tile, tile] + columns + columns,
            out_specs=pl.BlockSpec((step, width // 2), lambda j, ids: (j, 0)),
            scratch_shapes=[pltpu.VMEM((2 * rows, width // 2), BF)],
        ),
        out_shape=jax.ShapeDtypeStruct((units, width // 2), BF),
        name="grad_down",
        cost_estimate=cost(
            2 * rows * width * units, 4 * rows * units + 2 * rows * width + width * units
        ),
    )(ids, act, act_other, *([cot] * blocks), *([cot_other] * blocks))


def grad_in_kernel(groups, blocks, half, ids_ref, *refs):
    normeds, refs = refs[: groups * blocks], refs[groups * blocks :]
    gates, ups, (o_ref, held) = refs[:2], refs[2:4], refs[4:]

    @pl.when(pl.program_id(0) == 0)
    def _():
        fill_columns(held, normeds, groups)

    rows = gates[0].shape[0]

    def of(pair):
        o_ref[...] = (
            dims(held[:rows, :], pair[0][...], 0, 0) + dims(held[rows:, :], pair[1][...], 0, 0)
        ).astype(BF)

    pl.when(pl.program_id(0) < half)(lambda: of(gates))
    pl.when(pl.program_id(0) >= half)(lambda: of(ups))


def grad_in_of(ids, normeds, d_gates, d_ups, part):
    width = normeds[0].shape[1]
    rows, units = d_gates[0].shape
    blocks = width // (2 * part)
    step = min(512, units)
    half = units // step
    columns = column_specs(normeds[0].shape[0], part, blocks)
    first = pl.BlockSpec((rows, step), lambda j, ids: (0, jnp.minimum(j, half - 1)))
    second = pl.BlockSpec((rows, step), lambda j, ids: (0, jnp.maximum(j - half, 0)))
    return pl.pallas_call(
        functools.partial(grad_in_kernel, len(normeds), blocks, half),
        grid_spec=pltpu.PrefetchScalarGridSpec(
            num_scalar_prefetch=1,
            grid=(2 * half,),
            in_specs=columns * len(normeds) + [first] * 2 + [second] * 2,
            out_specs=pl.BlockSpec((width // 2, step), lambda j, ids: (0, j)),
            scratch_shapes=[pltpu.VMEM((2 * rows, width // 2), BF)],
        ),
        out_shape=jax.ShapeDtypeStruct((width // 2, 2 * units), BF),
        name="grad_gate_up",
        cost_estimate=cost(
            4 * rows * width * units, 8 * rows * units + 2 * rows * width + 2 * width * units
        ),
    )(ids, *[n for n in normeds for _ in range(blocks)], *d_gates, *d_ups)


def grad_proj_kernel(lefts, ids_ref, *refs):
    own, other = refs[:lefts], refs[lefts : 2 * lefts]
    right_ref, right_other_ref, o_ref = refs[2 * lefts :]
    at = 0
    rows = right_ref.shape[0]
    part = rows // lefts
    total = 0.0
    for group, right in ((own, right_ref), (other, right_other_ref)):
        for index, left in enumerate(group):
            total = total + jnp.dot(
                left[...],
                right[index * part : (index + 1) * part, :],
                preferred_element_type=F32,
            )
    o_ref[...] = total.astype(BF)


def grad_proj_of(ids, lefts, lefts_other, right, right_other, part, name):
    inner = lefts[0].shape[0]
    rows, width = right.shape
    blocks = width // (2 * part)
    left_spec = pl.BlockSpec(lefts[0].shape, lambda k, ids: (0, 0))
    right_spec = pl.BlockSpec((rows, part), lambda k, ids: (0, 2 * k + ids[1]))
    return pl.pallas_call(
        functools.partial(grad_proj_kernel, len(lefts)),
        grid_spec=pltpu.PrefetchScalarGridSpec(
            num_scalar_prefetch=1,
            grid=(blocks,),
            in_specs=[left_spec] * (2 * len(lefts)) + [right_spec] * 2,
            out_specs=pl.BlockSpec((inner, part), lambda k, ids: (0, k)),
        ),
        out_shape=jax.ShapeDtypeStruct((inner, width // 2), BF),
        name=name,
        cost_estimate=cost(
            2 * rows * width * inner, 4 * inner * rows + 2 * rows * width + inner * width
        ),
    )(ids, *lefts, *lefts_other, right, right_other)


def finish_kernel(in_ref, out_ref, *refs):
    at = out_ref.shape[0]
    out_ref[...] = in_ref[:at, :].astype(F32)
    for ref in refs:
        count = ref.shape[1]
        ref[...] = in_ref[at : at + count, :].astype(F32).T
        at += count


def finish(grads, sizes):
    part = grads.shape[1]
    return pl.pallas_call(
        finish_kernel,
        in_specs=[vmem_spec()],
        out_specs=[vmem_spec()] * len(sizes),
        out_shape=[jax.ShapeDtypeStruct((sizes[0], part), F32)]
        + [jax.ShapeDtypeStruct((part, size), F32) for size in sizes[1:]],
        name="finish",
        cost_estimate=cost(0, 6 * sum(sizes) * part),
    )(grads)


def together(*values):
    return lax.optimization_barrier(values)


def body(
    tokens,
    attn_gain,
    w_query,
    w_key,
    w_value,
    w_out,
    ffn_gain,
    w_gate,
    w_up,
    w_down,
    doc_lengths,
    cotangent,
):
    rows, width = tokens.shape
    wide = lax.axis_size("wide")
    narrow = lax.axis_size("narrow")
    me_wide = lax.axis_index("wide")
    me = lax.axis_index("narrow")
    core = me_wide % 2
    kv_heads = w_key.shape[1] // HD
    half_rows = rows // HALVES
    shard = rows // narrow
    part = width // wide
    hops = wide // 4
    units = w_gate.shape[1]
    q_width = w_query.shape[1]
    k_width = w_key.shape[1]
    chip_groups = [list(range(0, wide, 2)), list(range(1, wide, 2))]
    ids = jnp.stack([me, core, me_wide]).astype(jnp.int32)

    def other_core(value):
        return lax.ppermute(value, "wide", [(i, i ^ 1) for i in range(wide)])

    def chips_up(value, hop):
        return lax.ppermute(value, "wide", [(i, i + 2 * hop) for i in range(wide - 2 * hop)])

    def chips_down(value, hop):
        return lax.ppermute(value, "wide", [(i + 2 * hop, i) for i in range(wide - 2 * hop)])

    def swap(value, distance):
        return lax.ppermute(value, "narrow", [(i, i ^ distance) for i in range(narrow)])

    def rows_of(value, distance):
        return lax.dynamic_slice_in_dim(value, (me ^ distance) * shard, shard, 0)

    def exchange(pieces):
        return [pieces[0]] + [swap(pieces[d], d) for d in range(1, narrow)]

    def gather_near(value):
        return [value] + [swap(value, d) for d in range(1, narrow)]

    def scatter(value, dimension):
        return lax.psum_scatter(
            value,
            "wide",
            scatter_dimension=dimension,
            axis_index_groups=chip_groups,
            tiled=True,
        )

    gain_one = attn_gain.astype(F32)[None, :]
    gain_two = ffn_gain.astype(F32)[None, :]

    w_half = w_out.shape[0] // 2
    w_mine = lax.dynamic_slice_in_dim(w_out, core * w_half, w_half, 0)
    w_all = lax.all_gather(w_mine, "narrow", axis=0, tiled=True)

    base = me_wide * rows
    index = base + jnp.arange(rows, dtype=jnp.int32)
    start = doc_offsets(doc_lengths, index)
    angle = jnp.asarray(inverse_frequencies(HD))[:, None] * (index - start).astype(F32)[None, :]
    cosine = jnp.cos(angle)
    sine = jnp.sin(angle)
    normed, packed = keys_values(tokens, gain_one, w_key, w_value, cosine, sine)
    ups = [chips_up(packed, hop) for hop in range(1, hops + 1)]
    beside = other_core(packed)
    query_t = rotate_t(dims(w_query, normed, 0, 1), cosine, sine).astype(BF)
    d_act = dims(cotangent, w_down, 1, 1)
    cot_other = other_core(cotangent)
    normed_other = other_core(normed)
    ups, query_t, d_act = together(ups, query_t, d_act)
    blocks = [packed, beside]
    for near in ups:
        blocks += [near, other_core(near)]

    outs, mixes, lses, gathered = [], [], [], []
    for half in range(HALVES):
        out, mixed, lse = attend(half, ids, doc_lengths, query_t, blocks, kv_heads)
        if gathered:
            mixed_others = [other_core(mixes[0])]
            gathered[-1], mixed, w_all, normed_other, mixed_others = together(
                gathered[-1], mixed, w_all, normed_other, mixed_others
            )
            out_weights = [w_all, other_core(w_all)]
        outs.append(out)
        mixes.append(mixed)
        lses.append(lse)
        query_t, mixed = together(query_t, mixed)
        gathered.append(gather_near(mixed))
    hidden_first, normed_first = attn_out(0, ids, tokens, gain_two, gathered[0], out_weights)
    gathered[1], normed_first = together(gathered[1], normed_first)

    hidden_last, normed_last, act, d_gate, d_up = ffn_forward(
        ids, tokens, gain_two, gathered[1], out_weights, normed_first, d_act, w_gate, w_up
    )
    hiddens = [hidden_first, hidden_last]
    act_other = other_core(act)
    d_gates = [d_gate, other_core(d_gate)]
    d_ups = [d_up, other_core(d_up)]
    normed_twos = [normed_first, normed_last]
    normed_others = [other_core(n) for n in normed_twos]
    grad_down = grad_down_of(ids, act, act_other, cotangent, cot_other, part)
    d_gate_then, _ = together(d_gate, grad_down)
    grad_down = scatter(grad_down, 1)
    d_norm_pieces = pair_nt(narrow, ids, d_gate_then, d_up, w_gate, w_up)
    mixed_others += [other_core(m) for m in mixes[1:]]
    act_then, d_norm_pieces, d_gates, d_ups, normed_others, mixed_others = together(
        act, d_norm_pieces, d_gates, d_ups, normed_others, mixed_others
    )
    d_norm_pieces = exchange(d_norm_pieces)
    ffn_pieces = down_of(narrow, ids, act_then, w_down)
    d_norm_pieces[1], ffn_pieces, normed_twos = together(
        d_norm_pieces[1], ffn_pieces, normed_twos
    )
    grad_gate_up = grad_in_of(ids, normed_twos + normed_others, d_gates, d_ups, part)
    d_norm_pieces, ffn_pieces, _ = together(d_norm_pieces, ffn_pieces, grad_gate_up)

    d_hidden, d_hidden_b, gain_two_part, *made = norm_two_back(
        ids,
        doc_lengths,
        hiddens,
        cotangent,
        gain_two,
        d_norm_pieces,
        out_weights,
        ffn_pieces[1:],
    )
    d_mixed, travel = made[:narrow], made[narrow:]
    grad_gate_up, _ = together(grad_gate_up, d_hidden_b)
    grad_gate_up = scatter(grad_gate_up, 0)
    d_mixed = exchange(d_mixed)
    d_mixed, travel = together(d_mixed, travel)
    travel = [swap(value, d + 1) for d, value in enumerate(travel)]

    d_query_r, d_blocks = attend_back(
        ids, doc_lengths, query_t, d_mixed, outs, lses, blocks, kv_heads
    )
    d_query_r, d_blocks, travel[0] = together(d_query_r, d_blocks, travel[0])
    d_blocks = d_blocks.reshape(2 * (hops + 1), 2 * k_width, rows)
    for_other = other_core(d_blocks[1::2])
    both = [
        d_blocks[2 * hop].astype(F32) + for_other[hop].astype(F32) for hop in range(hops + 1)
    ]
    down = chips_down(both[hops].astype(BF), 1)
    for hop in range(hops - 1, 0, -1):
        down = chips_down((both[hop] + down.astype(F32)).astype(BF), 1)
    d_kv = both[0]

    d_query = rotate_t(d_query_r * (1.0 / math.sqrt(HD)), cosine, -sine).astype(BF)
    (d_hidden_full,) = in_order(ids, [d_hidden_b, *travel], 1)
    grad_query = grad_proj_of(
        ids, [d_query], [other_core(d_query)], normed, normed_other, part, "grad_query"
    )
    grad_out = grad_proj_of(
        ids, mixes, mixed_others, d_hidden_full, other_core(d_hidden_full), part, "grad_out"
    )
    down, grad_out, grad_query, grad_down = together(down, grad_out, grad_query, grad_down)
    d_kv = d_kv + down.astype(F32)
    d_keys = rotate_t(d_kv[:k_width], cosine, -sine).astype(BF)
    d_values = d_kv[k_width:].astype(BF)
    norm_one_part = (
        dims(d_query, w_query, 0, 1) + dims(d_keys, w_key, 0, 1) + dims(d_values, w_value, 0, 1)
    ).astype(BF)
    norm_one_pieces = [rows_of(norm_one_part, d) for d in range(narrow)]
    d_pair = jnp.concatenate([d_keys, d_values], axis=0)
    d_pair, norm_one_pieces = together(d_pair, norm_one_pieces)
    norm_one_pieces = exchange(norm_one_pieces)
    grad_pair = grad_proj_of(
        ids, [d_pair], [other_core(d_pair)], normed, normed_other, part, "grad_key_value"
    )
    grads = jnp.concatenate([grad_out, grad_query, grad_pair], axis=0)
    norm_one_pieces, grads = together(norm_one_pieces, grads)
    last, gain_one_part = last_rows(
        ids,
        tokens,
        hiddens,
        d_hidden,
        gain_one,
        norm_one_pieces,
        [ffn_pieces[0], *travel],
    )
    last_pieces = gather_near(last)
    gains = jnp.concatenate([gain_one_part, gain_two_part], axis=0)
    grads, grad_gate_up, last_pieces[1:-1] = together(grads, grad_gate_up, last_pieces[1:-1])
    grads = scatter(grads, 1)
    input_grad, output = in_order(ids, last_pieces, 2)
    gains, output = together(gains, output)
    gains = sum(gather_near(gains)[1:], gains)
    gains = gains + other_core(gains)
    gain_sum = 0.0
    for hop in range(wide // 2):
        target = lax.rem(me_wide + 2 * hop, wide)
        piece = lax.dynamic_slice_in_dim(gains, target * part, part, 1)
        if hop:
            piece = lax.ppermute(piece, "wide", [(i, (i + 2 * hop) % wide) for i in range(wide)])
        gain_sum = gain_sum + piece
    gains = gain_sum
    grad_gate = grad_gate_up[:, :units].astype(F32)
    grad_up = grad_gate_up[:, units:].astype(F32)
    grad_down = grad_down.astype(F32)
    grads, gains, input_grad, output, grad_gate, grad_up, grad_down = together(
        grads, gains, input_grad, output, grad_gate, grad_up, grad_down
    )
    grad_out, grad_query, grad_key, grad_value = finish(
        grads, (w_out.shape[0], q_width, k_width, k_width)
    )
    return (
        output,
        input_grad,
        gains[0],
        grad_query,
        grad_key,
        grad_value,
        grad_out,
        gains[1],
        grad_gate,
        grad_up,
        grad_down,
    )


def solution(mesh):
    in_specs = (
        P("wide", None),
        P(),
        P(None, "narrow"),
        P(None, "narrow"),
        P(None, "narrow"),
        P("narrow", None),
        P(),
        P(None, "narrow"),
        P(None, "narrow"),
        P("narrow", None),
        P(),
        P("wide", None),
    )
    out_specs = (
        P("wide", None),
        P("wide", None),
        P("wide"),
        P("wide", "narrow"),
        P("wide", "narrow"),
        P("wide", "narrow"),
        P("narrow", "wide"),
        P("wide"),
        P("wide", "narrow"),
        P("wide", "narrow"),
        P("narrow", "wide"),
    )
    return jax.shard_map(body, mesh=mesh, in_specs=in_specs, out_specs=out_specs, check_vma=False)
```

```python
import functools
import math

import jax
import jax.numpy as jnp
import numpy as np
from jax import lax
from jax.experimental import pallas as pl
from jax.experimental.pallas import tpu as pltpu
from jax.sharding import PartitionSpec as P

HD = 64
DOCS = 12
NORM_EPS = 1e-05
MASKED_SCORE = -1e30
LOG2E = math.log2(math.e)
SCALE2 = LOG2E / math.sqrt(HD)
KT = 256
HALVES = 2
BF = jnp.bfloat16
F32 = jnp.float32


def inverse_frequencies(head_size):
    frequency = 1.0 / 500000.0 ** (np.arange(0, head_size, 2) / head_size)
    wavelength = 2 * math.pi / frequency
    smoothing = (8192.0 / wavelength - 1.0) / 3.0
    scaled_freq = np.where(wavelength > 8192.0, frequency / 32.0, frequency)
    middle_band = (wavelength <= 8192.0) & (wavelength >= 2048.0)
    scaled_freq = np.where(
        middle_band, (1 - smoothing) * frequency / 32.0 + smoothing * frequency, scaled_freq
    )
    return scaled_freq.astype(np.float32)


def doc_offsets(doc_lengths, index):
    ends = jnp.cumsum(doc_lengths)
    passed = (index[None, :] >= ends[:, None]).astype(jnp.int32)
    return jnp.sum(passed * doc_lengths[:, None], axis=0)


def rotate_t(values, cosine, sine):
    heads = values.shape[0] // HD
    shaped = values.reshape(heads, 2, HD // 2, values.shape[1])
    first = shaped[:, 0]
    second = shaped[:, 1]
    return jnp.stack(
        [first * cosine - second * sine, second * cosine + first * sine], axis=1
    ).reshape(values.shape)


def dims(left, right, a, b):
    return lax.dot_general(left, right, (((a,), (b,)), ((), ())), preferred_element_type=F32)


def vmem_spec():
    return pl.BlockSpec(memory_space=pltpu.VMEM)


def smem_spec():
    return pl.BlockSpec(memory_space=pltpu.SMEM)


def any_spec():
    return pl.BlockSpec(memory_space=pl.ANY)


def cost(flops, moved, exps=0):
    return pl.CostEstimate(flops=int(flops), transcendentals=int(exps), bytes_accessed=int(moved))


def rms_scale(values):
    return lax.rsqrt(jnp.mean(values * values, axis=-1, keepdims=True) + NORM_EPS)


def keys_values_kernel(x_ref, gain_ref, wk_ref, wv_ref, cos_ref, sin_ref, normed_ref, packed_ref):
    rows = x_ref.shape[0]
    step = min(128, rows)
    for at in range(0, rows, step):
        values = x_ref[at : at + step, :].astype(F32)
        normed_ref[at : at + step, :] = (values * rms_scale(values) * gain_ref[...]).astype(BF)
    normed = normed_ref[...]
    keys = jnp.dot(normed, wk_ref[...], preferred_element_type=F32).T
    width = keys.shape[0]
    half = HD // 2
    for head in range(width // HD):
        first = keys[head * HD : head * HD + half]
        second = keys[head * HD + half : (head + 1) * HD]
        cosine, sine = cos_ref[...], sin_ref[...]
        packed_ref[head * HD : head * HD + half, :] = (first * cosine - second * sine).astype(BF)
        packed_ref[head * HD + half : (head + 1) * HD, :] = (
            second * cosine + first * sine
        ).astype(BF)
    packed_ref[width:, :] = jnp.dot(normed, wv_ref[...], preferred_element_type=F32).T.astype(BF)


def keys_values(tokens, gain, w_key, w_value, cosine, sine):
    rows, width = tokens.shape
    kv = w_key.shape[1]
    return pl.pallas_call(
        keys_values_kernel,
        in_specs=[vmem_spec()] * 6,
        out_specs=[vmem_spec()] * 2,
        out_shape=[
            jax.ShapeDtypeStruct((rows, width), BF),
            jax.ShapeDtypeStruct((2 * kv, rows), BF),
        ],
        name="keys_values",
        cost_estimate=cost(4 * rows * width * kv, 4 * rows * width + 4 * width * kv),
    )(tokens, gain, w_key, w_value, cosine, sine)


def window(lengths_ref, index):
    end = lengths_ref[0]
    start = jnp.zeros_like(index)
    for doc in range(1, DOCS):
        start = jnp.where(index >= end, end, start)
        if doc == DOCS - 1:
            last = end
        end = end + lengths_ref[doc]
    valid = index < last
    return jnp.where(valid, start, index), valid


def tile_state(ids_ref, edge, tile, half, q_rows, rows):
    me_wide = ids_ref[2]
    slot = tile // (rows // KT)
    block = (me_wide // 2 - slot // 2) * 2 + (ids_ref[1] ^ (slot % 2))
    key_base = block * rows + (tile % (rows // KT)) * KT
    q_base = me_wide * rows + half * q_rows
    low, high = edge
    active = (key_base <= q_base + q_rows - 1) & (key_base + KT > low)
    whole = (key_base + KT - 1 <= q_base) & (key_base >= high)
    return active, active & whole, key_base, q_base


def window_edge(ids_ref, lengths_ref, rows, half):
    base = ids_ref[2] * rows
    step = rows // HALVES
    return (
        window(lengths_ref, base + half * step)[0],
        window(lengths_ref, base + (half + 1) * step - 1)[0],
    )


def query_row(ids_ref, rows, half):
    step = rows // HALVES
    return ids_ref[2] * rows + half * step + lax.broadcasted_iota(jnp.int32, (1, step), 1)


def tile_mask(key_base, q_base, start_row):
    q_rows = start_row.shape[1]
    keys = key_base + lax.broadcasted_iota(jnp.int32, (KT, q_rows), 0)
    queries = q_base + lax.broadcasted_iota(jnp.int32, (KT, q_rows), 1)
    return (keys <= queries) & (keys >= start_row)


def both_ways(active, whole, run):
    pl.when(whole)(lambda: run(False))
    pl.when(active & jnp.logical_not(whole))(lambda: run(True))


def attend_kernel(slots, group, half, ids_ref, lengths_ref, q_ref, *refs):
    k_refs = refs[:slots]
    v_refs = refs[slots : 2 * slots]
    o_ref, mixed_ref, lse_ref, keys_s, values_s, top_s, sum_s, acc_s = refs[2 * slots :]
    q_rows = q_ref.shape[1]
    rows = k_refs[0].shape[1]
    per = rows // KT
    tiles = slots * per
    edge = window_edge(ids_ref, lengths_ref, rows, half)
    start_row, valid_row = window(lengths_ref, query_row(ids_ref, rows, half))
    for slot in range(slots):
        for part in range(per):
            tile = slot * per + part
            cut = slice(part * KT, (part + 1) * KT)

            @pl.when(tile_state(ids_ref, edge, tile, half, q_rows, rows)[0])
            def _(tile=tile, slot=slot, cut=cut):
                keys_s[tile] = k_refs[slot][:, cut].T
                values_s[tile] = v_refs[slot][:, cut]

    top_s[...] = jnp.full_like(top_s, MASKED_SCORE)
    sum_s[...] = jnp.zeros_like(sum_s)
    acc_s[...] = jnp.zeros_like(acc_s)
    heads = range(group)

    def step(tile, carry):
        active, whole, key_base, q_base = tile_state(ids_ref, edge, tile, half, q_rows, rows)

        def run(masked):
            keys = keys_s[tile]
            values = values_s[tile]
            scores = [
                jnp.dot(keys, q_ref[h * HD : (h + 1) * HD, :], preferred_element_type=F32)
                for h in heads
            ]
            if masked:
                allowed = tile_mask(key_base, q_base, start_row)
                scores = [jnp.where(allowed, s, MASKED_SCORE) for s in scores]
            tops, decays = [], []
            for h in heads:
                old = top_s[h : h + 1, :]
                new = jnp.maximum(old, jnp.max(scores[h], axis=0, keepdims=True))
                top_s[h : h + 1, :] = new
                tops.append(new)
                decays.append(jnp.exp2((old - new) * SCALE2))
            for h in heads:
                weight = jnp.exp2((scores[h] - tops[h]) * SCALE2)
                sum_s[h : h + 1, :] = sum_s[h : h + 1, :] * decays[h] + jnp.sum(
                    weight, axis=0, keepdims=True
                )
                acc_s[h] = acc_s[h] * decays[h] + jnp.dot(
                    values, weight.astype(BF), preferred_element_type=F32
                )

        both_ways(active, whole, run)
        return carry

    lax.fori_loop(0, tiles, step, 0)
    for h in heads:
        h_cut = slice(h * HD, (h + 1) * HD)
        total = sum_s[h : h + 1, :]
        out = acc_s[h] / total
        o_ref[h_cut, :] = out
        mixed_ref[h_cut, :] = jnp.where(valid_row, out, 0.0).astype(BF)
        lse_ref[0, h : h + 1, :] = top_s[h : h + 1, :] * SCALE2 + jnp.log(total) * LOG2E


def attend(half, ids, lengths, q_t, blocks, kv_heads):
    slots = len(blocks)
    heads = q_t.shape[0] // HD
    group = heads // kv_heads
    rows = q_t.shape[1]
    q_rows = rows // HALVES
    tiles = slots * (rows // KT)
    out_spec = pl.BlockSpec((group * HD, q_rows), lambda g: (g, 0))
    return pl.pallas_call(
        functools.partial(attend_kernel, slots, group, half),
        grid=(kv_heads,),
        in_specs=[
            smem_spec(),
            smem_spec(),
            pl.BlockSpec((group * HD, q_rows), lambda g: (g, half)),
        ]
        + [pl.BlockSpec((HD, rows), lambda g: (g, 0))] * slots
        + [pl.BlockSpec((HD, rows), lambda g: (kv_heads + g, 0))] * slots,
        out_specs=[out_spec, out_spec, pl.BlockSpec((1, group, q_rows), lambda g: (g, 0, 0))],
        out_shape=[
            jax.ShapeDtypeStruct((heads * HD, q_rows), F32),
            jax.ShapeDtypeStruct((heads * HD, q_rows), BF),
            jax.ShapeDtypeStruct((kv_heads, group, q_rows), F32),
        ],
        scratch_shapes=[
            pltpu.VMEM((tiles, KT, HD), BF),
            pltpu.VMEM((tiles, HD, KT), BF),
            pltpu.VMEM((group, q_rows), F32),
            pltpu.VMEM((group, q_rows), F32),
            pltpu.VMEM((group, HD, q_rows), F32),
        ],
        name="attend",
        cost_estimate=cost(
            16 * heads * q_rows * rows * HD, 8 * rows * heads * HD, heads * q_rows * rows * 4
        ),
    )(ids, lengths, q_t, *blocks, *blocks)


def attend_back_kernel(slots, group, members, ids_ref, lengths_ref, q_ref, *refs):
    do_refs, refs = refs[:members], refs[members:]
    o_refs, lse_refs, refs = refs[:HALVES], refs[HALVES : 2 * HALVES], refs[2 * HALVES :]
    k_refs, v_refs, refs = refs[:slots], refs[slots : 2 * slots], refs[2 * slots :]
    dq_ref, dkv_ref = refs[:2]
    keys_s, values_s, keys_t_s, dk_s, dv_s, q_s, do_s, do_t_s, dq_s, delta_s, lse_s = refs[2:]
    rows = q_ref.shape[1]
    q_rows = rows // HALVES
    per = rows // KT
    tiles = slots * per
    heads = range(group)
    edges = [window_edge(ids_ref, lengths_ref, rows, half) for half in range(HALVES)]

    def any_active(tile):
        found = tile_state(ids_ref, edges[0], tile, 0, q_rows, rows)[0]
        for half in range(1, HALVES):
            found = found | tile_state(ids_ref, edges[half], tile, half, q_rows, rows)[0]
        return found

    for slot in range(slots):
        for part in range(per):
            tile = slot * per + part
            cut = slice(part * KT, (part + 1) * KT)

            @pl.when(any_active(tile))
            def _(tile=tile, slot=slot, cut=cut):
                keys_s[tile] = k_refs[slot][:, cut].T
                keys_t_s[tile] = k_refs[slot][:, cut]
                values_s[tile] = v_refs[slot][:, cut].T
                dk_s[tile] = jnp.zeros((KT, HD), F32)
                dv_s[tile] = jnp.zeros((KT, HD), F32)

    shard = do_refs[0].shape[0]
    for distance in range(members):
        at = pl.multiple_of((ids_ref[0] ^ distance) * shard, shard)
        do_s[pl.ds(at, shard), :] = do_refs[distance][...]
    do_t_s[...] = do_s[...].T

    for half in range(HALVES):
        for h in heads:
            h_cut = slice(h * HD, (h + 1) * HD)
            do_h = do_t_s[h_cut, half * q_rows : (half + 1) * q_rows].astype(F32)
            delta_s[half, h : h + 1, :] = jnp.sum(
                do_h * o_refs[half][h_cut, :], axis=0, keepdims=True
            )
            lse_s[half, h : h + 1, :] = lse_refs[half][0, h : h + 1, :]

    def half_step(half, carry):
        q_cut = pl.ds(pl.multiple_of(half * q_rows, q_rows), q_rows)
        edge = window_edge(ids_ref, lengths_ref, rows, half)
        for h in heads:
            q_s[h] = q_ref[h * HD : (h + 1) * HD, q_cut].T
        dq_s[...] = jnp.zeros_like(dq_s)
        start_row = window(lengths_ref, query_row(ids_ref, rows, half))[0]

        def step(tile, carry):
            active, whole, key_base, q_base = tile_state(ids_ref, edge, tile, half, q_rows, rows)

            def run(masked):
                keys = keys_s[tile]
                values = values_s[tile]
                keys_t = keys_t_s[tile]
                scores = [
                    jnp.dot(keys, q_ref[h * HD : (h + 1) * HD, q_cut], preferred_element_type=F32)
                    for h in heads
                ]
                prob_grads = [
                    jnp.dot(values, do_t_s[h * HD : (h + 1) * HD, q_cut], preferred_element_type=F32)
                    for h in heads
                ]
                if masked:
                    allowed = tile_mask(key_base, q_base, start_row)
                probs, d_scores = [], []
                for h in heads:
                    scaled = scores[h] * SCALE2 - lse_s[half, h : h + 1, :]
                    if masked:
                        scaled = jnp.where(allowed, scaled, MASKED_SCORE)
                    prob = jnp.exp2(scaled)
                    probs.append(prob.astype(BF))
                    d_scores.append(
                        (prob * (prob_grads[h] - delta_s[half, h : h + 1, :])).astype(BF)
                    )
                dk = dk_s[tile]
                dv = dv_s[tile]
                for h in heads:
                    dv = dv + jnp.dot(
                        probs[h],
                        do_s[q_cut, h * HD : (h + 1) * HD],
                        preferred_element_type=F32,
                    )
                    dk = dk + jnp.dot(d_scores[h], q_s[h], preferred_element_type=F32)
                    dq_s[h] += jnp.dot(keys_t, d_scores[h], preferred_element_type=F32)
                dk_s[tile] = dk
                dv_s[tile] = dv

            both_ways(active, whole, run)
            return carry

        lax.fori_loop(0, tiles, step, 0)
        for h in heads:
            dq_ref[h * HD : (h + 1) * HD, q_cut] = dq_s[h]
        return carry

    lax.fori_loop(0, HALVES, half_step, 0)
    for slot in range(slots):
        for part in range(per):
            cut = slice(part * KT, (part + 1) * KT)
            tile = slot * per + part
            active = any_active(tile)

            @pl.when(active)
            def _(tile=tile, slot=slot, cut=cut):
                dkv_ref[slot, 0, :, cut] = (dk_s[tile].T * (1.0 / math.sqrt(HD))).astype(BF)
                dkv_ref[slot, 1, :, cut] = dv_s[tile].T.astype(BF)

            @pl.when(jnp.logical_not(active))
            def _(slot=slot, cut=cut):
                dkv_ref[slot, 0, :, cut] = jnp.zeros((HD, KT), BF)
                dkv_ref[slot, 1, :, cut] = jnp.zeros((HD, KT), BF)


def attend_back(ids, lengths, q_t, do_pieces, outs, lses, blocks, kv_heads):
    slots = len(blocks)
    heads = q_t.shape[0] // HD
    group = heads // kv_heads
    rows = q_t.shape[1]
    q_rows = rows // HALVES
    tiles = slots * (rows // KT)
    members = len(do_pieces)
    wide = group * HD
    q_spec = pl.BlockSpec((wide, rows), lambda g: (g, 0))
    return pl.pallas_call(
        functools.partial(attend_back_kernel, slots, group, members),
        grid=(kv_heads,),
        in_specs=[smem_spec(), smem_spec(), q_spec]
        + [pl.BlockSpec((rows // members, wide), lambda g: (0, g))] * members
        + [pl.BlockSpec((wide, q_rows), lambda g: (g, 0))] * HALVES
        + [pl.BlockSpec((1, group, q_rows), lambda g: (g, 0, 0))] * HALVES
        + [pl.BlockSpec((HD, rows), lambda g: (g, 0))] * slots
        + [pl.BlockSpec((HD, rows), lambda g: (kv_heads + g, 0))] * slots,
        out_specs=[q_spec, pl.BlockSpec((slots, 2, HD, rows), lambda g: (0, 0, g, 0))],
        out_shape=[
            jax.ShapeDtypeStruct(q_t.shape, F32),
            jax.ShapeDtypeStruct((slots, 2, kv_heads * HD, rows), BF),
        ],
        scratch_shapes=[
            pltpu.VMEM((tiles, KT, HD), BF),
            pltpu.VMEM((tiles, KT, HD), BF),
            pltpu.VMEM((tiles, HD, KT), BF),
            pltpu.VMEM((tiles, KT, HD), F32),
            pltpu.VMEM((tiles, KT, HD), F32),
            pltpu.VMEM((group, q_rows, HD), BF),
            pltpu.VMEM((rows, wide), BF),
            pltpu.VMEM((wide, rows), BF),
            pltpu.VMEM((group, HD, q_rows), F32),
            pltpu.VMEM((HALVES, group, q_rows), F32),
            pltpu.VMEM((HALVES, group, q_rows), F32),
        ],
        name="attend_back",
        cost_estimate=cost(
            40 * heads * rows * rows * HD, 16 * rows * heads * HD, heads * rows * rows * 4
        ),
    )(ids, lengths, q_t, *do_pieces, *outs, *lses, *blocks, *blocks)


def weight_copies(members, ids_ref, weights, held, sems, distance):
    size = held.shape[0] // (2 * members)
    copies = []
    for other in range(2):
        index = 2 * distance + other
        source = pl.multiple_of((ids_ref[0] ^ distance) * size, size)
        at = pl.multiple_of(index * size, size)
        copy = pltpu.make_async_copy(
            weights[other].at[pl.ds(source, size), :], held.at[pl.ds(at, size), :], sems.at[index]
        )
        copies.append((copy, at, pl.multiple_of((ids_ref[1] ^ other) * size, size)))
    return copies


def project(members, ids_ref, x_ref, gain_ref, mixes, weights, hidden_ref, normed_ref, scratch):
    held, left, sems = scratch
    size = held.shape[0] // (2 * members)
    for distance in range(members):
        for copy, _, _ in weight_copies(members, ids_ref, weights, held, sems, distance):
            copy.start()
    for distance in range(members):
        for other in range(2):
            at = (2 * distance + other) * size
            first = pl.multiple_of((ids_ref[1] ^ other) * size, size)
            left[at : at + size, :] = mixes[distance][pl.ds(first, size), :]
    hidden_ref[...] = x_ref[...].astype(F32)

    def add(distance, carry):
        for copy, _, _ in weight_copies(members, ids_ref, weights, held, sems, distance):
            copy.wait()
        at = pl.ds(pl.multiple_of(2 * distance * size, size), 2 * size)
        hidden_ref[...] += dims(left[at, :], held[at, :], 0, 0)
        return carry

    lax.fori_loop(0, members, add, 0)
    rows = hidden_ref.shape[0]
    step = min(64, rows)

    def norm(index, carry):
        at = pl.ds(pl.multiple_of(index * step, step), step)
        hidden = hidden_ref[at, :]
        normed_ref[at, :] = (hidden * rms_scale(hidden) * gain_ref[...]).astype(BF)
        return carry

    lax.fori_loop(0, rows // step, norm, 0)


def project_scratch(inner, width, half_rows, members):
    return [
        pltpu.VMEM((inner, width), BF),
        pltpu.VMEM((inner, half_rows), BF),
        pltpu.SemaphoreType.DMA((2 * members,)),
    ]


def attn_out_kernel(members, ids_ref, x_ref, gain_ref, *refs):
    mixes, weights, refs = refs[:members], refs[members : members + 2], refs[members + 2 :]
    hidden_ref, normed_ref = refs[:2]
    project(members, ids_ref, x_ref, gain_ref, mixes, weights, hidden_ref, normed_ref, refs[2:])


def attn_out(half, ids, tokens, gain, mixes, weights):
    rows, width = tokens.shape
    half_rows = rows // HALVES
    members = len(mixes)
    inner = 2 * weights[0].shape[0]
    return pl.pallas_call(
        functools.partial(attn_out_kernel, members),
        grid=(1,),
        in_specs=[
            smem_spec(),
            pl.BlockSpec((half_rows, width), lambda i: (half, 0)),
            vmem_spec(),
        ]
        + [vmem_spec()] * members
        + [any_spec()] * len(weights),
        out_specs=[vmem_spec()] * 2,
        out_shape=[
            jax.ShapeDtypeStruct((half_rows, width), F32),
            jax.ShapeDtypeStruct((half_rows, width), BF),
        ],
        scratch_shapes=project_scratch(inner, width, half_rows, members),
        name="attn_out",
        cost_estimate=cost(
            2 * half_rows * inner * width, 2 * inner * width + 12 * half_rows * width
        ),
    )(ids, tokens, gain, *mixes, *weights)


def row_sum(refs):
    total = refs[0][...].astype(F32)
    for ref in refs[1:]:
        total = total + ref[...].astype(F32)
    return total


def norm_back(grad_normed, gain, values, inverse):
    scaled = grad_normed * gain
    return inverse * scaled - values * inverse**3 * jnp.mean(
        scaled * values, axis=-1, keepdims=True
    )


def pick_half(members, ids_ref, refs, at):
    per = members // HALVES
    value = refs[0][at, :]
    for half in range(1, HALVES):
        value = jnp.where(ids_ref[0] // per == half, refs[half][at, :], value)
    return value


def norm_two_back_kernel(members, ids_ref, lengths_ref, *refs):
    hiddens, (cot_ref, gain_ref), refs = refs[:HALVES], refs[HALVES : HALVES + 2], refs[HALVES + 2 :]
    pieces, refs = refs[:members], refs[members:]
    weights, refs = refs[:2], refs[2:]
    refs = refs[members - 1 :]
    sum_ref, low_ref, part_ref = refs[:3]
    d_mixed, refs = refs[3 : 3 + members], refs[3 + members :]
    sent, (held, made, sems) = refs[:-3], refs[-3:]
    for distance in range(members):
        for copy, _, _ in weight_copies(members, ids_ref, weights, held, sems, distance):
            copy.start()
    shard = low_ref.shape[0]
    step = min(32, shard)
    part_ref[...] = jnp.zeros_like(part_ref)

    def rows_at(index, carry):
        at = pl.ds(pl.multiple_of(index * step, step), step)
        grad = row_sum([r.at[at, :] for r in pieces])
        hidden = pick_half(members, ids_ref, hiddens, at)
        inverse = rms_scale(hidden)
        part_ref[...] += jnp.sum(grad * hidden * inverse, axis=0, keepdims=True)
        total = cot_ref[at, :].astype(F32) + norm_back(grad, gain_ref[...], hidden, inverse)
        sum_ref[at, :] = total
        low = total.astype(BF)
        low_ref[at, :] = low
        for ref in sent:
            ref[at, :] = low
        return carry

    lax.fori_loop(0, shard // step, rows_at, 0)
    begin = (ids_ref[2] * members + ids_ref[0]) * shard
    keep = window(lengths_ref, begin + lax.broadcasted_iota(jnp.int32, (shard, 1), 0))[1]
    size = held.shape[0] // (2 * members)

    def heads_of(distance, carry):
        for copy, at, first in weight_copies(members, ids_ref, weights, held, sems, distance):
            copy.wait()
            out = dims(low_ref[...], held[pl.ds(at, size), :], 1, 1)
            made[distance, :, pl.ds(first, size)] = jnp.where(keep, out, 0.0).astype(BF)
        return carry

    lax.fori_loop(0, members, heads_of, 0)
    for distance, ref in enumerate(d_mixed):
        ref[...] = made[distance]


def norm_two_back(ids, lengths, hiddens, cotangent, gain, pieces, weights, travel):
    members = len(pieces)
    shard, width = pieces[0].shape
    inner = sum(w.shape[0] for w in weights)
    per = members // HALVES
    mine = pl.BlockSpec((shard, width), lambda i, ids, lengths: (ids[0], 0))
    mine_half = pl.BlockSpec((shard, width), lambda i, ids, lengths: (ids[0] % per, 0))
    whole = pl.BlockSpec((shard, width), lambda i, ids, lengths: (0, 0))
    line = pl.BlockSpec((1, width), lambda i, ids, lengths: (0, 0))
    head_spec = pl.BlockSpec((shard, inner // members), lambda i, ids, lengths: (0, 0))
    return pl.pallas_call(
        functools.partial(norm_two_back_kernel, members),
        grid_spec=pltpu.PrefetchScalarGridSpec(
            num_scalar_prefetch=2,
            grid=(1,),
            in_specs=[mine_half] * HALVES
            + [mine, line]
            + [whole] * members
            + [any_spec()] * (len(weights) + len(travel)),
            out_specs=[whole, whole, line] + [head_spec] * members + [whole] * len(travel),
            scratch_shapes=[
                pltpu.VMEM((inner, width), BF),
                pltpu.VMEM((members, shard, inner // members), BF),
                pltpu.SemaphoreType.DMA((2 * members,)),
            ],
        ),
        out_shape=[
            jax.ShapeDtypeStruct((shard, width), F32),
            jax.ShapeDtypeStruct((shard, width), BF),
            jax.ShapeDtypeStruct((1, width), F32),
        ]
        + [jax.ShapeDtypeStruct((shard, inner // members), BF)] * members
        + [jax.ShapeDtypeStruct(t.shape, BF) for t in travel],
        input_output_aliases={
            4 + HALVES + members + len(weights) + i: 3 + members + i for i in range(len(travel))
        },
        name="norm_two_back",
        cost_estimate=cost(2 * shard * inner * width, 2 * inner * width + 24 * shard * width),
    )(ids, lengths, *hiddens, cotangent, gain, *pieces, *weights, *travel)


def last_rows_kernel(members, ids_ref, x_ref, *refs):
    hiddens, (add_ref, gain_ref), refs = refs[:HALVES], refs[HALVES : HALVES + 2], refs[HALVES + 2 :]
    pieces, ffn, (low_ref, part_ref) = refs[:members], refs[members:-2], refs[-2:]
    shard = x_ref.shape[0]
    step = min(32, shard)
    part_ref[...] = jnp.zeros_like(part_ref)

    def rows_at(index, carry):
        first = pl.multiple_of(index * step, step)
        at = pl.ds(first, step)
        grad = row_sum([r.at[at, :] for r in pieces])
        values = x_ref[at, :].astype(F32)
        inverse = rms_scale(values)
        part_ref[...] += jnp.sum(grad * values * inverse, axis=0, keepdims=True)
        low_ref[at, :] = (
            add_ref[at, :] + norm_back(grad, gain_ref[...], values, inverse)
        ).astype(BF)
        hidden = pick_half(members, ids_ref, hiddens, at)
        low_ref[pl.ds(shard + first, step), :] = (
            hidden + row_sum([r.at[at, :] for r in ffn])
        ).astype(BF)
        return carry

    lax.fori_loop(0, shard // step, rows_at, 0)


def last_rows(ids, tokens, hiddens, add, gain, pieces, ffn_pieces):
    shard, width = pieces[0].shape
    per = len(pieces) // HALVES
    mine = pl.BlockSpec((shard, width), lambda i, ids: (ids[0], 0))
    mine_half = pl.BlockSpec((shard, width), lambda i, ids: (ids[0] % per, 0))
    first = pl.BlockSpec((shard, width), lambda i, ids: (0, 0))
    second = pl.BlockSpec((shard, width), lambda i, ids: (1, 0))
    line = pl.BlockSpec((1, width), lambda i, ids: (0, 0))
    both = pl.BlockSpec((2 * shard, width), lambda i, ids: (0, 0))
    return pl.pallas_call(
        functools.partial(last_rows_kernel, len(pieces)),
        grid_spec=pltpu.PrefetchScalarGridSpec(
            num_scalar_prefetch=1,
            grid=(1,),
            in_specs=[mine] + [mine_half] * HALVES + [first, line]
            + [first] * (len(pieces) + 1)
            + [second] * (len(ffn_pieces) - 1),
            out_specs=[both, line],
        ),
        out_shape=[
            jax.ShapeDtypeStruct((2 * shard, width), BF),
            jax.ShapeDtypeStruct((1, width), F32),
        ],
        name="last_rows",
        cost_estimate=cost(30 * shard * width, 32 * shard * width),
    )(ids, tokens, *hiddens, add, gain, *pieces, *ffn_pieces)


def in_order_kernel(shard, outs, ids_ref, *refs):
    pieces, out_refs = refs[:-outs], refs[-outs:]
    for distance, ref in enumerate(pieces):
        at = pl.multiple_of((ids_ref[0] ^ distance) * shard, shard)
        for index, out_ref in enumerate(out_refs):
            out_ref[pl.ds(at, shard), :] = ref[index * shard : (index + 1) * shard, :]


def in_order(ids, pieces, outs):
    width = pieces[0].shape[1]
    shard = pieces[0].shape[0] // outs if outs > 1 else pieces[0].shape[0]
    rows = shard * len(pieces)
    return pl.pallas_call(
        functools.partial(in_order_kernel, shard, outs),
        in_specs=[smem_spec()] + [vmem_spec()] * len(pieces),
        out_specs=[vmem_spec()] * outs,
        out_shape=[jax.ShapeDtypeStruct((rows, width), pieces[0].dtype)] * outs,
        name="token_order",
        cost_estimate=cost(0, 4 * rows * outs * width),
    )(ids, *pieces)


def ffn_kernel(members, ids_ref, x_ref, gain_ref, before_ref, da_ref, wg_ref, wu_ref, *refs):
    mixes, refs = refs[:members], refs[members:]
    weights, refs = refs[:2], refs[2:]
    hidden_ref, normed_ref, act_ref, dg_ref, du_ref, full_s = refs[:6]
    half_rows = before_ref.shape[0]

    @pl.when(pl.program_id(0) == 0)
    def _():
        full_s[:half_rows, :] = before_ref[...]
        project(
            members, ids_ref, x_ref, gain_ref, mixes, weights, hidden_ref, normed_ref, refs[6:]
        )
        full_s[half_rows:, :] = normed_ref[...]

    normed = full_s[...]
    gate = jnp.dot(normed, wg_ref[...], preferred_element_type=F32)
    up = jnp.dot(normed, wu_ref[...], preferred_element_type=F32)
    sig = jax.nn.sigmoid(gate)
    silu = gate * sig
    act_ref[...] = (silu * up).astype(BF)
    d_act = da_ref[...]
    dg_ref[...] = (d_act * up * sig * (1.0 + gate * (1.0 - sig))).astype(BF)
    du_ref[...] = (d_act * silu).astype(BF)


def ffn_forward(ids, tokens, gain, mixes, weights, before, d_act, w_gate, w_up):
    rows, width = tokens.shape
    half_rows = rows // HALVES
    members = len(mixes)
    inner = 2 * weights[0].shape[0]
    units = w_gate.shape[1]
    step = min(512, units)
    tile = pl.BlockSpec((rows, step), lambda j: (0, j))
    weight = pl.BlockSpec((width, step), lambda j: (0, j))
    half_spec = pl.BlockSpec((half_rows, width), lambda j: (0, 0))
    return pl.pallas_call(
        functools.partial(ffn_kernel, members),
        grid=(units // step,),
        in_specs=[
            smem_spec(),
            pl.BlockSpec((half_rows, width), lambda j: (HALVES - 1, 0)),
            pl.BlockSpec((1, width), lambda j: (0, 0)),
            half_spec,
            tile,
            weight,
            weight,
        ]
        + [pl.BlockSpec(m.shape, lambda j: (0, 0)) for m in mixes]
        + [any_spec()] * len(weights),
        out_specs=[half_spec, half_spec, tile, tile, tile],
        out_shape=[
            jax.ShapeDtypeStruct((half_rows, width), F32),
            jax.ShapeDtypeStruct((half_rows, width), BF),
        ]
        + [jax.ShapeDtypeStruct((rows, units), BF)] * 3,
        scratch_shapes=[pltpu.VMEM((rows, width), BF)]
        + project_scratch(inner, width, half_rows, members),
        name="gate_up",
        cost_estimate=cost(
            4 * rows * width * units + 2 * half_rows * inner * width,
            4 * width * units + 2 * rows * width + 10 * rows * units + 2 * inner * width,
            rows * units,
        ),
    )(ids, tokens, gain, before, d_act, w_gate, w_up, *mixes, *weights)


def store_by_distance(ids_ref, out_refs, held, value):
    shard = value.shape[0] // len(out_refs)
    held[...] = value.astype(BF)
    for distance, out_ref in enumerate(out_refs):
        at = pl.multiple_of((ids_ref[0] ^ distance) * shard, shard)
        out_ref[...] = held[pl.ds(at, shard), :]


def pair_nt_kernel(ids_ref, a_ref, b_ref, wa_ref, wb_ref, *refs):
    value = dims(a_ref[...], wa_ref[...], 1, 1) + dims(b_ref[...], wb_ref[...], 1, 1)
    store_by_distance(ids_ref, refs[:-1], refs[-1], value)


def pair_nt(members, ids, a, b, w_a, w_b):
    rows, units = a.shape
    width = w_a.shape[0]
    step = min(512, width)
    full = pl.BlockSpec((rows, units), lambda j: (0, 0))
    weight = pl.BlockSpec((step, units), lambda j: (j, 0))
    return pl.pallas_call(
        pair_nt_kernel,
        grid=(width // step,),
        in_specs=[smem_spec(), full, full, weight, weight],
        out_specs=[pl.BlockSpec((rows // members, step), lambda j: (0, j))] * members,
        out_shape=[jax.ShapeDtypeStruct((rows // members, width), BF)] * members,
        scratch_shapes=[pltpu.VMEM((rows, step), BF)],
        name="d_normed_two",
        cost_estimate=cost(
            4 * rows * width * units, 4 * width * units + 4 * rows * units + 2 * rows * width
        ),
    )(ids, a, b, w_a, w_b)


def down_kernel(ids_ref, a_ref, w_ref, *refs):
    value = jnp.dot(a_ref[...], w_ref[...], preferred_element_type=F32)
    store_by_distance(ids_ref, refs[:-1], refs[-1], value)


def down_of(members, ids, act, w_down):
    rows, units = act.shape
    shard = rows // members
    width = w_down.shape[1]
    step = min(512, width)
    return pl.pallas_call(
        down_kernel,
        grid=(width // step,),
        in_specs=[
            smem_spec(),
            pl.BlockSpec((rows, units), lambda j: (0, 0)),
            pl.BlockSpec((units, step), lambda j: (0, j)),
        ],
        out_specs=[pl.BlockSpec((shard, step), lambda j: (0, j))]
        + [pl.BlockSpec((shard, step), lambda j: (1, j))] * (members - 1),
        out_shape=[jax.ShapeDtypeStruct((shard, width), BF)]
        + [jax.ShapeDtypeStruct((2 * shard, width), BF)] * (members - 1),
        scratch_shapes=[pltpu.VMEM((rows, step), BF)],
        name="ffn_down",
        cost_estimate=cost(
            2 * rows * width * units, 2 * width * units + 2 * rows * units + 2 * rows * width
        ),
    )(ids, act, w_down)


def column_specs(rows, part, count):
    return [
        pl.BlockSpec((rows, part), lambda j, ids, k=k: (0, 2 * k + ids[1])) for k in range(count)
    ]


def fill_columns(held, refs, groups):
    count = len(refs) // groups
    rows, part = refs[0].shape
    for index, ref in enumerate(refs):
        top = (index // count) * rows
        left = (index % count) * part
        held[top : top + rows, left : left + part] = ref[...]


def pick_columns_kernel(blocks, ids_ref, *refs):
    fill_columns(refs[-1], refs[:-1], len(refs[:-1]) // blocks)


def pick_columns(ids, values, part):
    rows, width = values[0].shape
    blocks = width // (2 * part)
    return pl.pallas_call(
        functools.partial(pick_columns_kernel, blocks),
        grid_spec=pltpu.PrefetchScalarGridSpec(
            num_scalar_prefetch=1,
            grid=(1,),
            in_specs=column_specs(rows, part, blocks) * len(values),
            out_specs=pl.BlockSpec((len(values) * rows, width // 2), lambda j, ids: (0, 0)),
        ),
        out_shape=jax.ShapeDtypeStruct((len(values) * rows, width // 2), BF),
        name="pick_columns",
        cost_estimate=cost(0, 4 * len(values) * rows * width // 2),
    )(ids, *[v for v in values for _ in range(blocks)])


def grad_down_kernel(own_ref, other_ref, cot_ref, o_ref):
    rows = own_ref.shape[0]
    o_ref[...] = (
        dims(own_ref[...], cot_ref[:rows, :], 0, 0) + dims(other_ref[...], cot_ref[rows:, :], 0, 0)
    ).astype(BF)


def grad_down_of(act, act_other, cots):
    rows, units = act.shape
    width = cots.shape[1]
    step = min(512, units)
    tile = pl.BlockSpec((rows, step), lambda j: (0, j))
    return pl.pallas_call(
        grad_down_kernel,
        grid=(units // step,),
        in_specs=[tile, tile, pl.BlockSpec((2 * rows, width), lambda j: (0, 0))],
        out_specs=pl.BlockSpec((step, width), lambda j: (j, 0)),
        out_shape=jax.ShapeDtypeStruct((units, width), BF),
        name="grad_down",
        cost_estimate=cost(
            4 * rows * width * units, 4 * rows * units + 4 * rows * width + 2 * width * units
        ),
    )(act, act_other, cots)


def grad_in_kernel(groups, blocks, half, ids_ref, *refs):
    normeds, refs = refs[: groups * blocks], refs[groups * blocks :]
    gates, ups, (o_ref, held) = refs[:2], refs[2:4], refs[4:]

    @pl.when(pl.program_id(0) == 0)
    def _():
        fill_columns(held, normeds, groups)

    rows = gates[0].shape[0]

    def of(pair):
        o_ref[...] = (
            dims(held[:rows, :], pair[0][...], 0, 0) + dims(held[rows:, :], pair[1][...], 0, 0)
        ).astype(BF)

    pl.when(pl.program_id(0) < half)(lambda: of(gates))
    pl.when(pl.program_id(0) >= half)(lambda: of(ups))


def grad_in_of(ids, normeds, d_gates, d_ups, part):
    width = normeds[0].shape[1]
    rows, units = d_gates[0].shape
    blocks = width // (2 * part)
    step = min(512, units)
    half = units // step
    columns = column_specs(normeds[0].shape[0], part, blocks)
    first = pl.BlockSpec((rows, step), lambda j, ids: (0, jnp.minimum(j, half - 1)))
    second = pl.BlockSpec((rows, step), lambda j, ids: (0, jnp.maximum(j - half, 0)))
    return pl.pallas_call(
        functools.partial(grad_in_kernel, len(normeds), blocks, half),
        grid_spec=pltpu.PrefetchScalarGridSpec(
            num_scalar_prefetch=1,
            grid=(2 * half,),
            in_specs=columns * len(normeds) + [first] * 2 + [second] * 2,
            out_specs=pl.BlockSpec((width // 2, step), lambda j, ids: (0, j)),
            scratch_shapes=[pltpu.VMEM((2 * rows, width // 2), BF)],
        ),
        out_shape=jax.ShapeDtypeStruct((width // 2, 2 * units), BF),
        name="grad_gate_up",
        cost_estimate=cost(
            4 * rows * width * units, 8 * rows * units + 2 * rows * width + 2 * width * units
        ),
    )(ids, *[n for n in normeds for _ in range(blocks)], *d_gates, *d_ups)


def grad_proj_kernel(lefts, ids_ref, *refs):
    own, other = refs[:lefts], refs[lefts : 2 * lefts]
    right_ref, right_other_ref, o_ref = refs[2 * lefts :]
    at = 0
    rows = right_ref.shape[0]
    part = rows // lefts
    total = 0.0
    for group, right in ((own, right_ref), (other, right_other_ref)):
        for index, left in enumerate(group):
            total = total + jnp.dot(
                left[...],
                right[index * part : (index + 1) * part, :],
                preferred_element_type=F32,
            )
    o_ref[...] = total.astype(BF)


def grad_proj_of(ids, lefts, lefts_other, right, right_other, part, name):
    inner = lefts[0].shape[0]
    rows, width = right.shape
    blocks = width // (2 * part)
    left_spec = pl.BlockSpec(lefts[0].shape, lambda k, ids: (0, 0))
    right_spec = pl.BlockSpec((rows, part), lambda k, ids: (0, 2 * k + ids[1]))
    return pl.pallas_call(
        functools.partial(grad_proj_kernel, len(lefts)),
        grid_spec=pltpu.PrefetchScalarGridSpec(
            num_scalar_prefetch=1,
            grid=(blocks,),
            in_specs=[left_spec] * (2 * len(lefts)) + [right_spec] * 2,
            out_specs=pl.BlockSpec((inner, part), lambda k, ids: (0, k)),
        ),
        out_shape=jax.ShapeDtypeStruct((inner, width // 2), BF),
        name=name,
        cost_estimate=cost(
            2 * rows * width * inner, 4 * inner * rows + 2 * rows * width + inner * width
        ),
    )(ids, *lefts, *lefts_other, right, right_other)


def finish_kernel(in_ref, out_ref, *refs):
    at = out_ref.shape[0]
    out_ref[...] = in_ref[:at, :].astype(F32)
    for ref in refs:
        count = ref.shape[1]
        ref[...] = in_ref[at : at + count, :].astype(F32).T
        at += count


def finish(grads, sizes):
    part = grads.shape[1]
    return pl.pallas_call(
        finish_kernel,
        in_specs=[vmem_spec()],
        out_specs=[vmem_spec()] * len(sizes),
        out_shape=[jax.ShapeDtypeStruct((sizes[0], part), F32)]
        + [jax.ShapeDtypeStruct((part, size), F32) for size in sizes[1:]],
        name="finish",
        cost_estimate=cost(0, 6 * sum(sizes) * part),
    )(grads)


def together(*values):
    return lax.optimization_barrier(values)


def body(
    tokens,
    attn_gain,
    w_query,
    w_key,
    w_value,
    w_out,
    ffn_gain,
    w_gate,
    w_up,
    w_down,
    doc_lengths,
    cotangent,
):
    rows, width = tokens.shape
    wide = lax.axis_size("wide")
    narrow = lax.axis_size("narrow")
    me_wide = lax.axis_index("wide")
    me = lax.axis_index("narrow")
    core = me_wide % 2
    kv_heads = w_key.shape[1] // HD
    half_rows = rows // HALVES
    shard = rows // narrow
    part = width // wide
    hops = wide // 4
    units = w_gate.shape[1]
    q_width = w_query.shape[1]
    k_width = w_key.shape[1]
    chip_groups = [list(range(0, wide, 2)), list(range(1, wide, 2))]
    ids = jnp.stack([me, core, me_wide]).astype(jnp.int32)

    def other_core(value):
        return lax.ppermute(value, "wide", [(i, i ^ 1) for i in range(wide)])

    def chips_up(value, hop):
        return lax.ppermute(value, "wide", [(i, i + 2 * hop) for i in range(wide - 2 * hop)])

    def chips_down(value, hop):
        return lax.ppermute(value, "wide", [(i + 2 * hop, i) for i in range(wide - 2 * hop)])

    def swap(value, distance):
        return lax.ppermute(value, "narrow", [(i, i ^ distance) for i in range(narrow)])

    def rows_of(value, distance):
        return lax.dynamic_slice_in_dim(value, (me ^ distance) * shard, shard, 0)

    def exchange(pieces):
        return [pieces[0]] + [swap(pieces[d], d) for d in range(1, narrow)]

    def gather_near(value):
        return [value] + [swap(value, d) for d in range(1, narrow)]

    def scatter(value, dimension):
        return lax.psum_scatter(
            value,
            "wide",
            scatter_dimension=dimension,
            axis_index_groups=chip_groups,
            tiled=True,
        )

    gain_one = attn_gain.astype(F32)[None, :]
    gain_two = ffn_gain.astype(F32)[None, :]

    w_half = w_out.shape[0] // 2
    w_mine = lax.dynamic_slice_in_dim(w_out, core * w_half, w_half, 0)
    w_all = lax.all_gather(w_mine, "narrow", axis=0, tiled=True)

    base = me_wide * rows
    index = base + jnp.arange(rows, dtype=jnp.int32)
    start = doc_offsets(doc_lengths, index)
    angle = jnp.asarray(inverse_frequencies(HD))[:, None] * (index - start).astype(F32)[None, :]
    cosine = jnp.cos(angle)
    sine = jnp.sin(angle)
    normed, packed = keys_values(tokens, gain_one, w_key, w_value, cosine, sine)
    ups = [chips_up(packed, hop) for hop in range(1, hops + 1)]
    beside = other_core(packed)
    query_t = rotate_t(dims(w_query, normed, 0, 1), cosine, sine).astype(BF)
    d_act = dims(cotangent, w_down, 1, 1)
    cot_other = other_core(cotangent)
    normed_other = other_core(normed)
    ups, query_t, d_act = together(ups, query_t, d_act)
    blocks = [packed, beside]
    for near in ups:
        blocks += [near, other_core(near)]

    outs, mixes, lses, gathered = [], [], [], []
    for half in range(HALVES):
        out, mixed, lse = attend(half, ids, doc_lengths, query_t, blocks, kv_heads)
        if gathered:
            mixed_others = [other_core(mixes[0])]
            gathered[-1], mixed, w_all, normed_other, mixed_others = together(
                gathered[-1], mixed, w_all, normed_other, mixed_others
            )
            out_weights = [w_all, other_core(w_all)]
        outs.append(out)
        mixes.append(mixed)
        lses.append(lse)
        query_t, mixed = together(query_t, mixed)
        gathered.append(gather_near(mixed))
    hidden_first, normed_first = attn_out(0, ids, tokens, gain_two, gathered[0], out_weights)
    gathered[1], normed_first = together(gathered[1], normed_first)

    hidden_last, normed_last, act, d_gate, d_up = ffn_forward(
        ids, tokens, gain_two, gathered[1], out_weights, normed_first, d_act, w_gate, w_up
    )
    hiddens = [hidden_first, hidden_last]
    act_other = other_core(act)
    d_gates = [d_gate, other_core(d_gate)]
    d_ups = [d_up, other_core(d_up)]
    normed_twos = [normed_first, normed_last]
    normed_others = [other_core(n) for n in normed_twos]
    act, cot_other, cot_mine = together(act, cot_other, cotangent)
    cots = pick_columns(ids, [cot_mine, cot_other], part)
    act_other, cots = together(act_other, cots)
    grad_down = grad_down_of(act, act_other, cots)
    d_gate_then, _ = together(d_gate, grad_down)
    grad_down = scatter(grad_down, 1)
    d_norm_pieces = pair_nt(narrow, ids, d_gate_then, d_up, w_gate, w_up)
    mixed_others += [other_core(m) for m in mixes[1:]]
    act_then, d_norm_pieces, d_gates, d_ups, normed_others, mixed_others = together(
        act, d_norm_pieces, d_gates, d_ups, normed_others, mixed_others
    )
    d_norm_pieces = exchange(d_norm_pieces)
    ffn_pieces = down_of(narrow, ids, act_then, w_down)
    d_norm_pieces[1], ffn_pieces, normed_twos = together(
        d_norm_pieces[1], ffn_pieces, normed_twos
    )
    grad_gate_up = grad_in_of(ids, normed_twos + normed_others, d_gates, d_ups, part)
    d_norm_pieces, ffn_pieces, _ = together(d_norm_pieces, ffn_pieces, grad_gate_up)

    d_hidden, d_hidden_b, gain_two_part, *made = norm_two_back(
        ids,
        doc_lengths,
        hiddens,
        cotangent,
        gain_two,
        d_norm_pieces,
        out_weights,
        ffn_pieces[1:],
    )
    d_mixed, travel = made[:narrow], made[narrow:]
    grad_gate_up, _ = together(grad_gate_up, d_hidden_b)
    grad_gate_up = scatter(grad_gate_up, 0)
    d_mixed = exchange(d_mixed)
    d_mixed, travel = together(d_mixed, travel)
    travel = [swap(value, d + 1) for d, value in enumerate(travel)]

    d_query_r, d_blocks = attend_back(
        ids, doc_lengths, query_t, d_mixed, outs, lses, blocks, kv_heads
    )
    d_query_r, d_blocks, travel[0] = together(d_query_r, d_blocks, travel[0])
    d_blocks = d_blocks.reshape(2 * (hops + 1), 2 * k_width, rows)
    for_other = other_core(d_blocks[1::2])
    both = [
        d_blocks[2 * hop].astype(F32) + for_other[hop].astype(F32) for hop in range(hops + 1)
    ]
    down = chips_down(both[hops].astype(BF), 1)
    for hop in range(hops - 1, 0, -1):
        down = chips_down((both[hop] + down.astype(F32)).astype(BF), 1)
    d_kv = both[0]

    d_query = rotate_t(d_query_r * (1.0 / math.sqrt(HD)), cosine, -sine).astype(BF)
    (d_hidden_full,) = in_order(ids, [d_hidden_b, *travel], 1)
    grad_query = grad_proj_of(
        ids, [d_query], [other_core(d_query)], normed, normed_other, part, "grad_query"
    )
    grad_out = grad_proj_of(
        ids, mixes, mixed_others, d_hidden_full, other_core(d_hidden_full), part, "grad_out"
    )
    down, grad_out, grad_query, grad_down = together(down, grad_out, grad_query, grad_down)
    d_kv = d_kv + down.astype(F32)
    d_keys = rotate_t(d_kv[:k_width], cosine, -sine).astype(BF)
    d_values = d_kv[k_width:].astype(BF)
    norm_one_part = (
        dims(d_query, w_query, 0, 1) + dims(d_keys, w_key, 0, 1) + dims(d_values, w_value, 0, 1)
    ).astype(BF)
    norm_one_pieces = [rows_of(norm_one_part, d) for d in range(narrow)]
    d_pair = jnp.concatenate([d_keys, d_values], axis=0)
    d_pair, norm_one_pieces = together(d_pair, norm_one_pieces)
    norm_one_pieces = exchange(norm_one_pieces)
    grad_pair = grad_proj_of(
        ids, [d_pair], [other_core(d_pair)], normed, normed_other, part, "grad_key_value"
    )
    grads = jnp.concatenate([grad_out, grad_query, grad_pair], axis=0)
    norm_one_pieces, grads = together(norm_one_pieces, grads)
    last, gain_one_part = last_rows(
        ids,
        tokens,
        hiddens,
        d_hidden,
        gain_one,
        norm_one_pieces,
        [ffn_pieces[0], *travel],
    )
    last_pieces = gather_near(last)
    gains = jnp.concatenate([gain_one_part, gain_two_part], axis=0)
    grads, grad_gate_up, last_pieces[1:-1] = together(grads, grad_gate_up, last_pieces[1:-1])
    grads = scatter(grads, 1)
    input_grad, output = in_order(ids, last_pieces, 2)
    gains, output = together(gains, output)
    gains = sum(gather_near(gains)[1:], gains)
    gains = gains + other_core(gains)
    gain_sum = 0.0
    for hop in range(wide // 2):
        target = lax.rem(me_wide + 2 * hop, wide)
        piece = lax.dynamic_slice_in_dim(gains, target * part, part, 1)
        if hop:
            piece = lax.ppermute(piece, "wide", [(i, (i + 2 * hop) % wide) for i in range(wide)])
        gain_sum = gain_sum + piece
    gains = gain_sum
    grad_gate = grad_gate_up[:, :units].astype(F32)
    grad_up = grad_gate_up[:, units:].astype(F32)
    grad_down = grad_down.astype(F32)
    grads, gains, input_grad, output, grad_gate, grad_up, grad_down = together(
        grads, gains, input_grad, output, grad_gate, grad_up, grad_down
    )
    grad_out, grad_query, grad_key, grad_value = finish(
        grads, (w_out.shape[0], q_width, k_width, k_width)
    )
    return (
        output,
        input_grad,
        gains[0],
        grad_query,
        grad_key,
        grad_value,
        grad_out,
        gains[1],
        grad_gate,
        grad_up,
        grad_down,
    )


def solution(mesh):
    in_specs = (
        P("wide", None),
        P(),
        P(None, "narrow"),
        P(None, "narrow"),
        P(None, "narrow"),
        P("narrow", None),
        P(),
        P(None, "narrow"),
        P(None, "narrow"),
        P("narrow", None),
        P(),
        P("wide", None),
    )
    out_specs = (
        P("wide", None),
        P("wide", None),
        P("wide"),
        P("wide", "narrow"),
        P("wide", "narrow"),
        P("wide", "narrow"),
        P("narrow", "wide"),
        P("wide"),
        P("wide", "narrow"),
        P("wide", "narrow"),
        P("narrow", "wide"),
    )
    return jax.shard_map(body, mesh=mesh, in_specs=in_specs, out_specs=out_specs, check_vma=False)
```

```python
import functools
import math

import jax
import jax.numpy as jnp
import numpy as np
from jax import lax
from jax.experimental import pallas as pl
from jax.experimental.pallas import tpu as pltpu
from jax.sharding import PartitionSpec as P

HD = 64
DOCS = 12
NORM_EPS = 1e-05
MASKED_SCORE = -1e30
LOG2E = math.log2(math.e)
SCALE2 = LOG2E / math.sqrt(HD)
KT = 256
HALVES = 2
BF = jnp.bfloat16
F32 = jnp.float32


def inverse_frequencies(head_size):
    frequency = 1.0 / 500000.0 ** (np.arange(0, head_size, 2) / head_size)
    wavelength = 2 * math.pi / frequency
    smoothing = (8192.0 / wavelength - 1.0) / 3.0
    scaled_freq = np.where(wavelength > 8192.0, frequency / 32.0, frequency)
    middle_band = (wavelength <= 8192.0) & (wavelength >= 2048.0)
    scaled_freq = np.where(
        middle_band, (1 - smoothing) * frequency / 32.0 + smoothing * frequency, scaled_freq
    )
    return scaled_freq.astype(np.float32)


def doc_offsets(doc_lengths, index):
    ends = jnp.cumsum(doc_lengths)
    passed = (index[None, :] >= ends[:, None]).astype(jnp.int32)
    return jnp.sum(passed * doc_lengths[:, None], axis=0)


def rotate_t(values, cosine, sine):
    heads = values.shape[0] // HD
    shaped = values.reshape(heads, 2, HD // 2, values.shape[1])
    first = shaped[:, 0]
    second = shaped[:, 1]
    return jnp.stack(
        [first * cosine - second * sine, second * cosine + first * sine], axis=1
    ).reshape(values.shape)


def dims(left, right, a, b):
    return lax.dot_general(left, right, (((a,), (b,)), ((), ())), preferred_element_type=F32)


def vmem_spec():
    return pl.BlockSpec(memory_space=pltpu.VMEM)


def smem_spec():
    return pl.BlockSpec(memory_space=pltpu.SMEM)


def any_spec():
    return pl.BlockSpec(memory_space=pl.ANY)


def cost(flops, moved, exps=0):
    return pl.CostEstimate(flops=int(flops), transcendentals=int(exps), bytes_accessed=int(moved))


def rms_scale(values):
    return lax.rsqrt(jnp.mean(values * values, axis=-1, keepdims=True) + NORM_EPS)


def keys_values_kernel(x_ref, gain_ref, wk_ref, wv_ref, cos_ref, sin_ref, normed_ref, packed_ref):
    rows = x_ref.shape[0]
    step = min(128, rows)
    for at in range(0, rows, step):
        values = x_ref[at : at + step, :].astype(F32)
        normed_ref[at : at + step, :] = (values * rms_scale(values) * gain_ref[...]).astype(BF)
    normed = normed_ref[...]
    keys = jnp.dot(normed, wk_ref[...], preferred_element_type=F32).T
    width = keys.shape[0]
    half = HD // 2
    for head in range(width // HD):
        first = keys[head * HD : head * HD + half]
        second = keys[head * HD + half : (head + 1) * HD]
        cosine, sine = cos_ref[...], sin_ref[...]
        packed_ref[head * HD : head * HD + half, :] = (first * cosine - second * sine).astype(BF)
        packed_ref[head * HD + half : (head + 1) * HD, :] = (
            second * cosine + first * sine
        ).astype(BF)
    packed_ref[width:, :] = jnp.dot(normed, wv_ref[...], preferred_element_type=F32).T.astype(BF)


def keys_values(tokens, gain, w_key, w_value, cosine, sine):
    rows, width = tokens.shape
    kv = w_key.shape[1]
    return pl.pallas_call(
        keys_values_kernel,
        in_specs=[vmem_spec()] * 6,
        out_specs=[vmem_spec()] * 2,
        out_shape=[
            jax.ShapeDtypeStruct((rows, width), BF),
            jax.ShapeDtypeStruct((2 * kv, rows), BF),
        ],
        name="keys_values",
        cost_estimate=cost(4 * rows * width * kv, 4 * rows * width + 4 * width * kv),
    )(tokens, gain, w_key, w_value, cosine, sine)


def window(lengths_ref, index):
    end = lengths_ref[0]
    start = jnp.zeros_like(index)
    for doc in range(1, DOCS):
        start = jnp.where(index >= end, end, start)
        if doc == DOCS - 1:
            last = end
        end = end + lengths_ref[doc]
    valid = index < last
    return jnp.where(valid, start, index), valid


def tile_state(ids_ref, edge, tile, half, q_rows, rows):
    me_wide = ids_ref[2]
    slot = tile // (rows // KT)
    block = (me_wide // 2 - slot // 2) * 2 + (ids_ref[1] ^ (slot % 2))
    key_base = block * rows + (tile % (rows // KT)) * KT
    q_base = me_wide * rows + half * q_rows
    low, high = edge
    active = (key_base <= q_base + q_rows - 1) & (key_base + KT > low)
    whole = (key_base + KT - 1 <= q_base) & (key_base >= high)
    return active, active & whole, key_base, q_base


def window_edge(ids_ref, lengths_ref, rows, half):
    base = ids_ref[2] * rows
    step = rows // HALVES
    return (
        window(lengths_ref, base + half * step)[0],
        window(lengths_ref, base + (half + 1) * step - 1)[0],
    )


def query_row(ids_ref, rows, half):
    step = rows // HALVES
    return ids_ref[2] * rows + half * step + lax.broadcasted_iota(jnp.int32, (1, step), 1)


def tile_mask(key_base, q_base, start_row):
    q_rows = start_row.shape[1]
    keys = key_base + lax.broadcasted_iota(jnp.int32, (KT, q_rows), 0)
    queries = q_base + lax.broadcasted_iota(jnp.int32, (KT, q_rows), 1)
    return (keys <= queries) & (keys >= start_row)


def both_ways(active, whole, run):
    pl.when(whole)(lambda: run(False))
    pl.when(active & jnp.logical_not(whole))(lambda: run(True))


def attend_kernel(slots, group, half, ids_ref, lengths_ref, q_ref, *refs):
    k_refs = refs[:slots]
    v_refs = refs[slots : 2 * slots]
    o_ref, mixed_ref, lse_ref, keys_s, values_s, top_s, sum_s, acc_s = refs[2 * slots :]
    q_rows = q_ref.shape[1]
    rows = k_refs[0].shape[1]
    per = rows // KT
    tiles = slots * per
    edge = window_edge(ids_ref, lengths_ref, rows, half)
    start_row, valid_row = window(lengths_ref, query_row(ids_ref, rows, half))
    for slot in range(slots):
        for part in range(per):
            tile = slot * per + part
            cut = slice(part * KT, (part + 1) * KT)

            @pl.when(tile_state(ids_ref, edge, tile, half, q_rows, rows)[0])
            def _(tile=tile, slot=slot, cut=cut):
                keys_s[tile] = k_refs[slot][:, cut].T
                values_s[tile] = v_refs[slot][:, cut]

    top_s[...] = jnp.full_like(top_s, MASKED_SCORE)
    sum_s[...] = jnp.zeros_like(sum_s)
    acc_s[...] = jnp.zeros_like(acc_s)
    heads = range(group)

    def step(tile, carry):
        active, whole, key_base, q_base = tile_state(ids_ref, edge, tile, half, q_rows, rows)

        def run(masked):
            keys = keys_s[tile]
            values = values_s[tile]
            scores = [
                jnp.dot(keys, q_ref[h * HD : (h + 1) * HD, :], preferred_element_type=F32)
                for h in heads
            ]
            if masked:
                allowed = tile_mask(key_base, q_base, start_row)
                scores = [jnp.where(allowed, s, MASKED_SCORE) for s in scores]
            tops, decays = [], []
            for h in heads:
                old = top_s[h : h + 1, :]
                new = jnp.maximum(old, jnp.max(scores[h], axis=0, keepdims=True))
                top_s[h : h + 1, :] = new
                tops.append(new)
                decays.append(jnp.exp2((old - new) * SCALE2))
            for h in heads:
                weight = jnp.exp2((scores[h] - tops[h]) * SCALE2)
                sum_s[h : h + 1, :] = sum_s[h : h + 1, :] * decays[h] + jnp.sum(
                    weight, axis=0, keepdims=True
                )
                acc_s[h] = acc_s[h] * decays[h] + jnp.dot(
                    values, weight.astype(BF), preferred_element_type=F32
                )

        both_ways(active, whole, run)
        return carry

    lax.fori_loop(0, tiles, step, 0)
    for h in heads:
        h_cut = slice(h * HD, (h + 1) * HD)
        total = sum_s[h : h + 1, :]
        out = acc_s[h] / total
        o_ref[h_cut, :] = out
        mixed_ref[h_cut, :] = jnp.where(valid_row, out, 0.0).astype(BF)
        lse_ref[0, h : h + 1, :] = top_s[h : h + 1, :] * SCALE2 + jnp.log(total) * LOG2E


def attend(half, ids, lengths, q_t, blocks, kv_heads):
    slots = len(blocks)
    heads = q_t.shape[0] // HD
    group = heads // kv_heads
    rows = q_t.shape[1]
    q_rows = rows // HALVES
    tiles = slots * (rows // KT)
    out_spec = pl.BlockSpec((group * HD, q_rows), lambda g: (g, 0))
    return pl.pallas_call(
        functools.partial(attend_kernel, slots, group, half),
        grid=(kv_heads,),
        in_specs=[
            smem_spec(),
            smem_spec(),
            pl.BlockSpec((group * HD, q_rows), lambda g: (g, half)),
        ]
        + [pl.BlockSpec((HD, rows), lambda g: (g, 0))] * slots
        + [pl.BlockSpec((HD, rows), lambda g: (kv_heads + g, 0))] * slots,
        out_specs=[out_spec, out_spec, pl.BlockSpec((1, group, q_rows), lambda g: (g, 0, 0))],
        out_shape=[
            jax.ShapeDtypeStruct((heads * HD, q_rows), F32),
            jax.ShapeDtypeStruct((heads * HD, q_rows), BF),
            jax.ShapeDtypeStruct((kv_heads, group, q_rows), F32),
        ],
        scratch_shapes=[
            pltpu.VMEM((tiles, KT, HD), BF),
            pltpu.VMEM((tiles, HD, KT), BF),
            pltpu.VMEM((group, q_rows), F32),
            pltpu.VMEM((group, q_rows), F32),
            pltpu.VMEM((group, HD, q_rows), F32),
        ],
        name="attend",
        cost_estimate=cost(
            16 * heads * q_rows * rows * HD, 8 * rows * heads * HD, heads * q_rows * rows * 4
        ),
    )(ids, lengths, q_t, *blocks, *blocks)


def attend_back_kernel(slots, group, members, ids_ref, lengths_ref, q_ref, *refs):
    do_refs, refs = refs[:members], refs[members:]
    o_refs, lse_refs, refs = refs[:HALVES], refs[HALVES : 2 * HALVES], refs[2 * HALVES :]
    k_refs, v_refs, refs = refs[:slots], refs[slots : 2 * slots], refs[2 * slots :]
    dq_ref, dkv_ref = refs[:2]
    keys_s, values_s, keys_t_s, dk_s, dv_s, q_s, do_s, do_t_s, dq_s, delta_s, lse_s = refs[2:]
    rows = q_ref.shape[1]
    q_rows = rows // HALVES
    per = rows // KT
    tiles = slots * per
    heads = range(group)
    edges = [window_edge(ids_ref, lengths_ref, rows, half) for half in range(HALVES)]

    def any_active(tile):
        found = tile_state(ids_ref, edges[0], tile, 0, q_rows, rows)[0]
        for half in range(1, HALVES):
            found = found | tile_state(ids_ref, edges[half], tile, half, q_rows, rows)[0]
        return found

    for slot in range(slots):
        for part in range(per):
            tile = slot * per + part
            cut = slice(part * KT, (part + 1) * KT)

            @pl.when(any_active(tile))
            def _(tile=tile, slot=slot, cut=cut):
                keys_s[tile] = k_refs[slot][:, cut].T
                keys_t_s[tile] = k_refs[slot][:, cut]
                values_s[tile] = v_refs[slot][:, cut].T
                dk_s[tile] = jnp.zeros((KT, HD), F32)
                dv_s[tile] = jnp.zeros((KT, HD), F32)

    shard = do_refs[0].shape[0]
    for distance in range(members):
        at = pl.multiple_of((ids_ref[0] ^ distance) * shard, shard)
        do_s[pl.ds(at, shard), :] = do_refs[distance][...]
    do_t_s[...] = do_s[...].T

    for half in range(HALVES):
        for h in heads:
            h_cut = slice(h * HD, (h + 1) * HD)
            do_h = do_t_s[h_cut, half * q_rows : (half + 1) * q_rows].astype(F32)
            delta_s[half, h : h + 1, :] = jnp.sum(
                do_h * o_refs[half][h_cut, :], axis=0, keepdims=True
            )
            lse_s[half, h : h + 1, :] = lse_refs[half][0, h : h + 1, :]

    def half_step(half, carry):
        q_cut = pl.ds(pl.multiple_of(half * q_rows, q_rows), q_rows)
        edge = window_edge(ids_ref, lengths_ref, rows, half)
        for h in heads:
            q_s[h] = q_ref[h * HD : (h + 1) * HD, q_cut].T
        dq_s[...] = jnp.zeros_like(dq_s)
        start_row = window(lengths_ref, query_row(ids_ref, rows, half))[0]

        def step(tile, carry):
            active, whole, key_base, q_base = tile_state(ids_ref, edge, tile, half, q_rows, rows)

            def run(masked):
                keys = keys_s[tile]
                values = values_s[tile]
                keys_t = keys_t_s[tile]
                scores = [
                    jnp.dot(keys, q_ref[h * HD : (h + 1) * HD, q_cut], preferred_element_type=F32)
                    for h in heads
                ]
                prob_grads = [
                    jnp.dot(values, do_t_s[h * HD : (h + 1) * HD, q_cut], preferred_element_type=F32)
                    for h in heads
                ]
                if masked:
                    allowed = tile_mask(key_base, q_base, start_row)
                probs, d_scores = [], []
                for h in heads:
                    scaled = scores[h] * SCALE2 - lse_s[half, h : h + 1, :]
                    if masked:
                        scaled = jnp.where(allowed, scaled, MASKED_SCORE)
                    prob = jnp.exp2(scaled)
                    probs.append(prob.astype(BF))
                    d_scores.append(
                        (prob * (prob_grads[h] - delta_s[half, h : h + 1, :])).astype(BF)
                    )
                dk = dk_s[tile]
                dv = dv_s[tile]
                for h in heads:
                    dv = dv + jnp.dot(
                        probs[h],
                        do_s[q_cut, h * HD : (h + 1) * HD],
                        preferred_element_type=F32,
                    )
                    dk = dk + jnp.dot(d_scores[h], q_s[h], preferred_element_type=F32)
                    dq_s[h] += jnp.dot(keys_t, d_scores[h], preferred_element_type=F32)
                dk_s[tile] = dk
                dv_s[tile] = dv

            both_ways(active, whole, run)
            return carry

        lax.fori_loop(0, tiles, step, 0)
        for h in heads:
            dq_ref[h * HD : (h + 1) * HD, q_cut] = dq_s[h]
        return carry

    lax.fori_loop(0, HALVES, half_step, 0)
    for slot in range(slots):
        for part in range(per):
            cut = slice(part * KT, (part + 1) * KT)
            tile = slot * per + part
            active = any_active(tile)

            @pl.when(active)
            def _(tile=tile, slot=slot, cut=cut):
                dkv_ref[slot, 0, :, cut] = (dk_s[tile].T * (1.0 / math.sqrt(HD))).astype(BF)
                dkv_ref[slot, 1, :, cut] = dv_s[tile].T.astype(BF)

            @pl.when(jnp.logical_not(active))
            def _(slot=slot, cut=cut):
                dkv_ref[slot, 0, :, cut] = jnp.zeros((HD, KT), BF)
                dkv_ref[slot, 1, :, cut] = jnp.zeros((HD, KT), BF)


def attend_back(ids, lengths, q_t, do_pieces, outs, lses, blocks, kv_heads):
    slots = len(blocks)
    heads = q_t.shape[0] // HD
    group = heads // kv_heads
    rows = q_t.shape[1]
    q_rows = rows // HALVES
    tiles = slots * (rows // KT)
    members = len(do_pieces)
    wide = group * HD
    q_spec = pl.BlockSpec((wide, rows), lambda g: (g, 0))
    return pl.pallas_call(
        functools.partial(attend_back_kernel, slots, group, members),
        grid=(kv_heads,),
        in_specs=[smem_spec(), smem_spec(), q_spec]
        + [pl.BlockSpec((rows // members, wide), lambda g: (0, g))] * members
        + [pl.BlockSpec((wide, q_rows), lambda g: (g, 0))] * HALVES
        + [pl.BlockSpec((1, group, q_rows), lambda g: (g, 0, 0))] * HALVES
        + [pl.BlockSpec((HD, rows), lambda g: (g, 0))] * slots
        + [pl.BlockSpec((HD, rows), lambda g: (kv_heads + g, 0))] * slots,
        out_specs=[q_spec, pl.BlockSpec((slots, 2, HD, rows), lambda g: (0, 0, g, 0))],
        out_shape=[
            jax.ShapeDtypeStruct(q_t.shape, F32),
            jax.ShapeDtypeStruct((slots, 2, kv_heads * HD, rows), BF),
        ],
        scratch_shapes=[
            pltpu.VMEM((tiles, KT, HD), BF),
            pltpu.VMEM((tiles, KT, HD), BF),
            pltpu.VMEM((tiles, HD, KT), BF),
            pltpu.VMEM((tiles, KT, HD), F32),
            pltpu.VMEM((tiles, KT, HD), F32),
            pltpu.VMEM((group, q_rows, HD), BF),
            pltpu.VMEM((rows, wide), BF),
            pltpu.VMEM((wide, rows), BF),
            pltpu.VMEM((group, HD, q_rows), F32),
            pltpu.VMEM((HALVES, group, q_rows), F32),
            pltpu.VMEM((HALVES, group, q_rows), F32),
        ],
        name="attend_back",
        cost_estimate=cost(
            40 * heads * rows * rows * HD, 16 * rows * heads * HD, heads * rows * rows * 4
        ),
    )(ids, lengths, q_t, *do_pieces, *outs, *lses, *blocks, *blocks)


def weight_copies(members, ids_ref, weights, held, sems, distance):
    size = held.shape[0] // (2 * members)
    copies = []
    for other in range(2):
        index = 2 * distance + other
        source = pl.multiple_of((ids_ref[0] ^ distance) * size, size)
        at = pl.multiple_of(index * size, size)
        copy = pltpu.make_async_copy(
            weights[other].at[pl.ds(source, size), :], held.at[pl.ds(at, size), :], sems.at[index]
        )
        copies.append((copy, at, pl.multiple_of((ids_ref[1] ^ other) * size, size)))
    return copies


def project(members, ids_ref, x_ref, gain_ref, mixes, weights, hidden_ref, normed_ref, scratch):
    held, left, sems = scratch
    size = held.shape[0] // (2 * members)
    for distance in range(members):
        for copy, _, _ in weight_copies(members, ids_ref, weights, held, sems, distance):
            copy.start()
    for distance in range(members):
        for other in range(2):
            at = (2 * distance + other) * size
            first = pl.multiple_of((ids_ref[1] ^ other) * size, size)
            left[at : at + size, :] = mixes[distance][pl.ds(first, size), :]
    hidden_ref[...] = x_ref[...].astype(F32)

    def add(distance, carry):
        for copy, _, _ in weight_copies(members, ids_ref, weights, held, sems, distance):
            copy.wait()
        at = pl.ds(pl.multiple_of(2 * distance * size, size), 2 * size)
        hidden_ref[...] += dims(left[at, :], held[at, :], 0, 0)
        return carry

    lax.fori_loop(0, members, add, 0)
    rows = hidden_ref.shape[0]
    step = min(64, rows)

    def norm(index, carry):
        at = pl.ds(pl.multiple_of(index * step, step), step)
        hidden = hidden_ref[at, :]
        normed_ref[at, :] = (hidden * rms_scale(hidden) * gain_ref[...]).astype(BF)
        return carry

    lax.fori_loop(0, rows // step, norm, 0)


def project_scratch(inner, width, half_rows, members):
    return [
        pltpu.VMEM((inner, width), BF),
        pltpu.VMEM((inner, half_rows), BF),
        pltpu.SemaphoreType.DMA((2 * members,)),
    ]


def attn_out_kernel(members, ids_ref, x_ref, gain_ref, *refs):
    mixes, weights, refs = refs[:members], refs[members : members + 2], refs[members + 2 :]
    hidden_ref, normed_ref = refs[:2]
    project(members, ids_ref, x_ref, gain_ref, mixes, weights, hidden_ref, normed_ref, refs[2:])


def attn_out(half, ids, tokens, gain, mixes, weights):
    rows, width = tokens.shape
    half_rows = rows // HALVES
    members = len(mixes)
    inner = 2 * weights[0].shape[0]
    return pl.pallas_call(
        functools.partial(attn_out_kernel, members),
        grid=(1,),
        in_specs=[
            smem_spec(),
            pl.BlockSpec((half_rows, width), lambda i: (half, 0)),
            vmem_spec(),
        ]
        + [vmem_spec()] * members
        + [any_spec()] * len(weights),
        out_specs=[vmem_spec()] * 2,
        out_shape=[
            jax.ShapeDtypeStruct((half_rows, width), F32),
            jax.ShapeDtypeStruct((half_rows, width), BF),
        ],
        scratch_shapes=project_scratch(inner, width, half_rows, members),
        name="attn_out",
        cost_estimate=cost(
            2 * half_rows * inner * width, 2 * inner * width + 12 * half_rows * width
        ),
    )(ids, tokens, gain, *mixes, *weights)


def row_sum(refs):
    total = refs[0][...].astype(F32)
    for ref in refs[1:]:
        total = total + ref[...].astype(F32)
    return total


def norm_back(grad_normed, gain, values, inverse):
    scaled = grad_normed * gain
    return inverse * scaled - values * inverse**3 * jnp.mean(
        scaled * values, axis=-1, keepdims=True
    )


def pick_half(members, ids_ref, refs, at):
    per = members // HALVES
    value = refs[0][at, :]
    for half in range(1, HALVES):
        value = jnp.where(ids_ref[0] // per == half, refs[half][at, :], value)
    return value


def norm_two_back_kernel(members, ids_ref, lengths_ref, *refs):
    hiddens, (cot_ref, gain_ref), refs = refs[:HALVES], refs[HALVES : HALVES + 2], refs[HALVES + 2 :]
    pieces, refs = refs[:members], refs[members:]
    weights, refs = refs[:2], refs[2:]
    refs = refs[members - 1 :]
    sum_ref, low_ref, part_ref = refs[:3]
    d_mixed, refs = refs[3 : 3 + members], refs[3 + members :]
    sent, (held, made, sems) = refs[:-3], refs[-3:]
    for distance in range(members):
        for copy, _, _ in weight_copies(members, ids_ref, weights, held, sems, distance):
            copy.start()
    shard = low_ref.shape[0]
    step = min(32, shard)
    part_ref[...] = jnp.zeros_like(part_ref)

    def rows_at(index, carry):
        at = pl.ds(pl.multiple_of(index * step, step), step)
        grad = row_sum([r.at[at, :] for r in pieces])
        hidden = pick_half(members, ids_ref, hiddens, at)
        inverse = rms_scale(hidden)
        part_ref[...] += jnp.sum(grad * hidden * inverse, axis=0, keepdims=True)
        total = cot_ref[at, :].astype(F32) + norm_back(grad, gain_ref[...], hidden, inverse)
        sum_ref[at, :] = total
        low = total.astype(BF)
        low_ref[at, :] = low
        for ref in sent:
            ref[at, :] = low
        return carry

    lax.fori_loop(0, shard // step, rows_at, 0)
    begin = (ids_ref[2] * members + ids_ref[0]) * shard
    keep = window(lengths_ref, begin + lax.broadcasted_iota(jnp.int32, (shard, 1), 0))[1]
    size = held.shape[0] // (2 * members)

    def heads_of(distance, carry):
        for copy, at, first in weight_copies(members, ids_ref, weights, held, sems, distance):
            copy.wait()
            out = dims(low_ref[...], held[pl.ds(at, size), :], 1, 1)
            made[distance, :, pl.ds(first, size)] = jnp.where(keep, out, 0.0).astype(BF)
        return carry

    lax.fori_loop(0, members, heads_of, 0)
    for distance, ref in enumerate(d_mixed):
        ref[...] = made[distance]


def norm_two_back(ids, lengths, hiddens, cotangent, gain, pieces, weights, travel):
    members = len(pieces)
    shard, width = pieces[0].shape
    inner = sum(w.shape[0] for w in weights)
    per = members // HALVES
    mine = pl.BlockSpec((shard, width), lambda i, ids, lengths: (ids[0], 0))
    mine_half = pl.BlockSpec((shard, width), lambda i, ids, lengths: (ids[0] % per, 0))
    whole = pl.BlockSpec((shard, width), lambda i, ids, lengths: (0, 0))
    line = pl.BlockSpec((1, width), lambda i, ids, lengths: (0, 0))
    head_spec = pl.BlockSpec((shard, inner // members), lambda i, ids, lengths: (0, 0))
    return pl.pallas_call(
        functools.partial(norm_two_back_kernel, members),
        grid_spec=pltpu.PrefetchScalarGridSpec(
            num_scalar_prefetch=2,
            grid=(1,),
            in_specs=[mine_half] * HALVES
            + [mine, line]
            + [whole] * members
            + [any_spec()] * (len(weights) + len(travel)),
            out_specs=[whole, whole, line] + [head_spec] * members + [whole] * len(travel),
            scratch_shapes=[
                pltpu.VMEM((inner, width), BF),
                pltpu.VMEM((members, shard, inner // members), BF),
                pltpu.SemaphoreType.DMA((2 * members,)),
            ],
        ),
        out_shape=[
            jax.ShapeDtypeStruct((shard, width), F32),
            jax.ShapeDtypeStruct((shard, width), BF),
            jax.ShapeDtypeStruct((1, width), F32),
        ]
        + [jax.ShapeDtypeStruct((shard, inner // members), BF)] * members
        + [jax.ShapeDtypeStruct(t.shape, BF) for t in travel],
        input_output_aliases={
            4 + HALVES + members + len(weights) + i: 3 + members + i for i in range(len(travel))
        },
        name="norm_two_back",
        cost_estimate=cost(2 * shard * inner * width, 2 * inner * width + 24 * shard * width),
    )(ids, lengths, *hiddens, cotangent, gain, *pieces, *weights, *travel)


def last_rows_kernel(members, ids_ref, x_ref, *refs):
    hiddens, (add_ref, gain_ref), refs = refs[:HALVES], refs[HALVES : HALVES + 2], refs[HALVES + 2 :]
    pieces, ffn, (low_ref, part_ref) = refs[:members], refs[members:-2], refs[-2:]
    shard = x_ref.shape[0]
    step = min(32, shard)
    part_ref[...] = jnp.zeros_like(part_ref)

    def rows_at(index, carry):
        first = pl.multiple_of(index * step, step)
        at = pl.ds(first, step)
        grad = row_sum([r.at[at, :] for r in pieces])
        values = x_ref[at, :].astype(F32)
        inverse = rms_scale(values)
        part_ref[...] += jnp.sum(grad * values * inverse, axis=0, keepdims=True)
        low_ref[at, :] = (
            add_ref[at, :] + norm_back(grad, gain_ref[...], values, inverse)
        ).astype(BF)
        hidden = pick_half(members, ids_ref, hiddens, at)
        low_ref[pl.ds(shard + first, step), :] = (
            hidden + row_sum([r.at[at, :] for r in ffn])
        ).astype(BF)
        return carry

    lax.fori_loop(0, shard // step, rows_at, 0)


def last_rows(ids, tokens, hiddens, add, gain, pieces, ffn_pieces):
    shard, width = pieces[0].shape
    per = len(pieces) // HALVES
    mine = pl.BlockSpec((shard, width), lambda i, ids: (ids[0], 0))
    mine_half = pl.BlockSpec((shard, width), lambda i, ids: (ids[0] % per, 0))
    first = pl.BlockSpec((shard, width), lambda i, ids: (0, 0))
    second = pl.BlockSpec((shard, width), lambda i, ids: (1, 0))
    line = pl.BlockSpec((1, width), lambda i, ids: (0, 0))
    both = pl.BlockSpec((2 * shard, width), lambda i, ids: (0, 0))
    return pl.pallas_call(
        functools.partial(last_rows_kernel, len(pieces)),
        grid_spec=pltpu.PrefetchScalarGridSpec(
            num_scalar_prefetch=1,
            grid=(1,),
            in_specs=[mine] + [mine_half] * HALVES + [first, line]
            + [first] * (len(pieces) + 1)
            + [second] * (len(ffn_pieces) - 1),
            out_specs=[both, line],
        ),
        out_shape=[
            jax.ShapeDtypeStruct((2 * shard, width), BF),
            jax.ShapeDtypeStruct((1, width), F32),
        ],
        name="last_rows",
        cost_estimate=cost(30 * shard * width, 32 * shard * width),
    )(ids, tokens, *hiddens, add, gain, *pieces, *ffn_pieces)


def in_order_kernel(shard, outs, ids_ref, *refs):
    pieces, out_refs = refs[:-outs], refs[-outs:]
    for distance, ref in enumerate(pieces):
        at = pl.multiple_of((ids_ref[0] ^ distance) * shard, shard)
        for index, out_ref in enumerate(out_refs):
            out_ref[pl.ds(at, shard), :] = ref[index * shard : (index + 1) * shard, :]


def in_order(ids, pieces, outs):
    width = pieces[0].shape[1]
    shard = pieces[0].shape[0] // outs if outs > 1 else pieces[0].shape[0]
    rows = shard * len(pieces)
    return pl.pallas_call(
        functools.partial(in_order_kernel, shard, outs),
        in_specs=[smem_spec()] + [vmem_spec()] * len(pieces),
        out_specs=[vmem_spec()] * outs,
        out_shape=[jax.ShapeDtypeStruct((rows, width), pieces[0].dtype)] * outs,
        name="token_order",
        cost_estimate=cost(0, 4 * rows * outs * width),
    )(ids, *pieces)


def ffn_kernel(members, ids_ref, x_ref, gain_ref, before_ref, da_ref, wg_ref, wu_ref, *refs):
    mixes, refs = refs[:members], refs[members:]
    weights, refs = refs[:2], refs[2:]
    hidden_ref, normed_ref, act_ref, dg_ref, du_ref, full_s = refs[:6]
    half_rows = before_ref.shape[0]

    @pl.when(pl.program_id(0) == 0)
    def _():
        full_s[:half_rows, :] = before_ref[...]
        project(
            members, ids_ref, x_ref, gain_ref, mixes, weights, hidden_ref, normed_ref, refs[6:]
        )
        full_s[half_rows:, :] = normed_ref[...]

    normed = full_s[...]
    gate = jnp.dot(normed, wg_ref[...], preferred_element_type=F32)
    up = jnp.dot(normed, wu_ref[...], preferred_element_type=F32)
    sig = jax.nn.sigmoid(gate)
    silu = gate * sig
    act_ref[...] = (silu * up).astype(BF)
    d_act = da_ref[...]
    dg_ref[...] = (d_act * up * sig * (1.0 + gate * (1.0 - sig))).astype(BF)
    du_ref[...] = (d_act * silu).astype(BF)


def ffn_forward(ids, tokens, gain, mixes, weights, before, d_act, w_gate, w_up):
    rows, width = tokens.shape
    half_rows = rows // HALVES
    members = len(mixes)
    inner = 2 * weights[0].shape[0]
    units = w_gate.shape[1]
    step = min(512, units)
    tile = pl.BlockSpec((rows, step), lambda j: (0, j))
    weight = pl.BlockSpec((width, step), lambda j: (0, j))
    half_spec = pl.BlockSpec((half_rows, width), lambda j: (0, 0))
    return pl.pallas_call(
        functools.partial(ffn_kernel, members),
        grid=(units // step,),
        in_specs=[
            smem_spec(),
            pl.BlockSpec((half_rows, width), lambda j: (HALVES - 1, 0)),
            pl.BlockSpec((1, width), lambda j: (0, 0)),
            half_spec,
            tile,
            weight,
            weight,
        ]
        + [pl.BlockSpec(m.shape, lambda j: (0, 0)) for m in mixes]
        + [any_spec()] * len(weights),
        out_specs=[half_spec, half_spec, tile, tile, tile],
        out_shape=[
            jax.ShapeDtypeStruct((half_rows, width), F32),
            jax.ShapeDtypeStruct((half_rows, width), BF),
        ]
        + [jax.ShapeDtypeStruct((rows, units), BF)] * 3,
        scratch_shapes=[pltpu.VMEM((rows, width), BF)]
        + project_scratch(inner, width, half_rows, members),
        name="gate_up",
        cost_estimate=cost(
            4 * rows * width * units + 2 * half_rows * inner * width,
            4 * width * units + 2 * rows * width + 10 * rows * units + 2 * inner * width,
            rows * units,
        ),
    )(ids, tokens, gain, before, d_act, w_gate, w_up, *mixes, *weights)


def store_by_distance(ids_ref, out_refs, held, value):
    shard = value.shape[0] // len(out_refs)
    held[...] = value.astype(BF)
    for distance, out_ref in enumerate(out_refs):
        at = pl.multiple_of((ids_ref[0] ^ distance) * shard, shard)
        out_ref[...] = held[pl.ds(at, shard), :]


def pair_nt_kernel(ids_ref, a_ref, b_ref, wa_ref, wb_ref, *refs):
    value = dims(a_ref[...], wa_ref[...], 1, 1) + dims(b_ref[...], wb_ref[...], 1, 1)
    store_by_distance(ids_ref, refs[:-1], refs[-1], value)


def pair_nt(members, ids, a, b, w_a, w_b):
    rows, units = a.shape
    width = w_a.shape[0]
    step = min(512, width)
    full = pl.BlockSpec((rows, units), lambda j: (0, 0))
    weight = pl.BlockSpec((step, units), lambda j: (j, 0))
    return pl.pallas_call(
        pair_nt_kernel,
        grid=(width // step,),
        in_specs=[smem_spec(), full, full, weight, weight],
        out_specs=[pl.BlockSpec((rows // members, step), lambda j: (0, j))] * members,
        out_shape=[jax.ShapeDtypeStruct((rows // members, width), BF)] * members,
        scratch_shapes=[pltpu.VMEM((rows, step), BF)],
        name="d_normed_two",
        cost_estimate=cost(
            4 * rows * width * units, 4 * width * units + 4 * rows * units + 2 * rows * width
        ),
    )(ids, a, b, w_a, w_b)


def down_kernel(ids_ref, a_ref, w_ref, *refs):
    value = jnp.dot(a_ref[...], w_ref[...], preferred_element_type=F32)
    store_by_distance(ids_ref, refs[:-1], refs[-1], value)


def down_of(members, ids, act, w_down):
    rows, units = act.shape
    shard = rows // members
    width = w_down.shape[1]
    step = min(512, width)
    return pl.pallas_call(
        down_kernel,
        grid=(width // step,),
        in_specs=[
            smem_spec(),
            pl.BlockSpec((rows, units), lambda j: (0, 0)),
            pl.BlockSpec((units, step), lambda j: (0, j)),
        ],
        out_specs=[pl.BlockSpec((shard, step), lambda j: (0, j))]
        + [pl.BlockSpec((shard, step), lambda j: (1, j))] * (members - 1),
        out_shape=[jax.ShapeDtypeStruct((shard, width), BF)]
        + [jax.ShapeDtypeStruct((2 * shard, width), BF)] * (members - 1),
        scratch_shapes=[pltpu.VMEM((rows, step), BF)],
        name="ffn_down",
        cost_estimate=cost(
            2 * rows * width * units, 2 * width * units + 2 * rows * units + 2 * rows * width
        ),
    )(ids, act, w_down)


def column_specs(rows, part, count):
    return [
        pl.BlockSpec((rows, part), lambda j, ids, k=k: (0, 2 * k + ids[1])) for k in range(count)
    ]


def fill_columns(held, refs, groups):
    count = len(refs) // groups
    rows, part = refs[0].shape
    for index, ref in enumerate(refs):
        top = (index // count) * rows
        left = (index % count) * part
        held[top : top + rows, left : left + part] = ref[...]


def pick_columns_kernel(blocks, ids_ref, *refs):
    fill_columns(refs[-1], refs[:-1], len(refs[:-1]) // blocks)


def pick_columns(ids, values, part):
    rows, width = values[0].shape
    blocks = width // (2 * part)
    return pl.pallas_call(
        functools.partial(pick_columns_kernel, blocks),
        grid_spec=pltpu.PrefetchScalarGridSpec(
            num_scalar_prefetch=1,
            grid=(1,),
            in_specs=column_specs(rows, part, blocks) * len(values),
            out_specs=pl.BlockSpec((len(values) * rows, width // 2), lambda j, ids: (0, 0)),
        ),
        out_shape=jax.ShapeDtypeStruct((len(values) * rows, width // 2), BF),
        name="pick_columns",
        cost_estimate=cost(0, 4 * len(values) * rows * width // 2),
    )(ids, *[v for v in values for _ in range(blocks)])


def grad_down_kernel(own_ref, other_ref, cot_ref, o_ref):
    rows = own_ref.shape[0]
    o_ref[...] = (
        dims(own_ref[...], cot_ref[:rows, :], 0, 0) + dims(other_ref[...], cot_ref[rows:, :], 0, 0)
    ).astype(BF)


def grad_down_of(act, act_other, cots):
    rows, units = act.shape
    width = cots.shape[1]
    step = min(512, units)
    tile = pl.BlockSpec((rows, step), lambda j: (0, j))
    return pl.pallas_call(
        grad_down_kernel,
        grid=(units // step,),
        in_specs=[tile, tile, pl.BlockSpec((2 * rows, width), lambda j: (0, 0))],
        out_specs=pl.BlockSpec((step, width), lambda j: (j, 0)),
        out_shape=jax.ShapeDtypeStruct((units, width), BF),
        name="grad_down",
        cost_estimate=cost(
            4 * rows * width * units, 4 * rows * units + 4 * rows * width + 2 * width * units
        ),
    )(act, act_other, cots)


def grad_in_kernel(groups, blocks, half, ids_ref, *refs):
    normeds, refs = refs[: groups * blocks], refs[groups * blocks :]
    gates, ups, (o_ref, held) = refs[:2], refs[2:4], refs[4:]

    @pl.when(pl.program_id(0) == 0)
    def _():
        fill_columns(held, normeds, groups)

    rows = gates[0].shape[0]

    def of(pair):
        o_ref[...] = (
            dims(held[:rows, :], pair[0][...], 0, 0) + dims(held[rows:, :], pair[1][...], 0, 0)
        ).astype(BF)

    pl.when(pl.program_id(0) < half)(lambda: of(gates))
    pl.when(pl.program_id(0) >= half)(lambda: of(ups))


def grad_in_of(ids, normeds, d_gates, d_ups, part):
    width = normeds[0].shape[1]
    rows, units = d_gates[0].shape
    blocks = width // (2 * part)
    step = min(512, units)
    half = units // step
    columns = column_specs(normeds[0].shape[0], part, blocks)
    first = pl.BlockSpec((rows, step), lambda j, ids: (0, jnp.minimum(j, half - 1)))
    second = pl.BlockSpec((rows, step), lambda j, ids: (0, jnp.maximum(j - half, 0)))
    return pl.pallas_call(
        functools.partial(grad_in_kernel, len(normeds), blocks, half),
        grid_spec=pltpu.PrefetchScalarGridSpec(
            num_scalar_prefetch=1,
            grid=(2 * half,),
            in_specs=columns * len(normeds) + [first] * 2 + [second] * 2,
            out_specs=pl.BlockSpec((width // 2, step), lambda j, ids: (0, j)),
            scratch_shapes=[pltpu.VMEM((2 * rows, width // 2), BF)],
        ),
        out_shape=jax.ShapeDtypeStruct((width // 2, 2 * units), BF),
        name="grad_gate_up",
        cost_estimate=cost(
            4 * rows * width * units, 8 * rows * units + 2 * rows * width + 2 * width * units
        ),
    )(ids, *[n for n in normeds for _ in range(blocks)], *d_gates, *d_ups)


def grad_proj_kernel(lefts, ids_ref, *refs):
    own, other = refs[:lefts], refs[lefts : 2 * lefts]
    right_ref, right_other_ref, o_ref = refs[2 * lefts :]
    at = 0
    rows = right_ref.shape[0]
    part = rows // lefts
    total = 0.0
    for group, right in ((own, right_ref), (other, right_other_ref)):
        for index, left in enumerate(group):
            total = total + jnp.dot(
                left[...],
                right[index * part : (index + 1) * part, :],
                preferred_element_type=F32,
            )
    o_ref[...] = total.astype(BF)


def grad_proj_of(ids, lefts, lefts_other, right, right_other, part, name):
    inner = lefts[0].shape[0]
    rows, width = right.shape
    blocks = width // (2 * part)
    left_spec = pl.BlockSpec(lefts[0].shape, lambda k, ids: (0, 0))
    right_spec = pl.BlockSpec((rows, part), lambda k, ids: (0, 2 * k + ids[1]))
    return pl.pallas_call(
        functools.partial(grad_proj_kernel, len(lefts)),
        grid_spec=pltpu.PrefetchScalarGridSpec(
            num_scalar_prefetch=1,
            grid=(blocks,),
            in_specs=[left_spec] * (2 * len(lefts)) + [right_spec] * 2,
            out_specs=pl.BlockSpec((inner, part), lambda k, ids: (0, k)),
        ),
        out_shape=jax.ShapeDtypeStruct((inner, width // 2), BF),
        name=name,
        cost_estimate=cost(
            2 * rows * width * inner, 4 * inner * rows + 2 * rows * width + inner * width
        ),
    )(ids, *lefts, *lefts_other, right, right_other)


def finish_kernel(in_ref, out_ref, *refs):
    at = out_ref.shape[0]
    out_ref[...] = in_ref[:at, :].astype(F32)
    for ref in refs:
        count = ref.shape[1]
        ref[...] = in_ref[at : at + count, :].astype(F32).T
        at += count


def finish(grads, sizes):
    part = grads.shape[1]
    return pl.pallas_call(
        finish_kernel,
        in_specs=[vmem_spec()],
        out_specs=[vmem_spec()] * len(sizes),
        out_shape=[jax.ShapeDtypeStruct((sizes[0], part), F32)]
        + [jax.ShapeDtypeStruct((part, size), F32) for size in sizes[1:]],
        name="finish",
        cost_estimate=cost(0, 6 * sum(sizes) * part),
    )(grads)


def together(*values):
    return lax.optimization_barrier(values)


def body(
    tokens,
    attn_gain,
    w_query,
    w_key,
    w_value,
    w_out,
    ffn_gain,
    w_gate,
    w_up,
    w_down,
    doc_lengths,
    cotangent,
):
    rows, width = tokens.shape
    wide = lax.axis_size("wide")
    narrow = lax.axis_size("narrow")
    me_wide = lax.axis_index("wide")
    me = lax.axis_index("narrow")
    core = me_wide % 2
    kv_heads = w_key.shape[1] // HD
    half_rows = rows // HALVES
    shard = rows // narrow
    part = width // wide
    hops = wide // 4
    units = w_gate.shape[1]
    q_width = w_query.shape[1]
    k_width = w_key.shape[1]
    chip_groups = [list(range(0, wide, 2)), list(range(1, wide, 2))]
    ids = jnp.stack([me, core, me_wide]).astype(jnp.int32)

    def other_core(value):
        return lax.ppermute(value, "wide", [(i, i ^ 1) for i in range(wide)])

    def chips_up(value, hop):
        return lax.ppermute(value, "wide", [(i, i + 2 * hop) for i in range(wide - 2 * hop)])

    def chips_down(value, hop):
        return lax.ppermute(value, "wide", [(i + 2 * hop, i) for i in range(wide - 2 * hop)])

    def swap(value, distance):
        return lax.ppermute(value, "narrow", [(i, i ^ distance) for i in range(narrow)])

    def rows_of(value, distance):
        return lax.dynamic_slice_in_dim(value, (me ^ distance) * shard, shard, 0)

    def exchange(pieces):
        return [pieces[0]] + [swap(pieces[d], d) for d in range(1, narrow)]

    def gather_near(value):
        return [value] + [swap(value, d) for d in range(1, narrow)]

    def scatter(value, dimension):
        return lax.psum_scatter(
            value,
            "wide",
            scatter_dimension=dimension,
            axis_index_groups=chip_groups,
            tiled=True,
        )

    gain_one = attn_gain.astype(F32)[None, :]
    gain_two = ffn_gain.astype(F32)[None, :]

    w_half = w_out.shape[0] // 2
    w_mine = lax.dynamic_slice_in_dim(w_out, core * w_half, w_half, 0)
    w_all = lax.all_gather(w_mine, "narrow", axis=0, tiled=True)

    base = me_wide * rows
    index = base + jnp.arange(rows, dtype=jnp.int32)
    start = doc_offsets(doc_lengths, index)
    angle = jnp.asarray(inverse_frequencies(HD))[:, None] * (index - start).astype(F32)[None, :]
    cosine = jnp.cos(angle)
    sine = jnp.sin(angle)
    normed, packed = keys_values(tokens, gain_one, w_key, w_value, cosine, sine)
    ups = [chips_up(packed, hop) for hop in range(1, hops + 1)]
    beside = other_core(packed)
    query_t = rotate_t(dims(w_query, normed, 0, 1), cosine, sine).astype(BF)
    d_act = dims(cotangent, w_down, 1, 1)
    cot_other = other_core(cotangent)
    normed_other = other_core(normed)
    ups, query_t, d_act = together(ups, query_t, d_act)
    blocks = [packed, beside]
    for near in ups:
        blocks += [near, other_core(near)]

    outs, mixes, lses, gathered = [], [], [], []
    for half in range(HALVES):
        out, mixed, lse = attend(half, ids, doc_lengths, query_t, blocks, kv_heads)
        if gathered:
            gathered[-1], mixed, w_all = together(gathered[-1], mixed, w_all)
            out_weights = [w_all, other_core(w_all)]
        outs.append(out)
        mixes.append(mixed)
        lses.append(lse)
        query_t, mixed = together(query_t, mixed)
        gathered.append(gather_near(mixed))
    hidden_first, normed_first = attn_out(0, ids, tokens, gain_two, gathered[0], out_weights)
    mixed_others = [other_core(mixes[0])]
    gathered[1], normed_first, mixed_others = together(gathered[1], normed_first, mixed_others)

    hidden_last, normed_last, act, d_gate, d_up = ffn_forward(
        ids, tokens, gain_two, gathered[1], out_weights, normed_first, d_act, w_gate, w_up
    )
    hiddens = [hidden_first, hidden_last]
    act_other = other_core(act)
    d_gates = [d_gate, other_core(d_gate)]
    d_ups = [d_up, other_core(d_up)]
    normed_twos = [normed_first, normed_last]
    normed_others = [other_core(n) for n in normed_twos]
    act, cot_other, cot_mine = together(act, cot_other, cotangent)
    cots = pick_columns(ids, [cot_mine, cot_other], part)
    act_other, cots = together(act_other, cots)
    grad_down = grad_down_of(act, act_other, cots)
    d_gate_then, _ = together(d_gate, grad_down)
    grad_down = scatter(grad_down, 1)
    d_norm_pieces = pair_nt(narrow, ids, d_gate_then, d_up, w_gate, w_up)
    mixed_others += [other_core(m) for m in mixes[1:]]
    act_then, d_norm_pieces, d_gates, d_ups, normed_others, mixed_others = together(
        act, d_norm_pieces, d_gates, d_ups, normed_others, mixed_others
    )
    d_norm_pieces = exchange(d_norm_pieces)
    ffn_pieces = down_of(narrow, ids, act_then, w_down)
    d_norm_pieces[1], ffn_pieces, normed_twos = together(
        d_norm_pieces[1], ffn_pieces, normed_twos
    )
    grad_gate_up = grad_in_of(ids, normed_twos + normed_others, d_gates, d_ups, part)
    d_norm_pieces, ffn_pieces, _ = together(d_norm_pieces, ffn_pieces, grad_gate_up)

    d_hidden, d_hidden_b, gain_two_part, *made = norm_two_back(
        ids,
        doc_lengths,
        hiddens,
        cotangent,
        gain_two,
        d_norm_pieces,
        out_weights,
        ffn_pieces[1:],
    )
    d_mixed, travel = made[:narrow], made[narrow:]
    grad_gate_up, _ = together(grad_gate_up, d_hidden_b)
    grad_gate_up = scatter(grad_gate_up, 0)
    d_mixed = exchange(d_mixed)
    d_mixed, travel = together(d_mixed, travel)
    travel = [swap(value, d + 1) for d, value in enumerate(travel)]

    d_query_r, d_blocks = attend_back(
        ids, doc_lengths, query_t, d_mixed, outs, lses, blocks, kv_heads
    )
    d_query_r, d_blocks, travel[0] = together(d_query_r, d_blocks, travel[0])
    d_blocks = d_blocks.reshape(2 * (hops + 1), 2 * k_width, rows)
    for_other = other_core(d_blocks[1::2])
    both = [
        d_blocks[2 * hop].astype(F32) + for_other[hop].astype(F32) for hop in range(hops + 1)
    ]
    down = chips_down(both[hops].astype(BF), 1)
    for hop in range(hops - 1, 0, -1):
        down = chips_down((both[hop] + down.astype(F32)).astype(BF), 1)
    d_kv = both[0]

    d_query = rotate_t(d_query_r * (1.0 / math.sqrt(HD)), cosine, -sine).astype(BF)
    (d_hidden_full,) = in_order(ids, [d_hidden_b, *travel], 1)
    grad_query = grad_proj_of(
        ids, [d_query], [other_core(d_query)], normed, normed_other, part, "grad_query"
    )
    grad_out = grad_proj_of(
        ids, mixes, mixed_others, d_hidden_full, other_core(d_hidden_full), part, "grad_out"
    )
    down, grad_out, grad_query, grad_down = together(down, grad_out, grad_query, grad_down)
    d_kv = d_kv + down.astype(F32)
    d_keys = rotate_t(d_kv[:k_width], cosine, -sine).astype(BF)
    d_values = d_kv[k_width:].astype(BF)
    norm_one_part = (
        dims(d_query, w_query, 0, 1) + dims(d_keys, w_key, 0, 1) + dims(d_values, w_value, 0, 1)
    ).astype(BF)
    norm_one_pieces = [rows_of(norm_one_part, d) for d in range(narrow)]
    d_pair = jnp.concatenate([d_keys, d_values], axis=0)
    d_pair, norm_one_pieces = together(d_pair, norm_one_pieces)
    norm_one_pieces = exchange(norm_one_pieces)
    grad_pair = grad_proj_of(
        ids, [d_pair], [other_core(d_pair)], normed, normed_other, part, "grad_key_value"
    )
    grads = jnp.concatenate([grad_out, grad_query, grad_pair], axis=0)
    norm_one_pieces, grads = together(norm_one_pieces, grads)
    last, gain_one_part = last_rows(
        ids,
        tokens,
        hiddens,
        d_hidden,
        gain_one,
        norm_one_pieces,
        [ffn_pieces[0], *travel],
    )
    last_pieces = gather_near(last)
    gains = jnp.concatenate([gain_one_part, gain_two_part], axis=0)
    grads, grad_gate_up, last_pieces[1:-1] = together(grads, grad_gate_up, last_pieces[1:-1])
    grads = scatter(grads, 1)
    input_grad, output = in_order(ids, last_pieces, 2)
    gains, output = together(gains, output)
    gains = sum(gather_near(gains)[1:], gains)
    gains = gains + other_core(gains)
    gain_sum = 0.0
    for hop in range(wide // 2):
        target = lax.rem(me_wide + 2 * hop, wide)
        piece = lax.dynamic_slice_in_dim(gains, target * part, part, 1)
        if hop:
            piece = lax.ppermute(piece, "wide", [(i, (i + 2 * hop) % wide) for i in range(wide)])
        gain_sum = gain_sum + piece
    gains = gain_sum
    grad_gate = grad_gate_up[:, :units].astype(F32)
    grad_up = grad_gate_up[:, units:].astype(F32)
    grad_down = grad_down.astype(F32)
    grads, gains, input_grad, output, grad_gate, grad_up, grad_down = together(
        grads, gains, input_grad, output, grad_gate, grad_up, grad_down
    )
    grad_out, grad_query, grad_key, grad_value = finish(
        grads, (w_out.shape[0], q_width, k_width, k_width)
    )
    return (
        output,
        input_grad,
        gains[0],
        grad_query,
        grad_key,
        grad_value,
        grad_out,
        gains[1],
        grad_gate,
        grad_up,
        grad_down,
    )


def solution(mesh):
    in_specs = (
        P("wide", None),
        P(),
        P(None, "narrow"),
        P(None, "narrow"),
        P(None, "narrow"),
        P("narrow", None),
        P(),
        P(None, "narrow"),
        P(None, "narrow"),
        P("narrow", None),
        P(),
        P("wide", None),
    )
    out_specs = (
        P("wide", None),
        P("wide", None),
        P("wide"),
        P("wide", "narrow"),
        P("wide", "narrow"),
        P("wide", "narrow"),
        P("narrow", "wide"),
        P("wide"),
        P("wide", "narrow"),
        P("wide", "narrow"),
        P("narrow", "wide"),
    )
    return jax.shard_map(body, mesh=mesh, in_specs=in_specs, out_specs=out_specs, check_vma=False)
```
